32 devices in a mesh: dp: 8 (over z, core), seq: 4 (over y, x).
Axes of the slice: x: 2, y: 2, z: 4, core: 2. Of those that a mesh axis runs over, the one named last changes fastest.
Arguments:
- layer_in: bfloat16 [16384, 2048], P(('dp', 'seq')), may hold values from -6 to 6
- cotangent: bfloat16 [16384, 2048], P(('dp', 'seq')), may hold values from -6 to 6
- lengths: int32 [8, 4], P('dp'), may hold values from 1 to 1024, as said below
- w_query: bfloat16 [2048, 2048], P('dp', 'seq'), may hold values from -0.125 to 0.125
- w_key: bfloat16 [2048, 2048], P('dp', 'seq'), may hold values from -0.125 to 0.125
- w_value: bfloat16 [2048, 2048], P('dp', 'seq'), may hold values from -0.125 to 0.125
- w_out: bfloat16 [2048, 2048], P('seq', 'dp'), may hold values from -0.125 to 0.125
- w_gate: bfloat16 [2048, 8192], P(None, ('dp', 'seq')), may hold values from -0.125 to 0.125
- w_up: bfloat16 [2048, 8192], P(None, ('dp', 'seq')), may hold values from -0.125 to 0.125
- w_down: bfloat16 [8192, 2048], P(('dp', 'seq')), may hold values from -0.0625 to 0.0625
- gain_query: bfloat16 [2048], P(('dp', 'seq')), may hold values from 0.25 to 1.75
- gain_key: bfloat16 [2048], P(('dp', 'seq')), may hold values from 0.25 to 1.75
- gain_attn: bfloat16 [2048], P(('dp', 'seq')), may hold values from 0.25 to 1.75
- gain_ffn: bfloat16 [2048], P(('dp', 'seq')), may hold values from 0.25 to 1.75
Outputs:
- layer_out: bfloat16 [16384, 2048], P(('dp', 'seq'))
- grad_in: float32 [16384, 2048], P(('dp', 'seq'))
- grad_w_query: float32 [2048, 2048], P('dp', 'seq')
- grad_w_key: float32 [2048, 2048], P('dp', 'seq')
- grad_w_value: float32 [2048, 2048], P('dp', 'seq')
- grad_w_out: float32 [2048, 2048], P('seq', 'dp')
- grad_w_gate: float32 [2048, 8192], P(None, ('dp', 'seq'))
- grad_w_up: float32 [2048, 8192], P(None, ('dp', 'seq'))
- grad_w_down: float32 [8192, 2048], P(('dp', 'seq'))
- grad_gain_query: float32 [2048], P(('dp', 'seq'))
- grad_gain_key: float32 [2048], P(('dp', 'seq'))
- grad_gain_attn: float32 [2048], P(('dp', 'seq'))
- grad_gain_ffn: float32 [2048], P(('dp', 'seq'))
The draws below stay inside these ranges and needn't reach their ends.
Inputs may be any that keep to these rules, and one draw needn't show every extreme that they name: Row b holds the lengths of bucket b's 3 documents in order and, last, the number of padding slots at the bucket's end; each row sums to 2048, and in every bucket one document has exactly 1024 tokens.
All inputs are finite; a program needn't handle non-finite values.
Results may differ from the reference program's by a relative error of at most 0.024.
Values may be sent and summed in bfloat16 or wider, within the bound.
A program may use at most 320 MiB of HBM per device.

```python
import jax
import jax.numpy as jnp
from jax import lax

D = 2048
HEADS = 16
FF = 8192
DOCS = 3
MAX_DOC = 1024
BUCKET_TOK = 2048
BUCKETS = 8
TOKENS = 16384


def draw_lengths(key, part):
    remainder = BUCKET_TOK - MAX_DOC
    key_long = jax.random.fold_in(key, 11)
    key_cuts = jax.random.fold_in(key, 23)
    long_doc = jax.random.randint(key_long, (BUCKETS,), 0, DOCS)
    cut_points = jnp.sort(jax.random.randint(key_cuts, (BUCKETS, DOCS - 1), 0, remainder - DOCS + 1), axis=1)
    boundary = jnp.concatenate([jnp.zeros((BUCKETS, 1), jnp.int32), cut_points.astype(jnp.int32), jnp.full((BUCKETS, 1), remainder - DOCS, jnp.int32)], axis=1)
    pieces = boundary[:, 1:] - boundary[:, :-1] + 1
    doc_slot = jnp.arange(DOCS, dtype=jnp.int32)[None, :]
    source = jnp.clip(doc_slot - (doc_slot > long_doc[:, None]).astype(jnp.int32), 0, DOCS - 1)
    others = jnp.take_along_axis(pieces, source, axis=1)
    docs_len = jnp.where(doc_slot == long_doc[:, None], MAX_DOC, others)
    return jnp.concatenate([docs_len, pieces[:, DOCS - 1:]], axis=1).astype(jnp.int32)


def spiked(values, key, source, target, parts, factor):
    owner, partner = [(jnp.arange(values.shape[dim]) // (values.shape[dim] // parts)).reshape([-1 if axis == dim else 1 for axis in range(values.ndim)]) for dim in (source, target)]
    chosen = jax.random.permutation(key, parts)[partner]
    strong = (owner == chosen) | (owner == (partner + parts // 2) % parts)
    return jnp.where(strong, factor * values, values)


def steps_of(rng, shape, cuts, low, largest):
    loudness, own = 1.0, jax.random.fold_in(rng, 6)
    for dim, blocks in cuts:
        heights = jnp.exp(jax.random.uniform(jax.random.fold_in(own, dim), (blocks,), jnp.float32, low / len(cuts), largest / len(cuts)))
        loudness = loudness * jnp.repeat(heights, shape[dim] // blocks).reshape([-1 if axis == dim else 1 for axis in range(len(shape))])
    return loudness


def scatter_about(rng, extent, width, most, cuts=(), held_as=jnp.bfloat16):
    values = width * jax.random.normal(rng, extent, jnp.float32)
    if cuts:
        values = values * steps_of(rng, extent, cuts, -0.22, 0.18)
    return jnp.clip(values, -most, most).astype(held_as)


def gaussian_with(stream_key, extent, spread, limit, cuts, heavy, held_as=jnp.bfloat16):
    array = spread * jax.random.normal(stream_key, extent, jnp.float32)
    if cuts:
        array = array * steps_of(stream_key, extent, cuts, -0.22, 0.18)
    return jnp.clip(spiked(array, jax.random.fold_in(stream_key, 3), *heavy), -limit, limit).astype(held_as)


def setup_inputs(seed: int = 0) -> dict:
    key_of = jax.random.split(jax.random.key(seed), 15)
    return {
        "layer_in": gaussian_with(key_of[0], (TOKENS, D), 1.0, 6.0, ((0, 32),), (0, 1, 32, 2.75)),
        "cotangent": scatter_about(key_of[1], (TOKENS, D), 1.0, 6.0, ((0, 32),)),
        "lengths": draw_lengths(jax.random.fold_in(key_of[14], 71), 0),
        "w_query": scatter_about(key_of[3], (D, D), D ** -0.5, 0.125, ((0, 8), (1, 4))),
        "w_key": scatter_about(key_of[4], (D, D), D ** -0.5, 0.125, ((0, 8), (1, 4))),
        "w_value": scatter_about(key_of[5], (D, D), D ** -0.5, 0.125, ((0, 8), (1, 4))),
        "w_out": scatter_about(key_of[6], (D, D), D ** -0.5, 0.125, ((0, 4), (1, 8))),
        "w_gate": scatter_about(key_of[7], (D, FF), D ** -0.5, 0.125, ((1, 32),)),
        "w_up": scatter_about(key_of[8], (D, FF), D ** -0.5, 0.125, ((1, 32),)),
        "w_down": scatter_about(key_of[9], (FF, D), FF ** -0.5, 0.0625, ((0, 32),)),
        "gain_query": jnp.clip(1.0 + 0.15 * jax.random.normal(key_of[10], (D,), jnp.float32), 0.25, 1.75).astype(jnp.bfloat16),
        "gain_key": jnp.clip(1.0 + 0.15 * jax.random.normal(key_of[11], (D,), jnp.float32), 0.25, 1.75).astype(jnp.bfloat16),
        "gain_attn": jnp.clip(1.0 + 0.15 * jax.random.normal(key_of[12], (D,), jnp.float32), 0.25, 1.75).astype(jnp.bfloat16),
        "gain_ffn": jnp.clip(1.0 + 0.15 * jax.random.normal(key_of[13], (D,), jnp.float32), 0.25, 1.75).astype(jnp.bfloat16),
    }


@jax.custom_vjp
def low(v):
    return lax.optimization_barrier(v.astype(jnp.bfloat16)).astype(jnp.float32)

@jax.custom_vjp
def low_back(v):
    return v

def low_keep(v):
    return (low(v), None)

def low_pass(kept, grad):
    return (grad,)

def back_keep(v):
    return (v, None)

def back_low(kept, grad):
    return (low(grad),)
low.defvjp(low_keep, low_pass)
low_back.defvjp(back_keep, back_low)
HIGHEST = lax.Precision.HIGHEST
NORM_EPS = 1e-06
ROPE_BASE = 500000.0
MASKED = -1e+30

def matmul(left_op, right_op):
    return jnp.dot(left_op, right_op, precision=HIGHEST, preferred_element_type=jnp.float32)

def rms_norm(values, gain_vec):
    return values * lax.rsqrt(lax.optimization_barrier(jnp.mean(values * values, axis=-1, keepdims=True)) + NORM_EPS) * gain_vec

def rotate(values, positions, head_count):
    tokens_n = values.shape[0]
    head_width = values.shape[1] // head_count
    half_width = head_width // 2
    frequency = ROPE_BASE ** (-2.0 * jnp.arange(half_width, dtype=jnp.float32) / head_width)
    angles = positions.astype(jnp.float32)[:, None] * frequency[None, :]
    cosine = jnp.cos(angles)[:, None, :]
    sine_val = jnp.sin(angles)[:, None, :]
    pieces = values.reshape(tokens_n, head_count, head_width)
    lower_half = pieces[..., :half_width]
    upper_half = pieces[..., half_width:]
    turned = jnp.concatenate([lower_half * cosine - upper_half * sine_val, upper_half * cosine + lower_half * sine_val], axis=-1)
    return turned.reshape(tokens_n, head_count * head_width)

def doc_layout(length_row, slot_ids):
    bounds = jnp.cumsum(length_row).astype(jnp.int32)
    passed = slot_ids[:, None] >= bounds[None, :]
    segment = lax.optimization_barrier(jnp.sum(passed.astype(jnp.int32), axis=1)).astype(jnp.int32)
    starts = lax.optimization_barrier(jnp.sum(jnp.where(passed, length_row[None, :], 0), axis=1)).astype(jnp.int32)
    return (segment, (slot_ids - starts).astype(jnp.int32))

def allowed(seg_rows, slot_rows, seg_cols, slot_cols, pad_segment):
    matched = seg_rows[:, None] == seg_cols[None, :]
    causal = slot_cols[None, :] <= slot_rows[:, None]
    padded = (seg_cols[None, :] == pad_segment) & (slot_cols[None, :] != slot_rows[:, None])
    return matched & causal & jnp.logical_not(padded)

def bucket_attention(queries, keys_in, values_in, segment, pad_segment, head_count):
    bucket_len = queries.shape[0]
    head_width = queries.shape[1] // head_count
    block_rows = min(512, bucket_len)
    blocks = bucket_len // block_rows
    inv_root = head_width ** (-0.5)
    slot_ids = jnp.arange(bucket_len, dtype=jnp.int32)
    key_split = keys_in.reshape(bucket_len, head_count, head_width)
    value_split = values_in.reshape(bucket_len, head_count, head_width)

    def one_block(inputs):
        query_block, first_row = inputs
        rows_seg = lax.dynamic_slice_in_dim(segment, first_row, block_rows)
        rows_slot = first_row + jnp.arange(block_rows, dtype=jnp.int32)
        query_split = query_block.reshape(block_rows, head_count, head_width)
        scores = low_back(jnp.einsum('qhd,khd->hqk', query_split, key_split, precision=HIGHEST) * inv_root)
        visible = allowed(rows_seg, rows_slot, segment, slot_ids, pad_segment)
        scores = jnp.where(visible[None], scores, MASKED)
        attn_probs = jax.nn.softmax(scores, axis=-1)
        attended = jnp.einsum('hqk,khd->qhd', low(attn_probs), value_split, precision=HIGHEST)
        return attended.reshape(block_rows, head_count * head_width)
    starts = jnp.arange(blocks, dtype=jnp.int32) * block_rows
    result = lax.map(jax.checkpoint(one_block), (queries.reshape(blocks, block_rows, -1), starts))
    return result.reshape(bucket_len, -1)

def layer_forward(seg_all, pos_flat, pad_segment, layer_x, w_query, w_key, w_value, w_out, w_gate, w_up, w_down, gain_query, gain_key, gain_attn, gain_ffn):
    q_proj = low_back(matmul(layer_x, w_query))
    k_proj = low_back(matmul(layer_x, w_key))
    v_low = low(low_back(matmul(layer_x, w_value)))
    q_low = low(low_back(rotate(rms_norm(q_proj, gain_query), pos_flat, HEADS)))
    k_low = low(low_back(rotate(rms_norm(k_proj, gain_key), pos_flat, HEADS)))
    buckets_n = seg_all.shape[0]

    def shaped(array_in):
        return array_in.reshape(buckets_n, -1, array_in.shape[-1])

    def per_bucket(inputs):
        q_bucket, k_bucket, v_bucket, seg_bucket = inputs
        return bucket_attention(q_bucket, k_bucket, v_bucket, seg_bucket, pad_segment, HEADS)
    attended = lax.map(per_bucket, (shaped(q_low), shaped(k_low), shaped(v_low), seg_all))
    attn_low = low(low_back(attended.reshape(layer_x.shape[0], -1)))
    branch_a = low_back(matmul(attn_low, w_out))
    hidden_in = layer_x + rms_norm(branch_a, gain_attn)
    hidden_low = low(hidden_in)
    gate_proj = low_back(matmul(hidden_low, w_gate))
    up_proj = low_back(matmul(hidden_low, w_up))
    act_low = low(jax.nn.silu(gate_proj) * up_proj)
    branch_m = low_back(matmul(act_low, w_down))
    return hidden_in + rms_norm(branch_m, gain_ffn)

def reference(layer_in, cotangent, lengths, w_query, w_key, w_value, w_out, w_gate, w_up, w_down, gain_query, gain_key, gain_attn, gain_ffn):
    pad_segment = lengths.shape[1] - 1
    slot_ids = jnp.arange(BUCKET_TOK, dtype=jnp.int32)
    seg_all, pos_all = jax.vmap(doc_layout, in_axes=(0, None))(lengths, slot_ids)
    pos_flat = pos_all.reshape(-1)
    floats = [argument.astype(jnp.float32) for argument in (layer_in, w_query, w_key, w_value, w_out, w_gate, w_up, w_down, gain_query, gain_key, gain_attn, gain_ffn)]

    def forward(*params):
        return layer_forward(seg_all, pos_flat, pad_segment, *params)
    result, backward = jax.vjp(forward, *floats)
    gradients = backward(cotangent.astype(jnp.float32))
    return (result.astype(jnp.bfloat16), gradients[0], gradients[1], gradients[2], gradients[3], gradients[4], gradients[5], gradients[6], gradients[7], gradients[8], gradients[9], gradients[10], gradients[11])
```

```python
import functools

import jax
import jax.numpy as jnp
from jax import lax
from jax.experimental import pallas as pl
from jax.experimental.pallas import tpu as pltpu
from jax.sharding import PartitionSpec as P

HEADS = 16
NORM_EPS = 1e-06
ROPE_BASE = 500000.0
MASKED = -1e30
LOG2E = 1.4426950408889634

F32 = jnp.float32
BF16 = jnp.bfloat16
MESH = pl.DeviceIdType.MESH
VMEM_BYTES = 60 * 1024 * 1024
ANY = pl.BlockSpec(memory_space=pl.ANY)
VM = pl.BlockSpec(memory_space=pltpu.VMEM)


def dot_nn(a, b):
    return lax.dot_general(a, b, (((1,), (0,)), ((), ())), preferred_element_type=F32)


def dot_nt(a, b):
    return lax.dot_general(a, b, (((1,), (1,)), ((), ())), preferred_element_type=F32)


def dot_tn(a, b):
    return lax.dot_general(a, b, (((0,), (0,)), ((), ())), preferred_element_type=F32)


def row_sums(values):
    folded = values[:, 0:128]
    for k in range(1, values.shape[1] // 128):
        folded = folded + values[:, k * 128 : (k + 1) * 128]
    return jnp.sum(jnp.transpose(folded), axis=0, keepdims=True)


def as_columns(rows8):
    return jnp.transpose(jnp.concatenate([rows8] * 16, axis=0))


def tile_of(extent, most):
    return most if extent % most == 0 else extent


class Square:
    def __init__(self, ways):
        self.ways = ways
        self.me = lax.axis_index("seq")
        self.square = ways == 4
        if self.square:
            self.x = self.me + 1 - 2 * lax.rem(self.me, 2)
            self.y = lax.rem(self.me + 2, 4)
            self.d = 3 - self.me

    def peer(self, p):
        return lax.rem(self.me + p, self.ways)

    def near(self):
        if self.square:
            return [self.x, self.y]
        return [self.peer(p) for p in range(1, self.ways)]

    def everyone(self):
        return [self.peer(p) for p in range(1, self.ways)]


def greet(devices):
    barrier = pltpu.get_barrier_semaphore()
    for device in devices:
        pl.semaphore_signal(barrier, inc=1, device_id=device, device_id_type=MESH)
    pl.semaphore_wait(barrier, len(devices))


def to_seq(src, dst, send, recv, peer):
    return pltpu.make_async_remote_copy(
        src_ref=src, dst_ref=dst, send_sem=send, recv_sem=recv, device_id={"seq": peer}, device_id_type=MESH
    )


def to_dp(src, dst, send, recv, peer):
    return pltpu.make_async_remote_copy(
        src_ref=src, dst_ref=dst, send_sem=send, recv_sem=recv, device_id={"dp": peer}, device_id_type=MESH
    )


class Gather:
    def __init__(self, group, src, full, send, recv, own_sem):
        self.g, self.src, self.full, self.send, self.recv = group, src, full, send, recv
        self.rows = src.shape[0]
        self.own = pltpu.make_async_copy(src, self.chunk(group.me), own_sem)

    @staticmethod
    def sems(ways):
        return 6 if ways == 4 else ways - 1

    def chunk(self, index):
        return self.full.at[pl.ds(index * self.rows, self.rows)]

    def half(self, index, which):
        h = self.rows // 2
        return self.full.at[pl.ds(index * self.rows + which * h, h)]

    def cp(self, k, src, dst, peer):
        return to_seq(src, dst, self.send.at[k], self.recv.at[k], peer)

    def start(self):
        g, h = self.g, self.rows // 2
        if g.square:
            top, low = self.src.at[pl.ds(0, h)], self.src.at[pl.ds(h, h)]
            self.first = [
                self.cp(0, top, self.half(g.me, 0), g.x),
                self.cp(1, low, self.half(g.me, 1), g.y),
                self.cp(2, low, self.half(g.me, 1), g.x),
                self.cp(3, top, self.half(g.me, 0), g.y),
            ]
        else:
            self.first = [self.cp(p - 1, self.src, self.chunk(g.me), g.peer(p)) for p in range(1, g.ways)]
        for c in self.first:
            c.start()
        self.own.start()

    def relay(self):
        g = self.g
        if g.square:
            self.first[0].wait_recv()
            a = self.cp(4, self.half(g.x, 0), self.half(g.x, 0), g.y)
            a.start()
            self.first[1].wait_recv()
            b = self.cp(5, self.half(g.y, 1), self.half(g.y, 1), g.x)
            b.start()
            self.second = [a, b]
        else:
            self.second = []

    def finish(self):
        g = self.g
        if g.square:
            self.first[2].wait_recv()
            self.first[3].wait_recv()
        else:
            for c in self.first:
                c.wait_recv()
        for c in self.second:
            c.wait_recv()
        for c in self.first + self.second:
            c.wait_send()
        self.own.wait()


class Scatter:
    @staticmethod
    def buffers(ways, rows, width):
        if ways == 4:
            return [
                pltpu.VMEM((3, rows, width), BF16),
                pltpu.VMEM((2, rows, width), BF16),
                pltpu.VMEM((2, rows // 2, width), BF16),
            ]
        return [
            pltpu.VMEM((ways - 1, rows, width), BF16),
            pltpu.VMEM((ways - 1, rows, width), BF16),
            pltpu.VMEM((2, 16, width), BF16),
        ]

    def __init__(self, group, out, arrived, relayed, send, recv):
        self.g, self.out, self.arrived, self.relayed, self.send, self.recv = group, out, arrived, relayed, send, recv
        self.rows = out.shape[1]

    def cp(self, k, src, dst, peer):
        return to_seq(src, dst, self.send.at[k], self.recv.at[k], peer)

    def run(self, partial):
        g, h = self.g, self.rows // 2
        out, arrived, relayed = self.out, self.arrived, self.relayed
        if not g.square:
            self.sent = []
            for p in range(1, g.ways):
                partial(g.peer(p), out.at[p - 1])
                c = self.cp(p - 1, out.at[p - 1], arrived.at[p - 1], g.peer(p))
                c.start()
                self.sent.append(c)
            return
        top, low = pl.ds(0, h), pl.ds(h, h)
        partial(g.d, out.at[2])
        c0 = self.cp(0, out.at[2, top], relayed.at[0], g.x)
        c1 = self.cp(1, out.at[2, low], relayed.at[1], g.y)
        c0.start()
        c1.start()
        partial(g.x, out.at[0])
        c2 = self.cp(2, out.at[0, top], arrived.at[0, top], g.x)
        c2.start()
        partial(g.y, out.at[1])
        c3 = self.cp(3, out.at[1, low], arrived.at[1, low], g.y)
        c3.start()
        self.sent = [c0, c1, c2, c3]

    def relay(self):
        g, h = self.g, self.rows // 2
        if not g.square:
            return
        out, arrived, relayed = self.out, self.arrived, self.relayed
        top, low = pl.ds(0, h), pl.ds(h, h)
        c0, c1, c2, c3 = self.sent
        step = tile_of(h, 64)

        def add(slot, base, which):
            def body(t, carry):
                rows = pl.ds(base + t * step, step)
                have = out[slot, rows, :].astype(F32)
                out[slot, rows, :] = (have + relayed[which, pl.ds(t * step, step), :].astype(F32)).astype(BF16)
                return carry

            lax.fori_loop(0, h // step, body, 0)

        c1.wait_recv()
        add(0, h, 1)
        c4 = self.cp(4, out.at[0, low], arrived.at[0, low], g.x)
        c4.start()
        c0.wait_recv()
        add(1, 0, 0)
        c5 = self.cp(5, out.at[1, top], arrived.at[1, top], g.y)
        c5.start()
        self.sent += [c4, c5]

    def finish(self):
        if self.g.square:
            arriving, done = self.sent[2:], self.sent[:2]
        else:
            arriving, done = self.sent, self.sent[:1]
        for c in arriving:
            c.wait_recv()
        for c in done:
            c.wait_send()

    def spare(self):
        return self.out.at[2 if self.g.square else 0]

    def drain(self):
        for c in self.sent[2:] if self.g.square else self.sent[1:]:
            c.wait_send()

    def total(self, own, rows):
        value = own[rows, :]
        for k in range(self.arrived.shape[0]):
            value = value + self.arrived[k, rows, :].astype(F32)
        return value


def remote_call(kernel, outs, in_specs, out_specs, scratch, collective_id, flops, nbytes):
    return pl.pallas_call(
        kernel,
        out_shape=outs,
        in_specs=in_specs,
        out_specs=out_specs,
        scratch_shapes=scratch,
        compiler_params=pltpu.CompilerParams(
            collective_id=collective_id, has_side_effects=True, vmem_limit_bytes=VMEM_BYTES
        ),
        cost_estimate=pl.CostEstimate(flops=flops, bytes_accessed=nbytes, transcendentals=0),
    )


def sems(n):
    return [pltpu.SemaphoreType.DMA((n,)), pltpu.SemaphoreType.DMA((n,))]


def enter_kernel(ways, dp_ways, x_ref, gain_ref, full_ref, gains_ref, send, recv, own_sem, gsend, grecv):
    g = Square(ways)
    dp_me = lax.axis_index("dp")
    dp_peers = [lax.rem(dp_me + p, dp_ways) for p in range(1, dp_ways)]
    greet([{"seq": q} for q in g.everyone()] + [{"dp": p} for p in dp_peers])
    ag = Gather(g, x_ref, full_ref, send, recv, own_sem.at[0])
    ag.start()
    gains_ref[g.me, dp_me] = gain_ref[...]
    first = [
        to_dp(gain_ref, gains_ref.at[g.me, dp_me], gsend.at[k], grecv.at[k], p) for k, p in enumerate(dp_peers)
    ]
    for c in first:
        c.start()
    for c in first:
        c.wait_recv()
    base = dp_ways - 1
    second = [
        to_seq(gains_ref.at[g.me], gains_ref.at[g.me], gsend.at[base + k], grecv.at[base + k], q)
        for k, q in enumerate(g.everyone())
    ]
    for c in second:
        c.start()
    ag.relay()
    for c in second:
        c.wait_recv()
    for c in first + second:
        c.wait_send()
    ag.finish()


def enter(ways, dp_ways, x, gains):
    rows, width = x.shape
    n = Gather.sems(ways)
    m = dp_ways - 1 + ways - 1
    return remote_call(
        functools.partial(enter_kernel, ways, dp_ways),
        (
            jax.ShapeDtypeStruct((ways * rows, width), BF16),
            jax.ShapeDtypeStruct((ways, dp_ways, 8, 128), F32),
        ),
        [ANY, VM],
        (ANY, VM),
        sems(n) + [pltpu.SemaphoreType.DMA((1,))] + sems(m),
        0,
        0,
        80_000_000,
    )(x, gains)


def exchange_rows(g, mine, arrived, send, recv):
    copies = [
        to_seq(mine, arrived.at[k], send.at[k], recv.at[k], q) for k, q in enumerate(g.everyone())
    ]
    for c in copies:
        c.start()
    for c in copies:
        c.wait_recv()
    total = mine[...]
    for k in range(g.ways - 1):
        total = total + arrived[k]
    for c in copies:
        c.wait_send()
    return total


def project_kernel(
    ways, x_ref, w_ref, gain_ref, cos_ref, sin_ref, q_ref, k_ref, v_ref, qn_ref, kn_ref, stat_ref,
    qf, kf, mine, arrived, send, recv,
):
    g = Square(ways)
    greet([{"seq": q} for q in g.everyone()])
    count, width = x_ref.shape
    cols = q_ref.shape[1]
    step = tile_of(count, 512)
    mine[...] = jnp.zeros_like(mine)

    def project(i, carry):
        rows = pl.ds(pl.multiple_of(i * step, step), step)
        xs = x_ref[rows, :]
        for part, ref in ((0, qf), (1, kf)):
            value = dot_nn(xs, w_ref[:, part * cols : (part + 1) * cols])
            ref[rows, :] = value
            mine[part : part + 1, rows] = row_sums(value * value)
        v_ref[rows, :] = dot_nn(xs, w_ref[:, 2 * cols : 3 * cols]).astype(BF16)
        return carry

    lax.fori_loop(0, count // step, project, 0)
    stat_ref[...] = exchange_rows(g, mine, arrived, send, recv)
    small = tile_of(count, 256)

    def finish(i, carry):
        rows = pl.ds(pl.multiple_of(i * small, small), small)
        inverse = lax.rsqrt(as_columns(stat_ref[:, rows]) * (1.0 / width) + NORM_EPS)
        cosine, sine = cos_ref[rows, :], sin_ref[rows, :]
        for part, src, normed, out in ((0, qf, qn_ref, q_ref), (1, kf, kn_ref, k_ref)):
            scale = inverse[:, part : part + 1]
            for h in range(cols // 128):
                at = slice(h * 128, (h + 1) * 128)
                unit = src[rows, at] * scale
                normed[rows, at] = unit.astype(BF16)
                start = pl.multiple_of(g.me * cols + h * 128, 128)
                value = unit * gain_ref[part : part + 1, pl.ds(start, 128)]
                out[rows, at] = (value * cosine + pltpu.roll(value, 64, 1) * sine).astype(BF16)
        return carry

    lax.fori_loop(0, count // small, finish, 0)


def project(ways, x_full, w_qkv, gains, cosine, sine):
    count, width = x_full.shape
    cols = w_qkv.shape[1] // 3
    low = jax.ShapeDtypeStruct((count, cols), BF16)
    return remote_call(
        functools.partial(project_kernel, ways),
        (low, low, low, low, low, jax.ShapeDtypeStruct((8, count), F32)),
        [VM] * 5,
        (VM,) * 6,
        [
            pltpu.VMEM((count, cols), F32),
            pltpu.VMEM((count, cols), F32),
            pltpu.VMEM((8, count), F32),
            pltpu.VMEM((ways - 1, 8, count), F32),
        ]
        + sems(ways - 1),
        1,
        2 * count * width * 3 * cols,
        40_000_000,
    )(x_full, w_qkv, gains, cosine, sine)


def unproject_kernel(
    ways, gq_ref, gk_ref, gv_ref, q_ref, k_ref, qn_ref, kn_ref, stat_ref, gain_ref, cos_ref, sin_ref,
    out_ref, sums_ref, mine, arrived, total, send, recv,
):
    g = Square(ways)
    greet([{"seq": q} for q in g.everyone()])
    count, cols = gq_ref.shape
    width = gain_ref.shape[1]
    step = tile_of(count, 256)
    mine[...] = jnp.zeros_like(mine)

    def inner(i, carry):
        rows = pl.ds(pl.multiple_of(i * step, step), step)
        for part, grad, rot in ((0, gq_ref, q_ref), (1, gk_ref, k_ref)):
            both = grad[rows, :].astype(F32) * rot[rows, :].astype(F32)
            mine[part : part + 1, rows] = row_sums(both)
        out_ref[rows, 2 * cols : 3 * cols] = gv_ref[rows, :]
        return carry

    lax.fori_loop(0, count // step, inner, 0)
    total[...] = exchange_rows(g, mine, arrived, send, recv)
    sums_ref[...] = jnp.zeros_like(sums_ref)
    small = tile_of(count, 256)

    def finish(i, carry):
        rows = pl.ds(pl.multiple_of(i * small, small), small)
        inverse = lax.rsqrt(as_columns(stat_ref[:, rows]) * (1.0 / width) + NORM_EPS)
        mean = as_columns(total[:, rows]) * (1.0 / width)
        cosine, sine = cos_ref[rows, :], sin_ref[rows, :]
        for part, grad, normed in ((0, gq_ref, qn_ref), (1, gk_ref, kn_ref)):
            scale, centre = inverse[:, part : part + 1], mean[:, part : part + 1]
            for h in range(cols // 128):
                at = slice(h * 128, (h + 1) * 128)
                value = grad[rows, at].astype(F32)
                e = value * cosine - pltpu.roll(value, 64, 1) * sine
                unit = normed[rows, at].astype(F32)
                start = pl.multiple_of(g.me * cols + h * 128, 128)
                gain = gain_ref[part : part + 1, pl.ds(start, 128)]
                to = slice(part * cols + h * 128, part * cols + (h + 1) * 128)
                out_ref[rows, to] = (scale * (e * gain - unit * centre)).astype(BF16)
                sums_ref[part : part + 1, at] += jnp.sum(e * unit, axis=0, keepdims=True)
        return carry

    lax.fori_loop(0, count // small, finish, 0)


def unproject(ways, grads, q_low, k_low, qn, kn, stats, gains, cosine, sine):
    count, cols = q_low.shape
    return remote_call(
        functools.partial(unproject_kernel, ways),
        (jax.ShapeDtypeStruct((count, 3 * cols), BF16), jax.ShapeDtypeStruct((8, cols), F32)),
        [VM] * 11,
        (VM, VM),
        [
            pltpu.VMEM((8, count), F32),
            pltpu.VMEM((ways - 1, 8, count), F32),
            pltpu.VMEM((8, count), F32),
        ]
        + sems(ways - 1),
        2,
        0,
        30_000_000,
    )(*grads, q_low, k_low, qn, kn, stats, gains, cosine, sine)


def bounds_of(lens_ref):
    first = lens_ref[0]
    second = first + lens_ref[1]
    return first, second, second + lens_ref[2]


def first_key(slot, bounds):
    a, b, c = bounds
    return jnp.where(slot < a, 0, jnp.where(slot < b, a, jnp.where(slot < c, b, slot)))


def attend_kernel(head_width, lens_ref, q_ref, k_ref, v_ref, o_ref, lse_ref, acc, top, tot):
    block, cols = q_ref.shape
    heads = cols // head_width
    i = pl.program_id(0)
    bounds = bounds_of(lens_ref)
    slots = i * block + lax.broadcasted_iota(jnp.int32, (1, block), 1)
    begins = first_key(slots, bounds)
    factor = head_width ** (-0.5) * LOG2E

    def scores_of(kb, h):
        at = slice(h * head_width, (h + 1) * head_width)
        rows = pl.ds(pl.multiple_of(kb * block, block), block)
        keys = kb * block + lax.broadcasted_iota(jnp.int32, (block, block), 0)
        visible = (keys <= slots) & (keys >= begins)
        scores = dot_nt(k_ref[rows, at], q_ref[:, at]) * factor
        return jnp.where(visible, scores, MASKED), v_ref[rows, at], at

    for h in range(heads):
        scores, values, at = scores_of(i, h)
        largest = jnp.max(scores, axis=0, keepdims=True)
        weights = jnp.exp2(scores - largest)
        top[h : h + 1, :] = largest
        tot[h : h + 1, :] = jnp.sum(weights, axis=0, keepdims=True)
        acc[at, :] = dot_tn(values, weights.astype(BF16))

    def earlier(t, carry):
        kb = i - 1 - t
        for h in range(heads):
            scores, values, at = scores_of(kb, h)
            before = top[h : h + 1, :]
            largest = jnp.maximum(before, jnp.max(scores, axis=0, keepdims=True))
            weights = jnp.exp2(scores - largest)
            shrink = jnp.exp2(before - largest)
            top[h : h + 1, :] = largest
            tot[h : h + 1, :] = tot[h : h + 1, :] * shrink + jnp.sum(weights, axis=0, keepdims=True)
            acc[at, :] = acc[at, :] * shrink + dot_tn(values, weights.astype(BF16))
        return carry

    lowest = first_key(i * block, bounds) // block
    lax.fori_loop(0, i - lowest, earlier, 0)
    lse_ref[...] = jnp.zeros_like(lse_ref)
    for h in range(heads):
        at = slice(h * head_width, (h + 1) * head_width)
        total = tot[h : h + 1, :]
        o_ref[:, at] = jnp.transpose(acc[at, :] * (1.0 / total)).astype(BF16)
        lse_ref[h : h + 1, :] = top[h : h + 1, :] + jnp.log2(total)


def attend(lens, q_low, k_low, v_low, head_width):
    count, cols = q_low.shape
    block = tile_of(count, 256)
    tile = pl.BlockSpec((block, cols), lambda i, lens: (i, 0))
    whole = pl.BlockSpec((count, cols), lambda i, lens: (0, 0))
    line = pl.BlockSpec((8, block), lambda i, lens: (0, i))
    return pl.pallas_call(
        functools.partial(attend_kernel, head_width),
        out_shape=(jax.ShapeDtypeStruct((count, cols), BF16), jax.ShapeDtypeStruct((8, count), F32)),
        grid_spec=pltpu.PrefetchScalarGridSpec(
            num_scalar_prefetch=1,
            grid=(count // block,),
            in_specs=[tile, whole, whole],
            out_specs=(tile, line),
            scratch_shapes=[pltpu.VMEM((cols, block), F32), pltpu.VMEM((8, block), F32), pltpu.VMEM((8, block), F32)],
        ),
        compiler_params=pltpu.CompilerParams(dimension_semantics=("arbitrary",), vmem_limit_bytes=VMEM_BYTES),
        cost_estimate=pl.CostEstimate(flops=20_000_000_000, bytes_accessed=20_000_000, transcendentals=0),
    )(lens, q_low, k_low, v_low)


def attend_back_kernel(
    head_width, lens_ref, q_ref, g_ref, o_ref, lse_ref, k_ref, v_ref, gq_ref, gk_ref, gv_ref, qacc, kacc, vacc, centre
):
    block, cols = q_ref.shape
    heads = cols // head_width
    i = pl.program_id(0)
    bounds = bounds_of(lens_ref)
    slots = i * block + lax.broadcasted_iota(jnp.int32, (1, block), 1)
    begins = first_key(slots, bounds)
    root = head_width ** (-0.5)
    factor = root * LOG2E

    @pl.when(i == 0)
    def _():
        kacc[...] = jnp.zeros_like(kacc)
        vacc[...] = jnp.zeros_like(vacc)

    for h in range(heads):
        at = slice(h * head_width, (h + 1) * head_width)
        both = g_ref[:, at].astype(F32) * o_ref[:, at].astype(F32)
        centre[h : h + 1, :] = row_sums(both)
    qacc[...] = jnp.zeros_like(qacc)

    def keys_block(t, carry):
        kb = i - t
        rows = pl.ds(pl.multiple_of(kb * block, block), block)
        keys = kb * block + lax.broadcasted_iota(jnp.int32, (block, block), 0)
        visible = (keys <= slots) & (keys >= begins)
        for h in range(heads):
            at = slice(h * head_width, (h + 1) * head_width)
            keys_h, query, grad = k_ref[rows, at], q_ref[:, at], g_ref[:, at]
            scores = dot_nt(keys_h, query) * factor - lse_ref[h : h + 1, :]
            weights = jnp.where(visible, jnp.exp2(scores), 0.0)
            grad_probs = dot_nt(v_ref[rows, at], grad)
            grad_scores = (weights * (grad_probs - centre[h : h + 1, :])).astype(BF16)
            vacc[rows, at] += dot_nn(weights.astype(BF16), grad)
            kacc[rows, at] += dot_nn(grad_scores, query)
            qacc[:, at] += dot_tn(grad_scores, keys_h)
        return carry

    lowest = first_key(i * block, bounds) // block
    lax.fori_loop(0, i - lowest + 1, keys_block, 0)
    gq_ref[...] = (qacc[...] * root).astype(BF16)

    @pl.when(i == pl.num_programs(0) - 1)
    def _():
        gk_ref[...] = (kacc[...] * root).astype(BF16)
        gv_ref[...] = vacc[...].astype(BF16)


def attend_back(lens, q_low, grad, out, lse, k_low, v_low, head_width):
    count, cols = q_low.shape
    block = tile_of(count, 256)
    tile = pl.BlockSpec((block, cols), lambda i, lens: (i, 0))
    whole = pl.BlockSpec((count, cols), lambda i, lens: (0, 0))
    line = pl.BlockSpec((8, block), lambda i, lens: (0, i))
    low = jax.ShapeDtypeStruct((count, cols), BF16)
    return pl.pallas_call(
        functools.partial(attend_back_kernel, head_width),
        out_shape=(low, low, low),
        grid_spec=pltpu.PrefetchScalarGridSpec(
            num_scalar_prefetch=1,
            grid=(count // block,),
            in_specs=[tile, tile, tile, line, whole, whole],
            out_specs=(tile, whole, whole),
            scratch_shapes=[
                pltpu.VMEM((block, cols), F32),
                pltpu.VMEM((count, cols), F32),
                pltpu.VMEM((count, cols), F32),
                pltpu.VMEM((8, block), F32),
            ],
        ),
        compiler_params=pltpu.CompilerParams(dimension_semantics=("arbitrary",), vmem_limit_bytes=VMEM_BYTES),
        cost_estimate=pl.CostEstimate(flops=40_000_000_000, bytes_accessed=30_000_000, transcendentals=0),
    )(lens, q_low, grad, out, lse, k_low, v_low)


def matmul_tiles(ref, rows, pairs, transposed, dtype):
    width = ref.shape[1]
    tile = tile_of(width, 512)

    def body(t, carry):
        at = pl.ds(pl.multiple_of(t * tile, tile), tile)
        value = None
        for lhs, rhs in pairs:
            term = dot_nt(lhs[rows, :], rhs[at, :]) if transposed else dot_nn(lhs[rows, :], rhs[:, at])
            value = term if value is None else value + term
        ref[:, at] = value.astype(dtype)
        return carry

    lax.fori_loop(0, width // tile, body, 0)


def fold8(value):
    return jnp.sum(value.reshape(value.shape[0] // 8, 8, value.shape[1]), axis=0)


def meet_kernel(ways, n_pairs, transposed, gather, epilogue, n_extra, n_out, own_is_out, *refs):
    pairs = [(refs[2 * k], refs[2 * k + 1]) for k in range(n_pairs)]
    refs = refs[2 * n_pairs :]
    extra, outs, scratch = refs[:n_extra], refs[n_extra : n_extra + n_out], refs[n_extra + n_out :]
    own = outs[0] if own_is_out else scratch[0]
    scratch = scratch if own_is_out else scratch[1:]
    out, arrived, relayed, send, recv = scratch[:5]
    g = Square(ways)
    greet([{"seq": q} for q in g.near()])
    count = own.shape[0]

    def rows_of(index):
        return pl.ds(pl.multiple_of(index * count, count), count)

    rs = Scatter(g, out, arrived, relayed, send, recv)
    rs.run(lambda index, ref: matmul_tiles(ref, rows_of(index), pairs, transposed, BF16))
    rs.relay()
    matmul_tiles(own, rows_of(g.me), pairs, transposed, F32)
    rs.finish()
    step = tile_of(count, 64)
    source = rs.spare() if gather else None

    def body(t, carry):
        rows = pl.ds(pl.multiple_of(t * step, step), step)
        epilogue(rows, rs.total(own, rows), extra, outs, source, t)
        return carry

    lax.fori_loop(0, count // step, body, 0)
    if gather:
        ag = Gather(g, source, outs[-1], scratch[5], scratch[6], scratch[7].at[0])
        ag.start()
        ag.relay()
        ag.finish()
    rs.drain()


def meet(ways, pairs, transposed, gather, epilogue, extra, outs, collective_id):
    count = pairs[0][0].shape[0]
    rhs = pairs[0][1]
    width = rhs.shape[0] if transposed else rhs.shape[1]
    rows = count // ways
    n = 6 if ways == 4 else ways - 1
    own_is_out = outs[0].dtype == F32
    scratch = [] if own_is_out else [pltpu.VMEM((rows, width), F32)]
    scratch += Scatter.buffers(ways, rows, width) + sems(n)
    out_specs = [VM] * len(outs)
    if gather:
        outs = [*outs, jax.ShapeDtypeStruct((count, width), BF16)]
        out_specs = [*out_specs, ANY]
        scratch += sems(Gather.sems(ways)) + [pltpu.SemaphoreType.DMA((1,))]
    flops = sum(2 * count * width * (a.shape[1]) for a, _ in pairs)
    return remote_call(
        functools.partial(
            meet_kernel, ways, len(pairs), transposed, gather, epilogue, len(extra), len(outs), own_is_out
        ),
        tuple(outs),
        [VM] * (2 * len(pairs) + len(extra)),
        tuple(out_specs),
        scratch,
        collective_id,
        flops,
        150_000_000,
    )(*[ref for pair in pairs for ref in pair], *extra)


def after_attention(rows, branch, extra, outs, source, t):
    x_ref, gain_ref = extra
    hidden_ref, unit_ref, inv_ref = outs[:3]
    inverse = lax.rsqrt(jnp.mean(branch * branch, axis=1, keepdims=True) + NORM_EPS)
    unit = branch * inverse
    hidden = x_ref[rows, :].astype(F32) + unit * gain_ref[2:3, :]
    hidden_ref[rows, :] = hidden
    unit_ref[rows, :] = unit.astype(BF16)
    inv_ref[rows, :] = jnp.broadcast_to(inverse, (inverse.shape[0], 128))
    source[rows, :] = hidden.astype(BF16)


def after_ffn(rows, branch, extra, outs, source, t):
    hidden_ref, cot_ref, gain_ref = extra
    out_ref, sums_ref = outs[:2]
    gain = gain_ref[3:4, :]
    inverse = lax.rsqrt(jnp.mean(branch * branch, axis=1, keepdims=True) + NORM_EPS)
    unit = branch * inverse
    out_ref[rows, :] = (hidden_ref[rows, :] + unit * gain).astype(BF16)
    e = cot_ref[rows, :].astype(F32)
    term = fold8(e * unit)

    @pl.when(t == 0)
    def _():
        sums_ref[...] = term

    @pl.when(t > 0)
    def _():
        sums_ref[...] += term

    eg = e * gain
    mean = jnp.mean(eg * unit, axis=1, keepdims=True)
    source[rows, :] = (inverse * (eg - unit * mean)).astype(BF16)


def before_ffn(rows, terms, extra, outs, source, t):
    cot_ref, unit_ref, inv_ref, gain_ref = extra
    hidden_ref, sums_ref = outs[:2]
    e = cot_ref[rows, :].astype(F32) + terms
    hidden_ref[rows, :] = e
    unit = unit_ref[rows, :].astype(F32)
    term = fold8(e * unit)

    @pl.when(t == 0)
    def _():
        sums_ref[...] = term

    @pl.when(t > 0)
    def _():
        sums_ref[...] += term

    eg = e * gain_ref[2:3, :]
    mean = jnp.mean(eg * unit, axis=1, keepdims=True)
    source[rows, :] = (inv_ref[rows, 0:1] * (eg - unit * mean)).astype(BF16)


def leave_kernel(
    ways, dp_ways, d_ref, w_ref, hidden_ref, tiles_ref, grad_ref, gains_ref,
    own, out, arrived, relayed, send, recv, from_dp, partial, from_seq, gsend, grecv,
):
    g = Square(ways)
    dp_me = lax.axis_index("dp")
    dp_peers = [lax.rem(dp_me + p, dp_ways) for p in range(1, dp_ways)]
    greet([{"seq": q} for q in g.everyone()] + [{"dp": p} for p in dp_peers])
    first = [
        to_dp(tiles_ref.at[p], from_dp.at[k], gsend.at[k], grecv.at[k], p) for k, p in enumerate(dp_peers)
    ]
    for c in first:
        c.start()
    count = own.shape[0]

    def rows_of(index):
        return pl.ds(pl.multiple_of(index * count, count), count)

    rs = Scatter(g, out, arrived, relayed, send, recv)
    rs.run(lambda index, ref: matmul_tiles(ref, rows_of(index), [(d_ref, w_ref)], True, BF16))
    for c in first:
        c.wait_recv()
    value = tiles_ref[dp_me]
    for k in range(dp_ways - 1):
        value = value + from_dp[k]
    partial[...] = value
    base = dp_ways - 1
    second = [
        to_seq(partial.at[q], from_seq.at[k], gsend.at[base + k], grecv.at[base + k], q)
        for k, q in enumerate(g.everyone())
    ]
    for c in second:
        c.start()
    rs.relay()
    matmul_tiles(own, rows_of(g.me), [(d_ref, w_ref)], True, F32)
    for c in second:
        c.wait_recv()
    value = partial[g.me]
    for k in range(ways - 1):
        value = value + from_seq[k]
    gains_ref[...] = value
    rs.finish()
    step = tile_of(count, 64)

    def body(t, carry):
        rows = pl.ds(pl.multiple_of(t * step, step), step)
        grad_ref[rows, :] = hidden_ref[rows, :] + rs.total(own, rows)
        return carry

    lax.fori_loop(0, count // step, body, 0)
    for c in first + second:
        c.wait_send()
    rs.drain()


def leave(ways, dp_ways, d_qkv, w_qkv, grad_hidden, tiles):
    count, depth = d_qkv.shape
    rows, width = grad_hidden.shape
    n = 6 if ways == 4 else ways - 1
    m = dp_ways - 1 + ways - 1
    return remote_call(
        functools.partial(leave_kernel, ways, dp_ways),
        (jax.ShapeDtypeStruct((rows, width), F32), jax.ShapeDtypeStruct((8, 128), F32)),
        [VM] * 4,
        (VM, VM),
        [pltpu.VMEM((rows, width), F32)]
        + Scatter.buffers(ways, rows, width)
        + sems(n)
        + [
            pltpu.VMEM((dp_ways - 1, ways, 8, 128), F32),
            pltpu.VMEM((ways, 8, 128), F32),
            pltpu.VMEM((ways - 1, 8, 128), F32),
        ]
        + sems(m),
        6,
        2 * count * width * depth,
        80_000_000,
    )(d_qkv, w_qkv, grad_hidden, tiles)


def expand_kernel(h_ref, wg_ref, wu_ref, gate_ref, up_ref, act_ref):
    rows = h_ref[...]
    gate = dot_nn(rows, wg_ref[...])
    up = dot_nn(rows, wu_ref[...])
    gate_ref[...] = gate.astype(BF16)
    up_ref[...] = up.astype(BF16)
    act_ref[...] = (gate * (1.0 / (1.0 + jnp.exp(-gate))) * up).astype(BF16)


def expand(hidden, w_gate, w_up):
    count, width = hidden.shape
    units = w_gate.shape[1]
    tm, tn = tile_of(count, 512), tile_of(units, 512)
    low = jax.ShapeDtypeStruct((count, units), BF16)
    weight = pl.BlockSpec((width, tn), lambda j, i: (0, j))
    tile = pl.BlockSpec((tm, tn), lambda j, i: (i, j))
    return pl.pallas_call(
        expand_kernel,
        out_shape=(low, low, low),
        grid=(units // tn, count // tm),
        in_specs=[pl.BlockSpec((tm, width), lambda j, i: (i, 0)), weight, weight],
        out_specs=(tile, tile, tile),
        compiler_params=pltpu.CompilerParams(
            dimension_semantics=("arbitrary", "arbitrary"), vmem_limit_bytes=VMEM_BYTES
        ),
        cost_estimate=pl.CostEstimate(flops=4 * count * width * units, bytes_accessed=50_000_000, transcendentals=0),
    )(hidden, w_gate, w_up)


def expand_back_kernel(g_ref, w_ref, gate_ref, up_ref, dgate_ref, dup_ref):
    grad = dot_nt(g_ref[...], w_ref[...])
    gate = gate_ref[...].astype(F32)
    up = up_ref[...].astype(F32)
    s = 1.0 / (1.0 + jnp.exp(-gate))
    dgate_ref[...] = (grad * up * s * (1.0 + gate * (1.0 - s))).astype(BF16)
    dup_ref[...] = (grad * gate * s).astype(BF16)


def expand_back(grad, w_down, gate, up):
    count, width = grad.shape
    units = w_down.shape[0]
    tm, tn = tile_of(count, 512), tile_of(units, 512)
    low = jax.ShapeDtypeStruct((count, units), BF16)
    tile = pl.BlockSpec((tm, tn), lambda j, i: (i, j))
    return pl.pallas_call(
        expand_back_kernel,
        out_shape=(low, low),
        grid=(units // tn, count // tm),
        in_specs=[
            pl.BlockSpec((tm, width), lambda j, i: (i, 0)),
            pl.BlockSpec((tn, width), lambda j, i: (j, 0)),
            tile,
            tile,
        ],
        out_specs=(tile, tile),
        compiler_params=pltpu.CompilerParams(
            dimension_semantics=("arbitrary", "arbitrary"), vmem_limit_bytes=VMEM_BYTES
        ),
        cost_estimate=pl.CostEstimate(flops=2 * count * width * units, bytes_accessed=50_000_000, transcendentals=0),
    )(grad, w_down, gate, up)


def rotation_tables(lens, count, head_width):
    slots = jnp.arange(count, dtype=jnp.int32)
    first, second, third = lens[0], lens[0] + lens[1], lens[0] + lens[1] + lens[2]
    start = jnp.where(slots < first, 0, jnp.where(slots < second, first, jnp.where(slots < third, second, third)))
    half = head_width // 2
    lane = jnp.arange(head_width, dtype=jnp.int32)
    frequency = ROPE_BASE ** (-2.0 * (lane % half).astype(F32) / head_width)
    angles = (slots - start).astype(F32)[:, None] * frequency[None, :]
    return jnp.cos(angles), jnp.sin(angles) * jnp.where(lane < half, -1.0, 1.0)[None, :]


def scatter_dp(terms, axis):
    return lax.psum_scatter(terms.astype(BF16), "dp", scatter_dimension=axis, tiled=True).astype(F32)


def gather_dp(weights, axis):
    return lax.all_gather(weights, "dp", axis=axis, tiled=True)


def local(
    layer_in, cotangent, lengths, w_query, w_key, w_value, w_out, w_gate, w_up, w_down,
    gain_query, gain_key, gain_attn, gain_ffn,
):
    rows, width = layer_in.shape
    ways, dp_ways = lax.axis_size("seq"), lax.axis_size("dp")
    count = rows * ways
    head_width = width // HEADS
    cols = width // ways
    part = gain_query.shape[0]
    lens = lengths[0]
    seq_me = lax.axis_index("seq")

    w_qkv = gather_dp(jnp.concatenate([w_query, w_key, w_value], axis=1), 0)
    w_rows = gather_dp(w_out, 1)
    all_gate, all_up, all_down = gather_dp(w_gate, 1), gather_dp(w_up, 1), gather_dp(w_down, 0)

    four = jnp.stack([gain_query, gain_key, gain_attn, gain_ffn]).astype(F32)
    x_full, gain_tiles = enter(ways, dp_ways, layer_in, jnp.pad(four, ((0, 4), (0, 128 - part))))
    gains = gain_tiles[:, :, :4, :part].transpose(2, 1, 0, 3).reshape(4, width)
    cosine, sine = rotation_tables(lens, count, head_width)

    q_low, k_low, v_low, qn, kn, stats = project(ways, x_full, w_qkv, gains, cosine, sine)
    attn, lse = attend(lens, q_low, k_low, v_low, head_width)

    whole = jax.ShapeDtypeStruct((rows, width), F32)
    half = jax.ShapeDtypeStruct((rows, width), BF16)
    eight = jax.ShapeDtypeStruct((8, width), F32)
    hidden, unit_a, inv_a, hidden_full = meet(
        ways, [(attn, w_rows)], False, True, after_attention, (layer_in, gains),
        (whole, half, jax.ShapeDtypeStruct((rows, 128), F32)), 3,
    )
    gate, up, act = expand(hidden_full, all_gate, all_up)
    layer_out, sums_f, grad_m_full = meet(
        ways, [(act, all_down)], False, True, after_ffn, (hidden, cotangent, gains), (half, eight), 4
    )
    grad_down = dot_tn(act, grad_m_full).astype(BF16)
    grad_m_full, grad_down = lax.optimization_barrier((grad_m_full, grad_down))
    out_down = scatter_dp(grad_down, 0)
    d_gate, d_up = expand_back(grad_m_full, all_down, gate, up)
    grad_gate = dot_tn(hidden_full, d_gate).astype(BF16)
    grad_up = dot_tn(hidden_full, d_up).astype(BF16)
    d_gate, d_up, grad_gate, grad_up, out_down = lax.optimization_barrier((d_gate, d_up, grad_gate, grad_up, out_down))
    out_gate = scatter_dp(grad_gate, 1)
    out_up = scatter_dp(grad_up, 1)
    grad_hidden, sums_a, grad_a_full = meet(
        ways, [(d_gate, all_gate), (d_up, all_up)], True, True, before_ffn, (cotangent, unit_a, inv_a, gains),
        (whole, eight), 5,
    )
    grad_attn = dot_nt(grad_a_full, w_rows).astype(BF16)
    grad_rows = dot_tn(attn, grad_a_full).astype(BF16)
    grad_attn, grad_rows, out_gate, out_up = lax.optimization_barrier((grad_attn, grad_rows, out_gate, out_up))
    out_out = scatter_dp(grad_rows, 1)
    grads = attend_back(lens, q_low, grad_attn, attn, lse, k_low, v_low, head_width)
    d_qkv, sums_qk = unproject(ways, grads, q_low, k_low, qn, kn, stats, gains, cosine, sine)
    grad_qkv = dot_tn(x_full, d_qkv).astype(BF16)
    d_qkv, grad_qkv, out_out = lax.optimization_barrier((d_qkv, grad_qkv, out_out))
    out_qkv = scatter_dp(grad_qkv, 0)

    own = lax.dynamic_update_slice(jnp.zeros((2, width), F32), sums_qk[:2], (0, seq_me * cols))
    norms = jnp.stack([jnp.sum(sums_a, axis=0), jnp.sum(sums_f, axis=0)])
    tiles = jnp.concatenate([own, norms]).reshape(4, dp_ways, ways, part).transpose(1, 2, 0, 3)
    tiles = jnp.pad(tiles, ((0, 0), (0, 0), (0, 4), (0, 128 - part)))
    grad_in, gain_sums = leave(ways, dp_ways, d_qkv, w_qkv, grad_hidden, tiles)
    return (
        layer_out,
        grad_in,
        out_qkv[:, :cols],
        out_qkv[:, cols : 2 * cols],
        out_qkv[:, 2 * cols :],
        out_out,
        out_gate,
        out_up,
        out_down,
        gain_sums[0, :part],
        gain_sums[1, :part],
        gain_sums[2, :part],
        gain_sums[3, :part],
    )


def solution(mesh):
    both = P(("dp", "seq"))
    rows = P(("dp", "seq"), None)
    columns = P(None, ("dp", "seq"))
    square = P("dp", "seq")
    in_specs = (
        rows, rows, P("dp", None), square, square, square, P("seq", "dp"), columns, columns, rows, both, both, both, both,
    )
    out_specs = (
        rows, rows, square, square, square, P("seq", "dp"), columns, columns, rows, both, both, both, both,
    )
    return jax.shard_map(local, mesh=mesh, in_specs=in_specs, out_specs=out_specs, check_vma=False)
```

```python
import functools
import math

import jax
import jax.numpy as jnp
from jax import lax
from jax.experimental import pallas as pl
from jax.experimental.pallas import tpu as pltpu
from jax.sharding import PartitionSpec as P

HEADS = 16
NORM_EPS = 1e-06
ROPE_BASE = 500000.0
MASKED = -1e30
LOG2E = 1.4426950408889634

F32 = jnp.float32
BF16 = jnp.bfloat16
MESH = pl.DeviceIdType.MESH
VMEM_BYTES = 60 * 1024 * 1024
ANY = pl.BlockSpec(memory_space=pl.ANY)
VM = pl.BlockSpec(memory_space=pltpu.VMEM)


def dot_nn(a, b):
    return lax.dot_general(a, b, (((1,), (0,)), ((), ())), preferred_element_type=F32)


def dot_nt(a, b):
    return lax.dot_general(a, b, (((1,), (1,)), ((), ())), preferred_element_type=F32)


def dot_tn(a, b):
    return lax.dot_general(a, b, (((0,), (0,)), ((), ())), preferred_element_type=F32)


def row_sums(values):
    folded = values[:, 0:128]
    for k in range(1, values.shape[1] // 128):
        folded = folded + values[:, k * 128 : (k + 1) * 128]
    return jnp.sum(jnp.transpose(folded), axis=0, keepdims=True)


def as_columns(rows8):
    return jnp.transpose(jnp.concatenate([rows8] * 16, axis=0))


def tile_of(extent, most):
    return most if extent % most == 0 else extent


def bounds_of(lens_ref):
    first = lens_ref[0]
    second = first + lens_ref[1]
    return first, second, second + lens_ref[2]


def first_key(slot, bounds):
    a, b, c = bounds
    return jnp.where(slot < a, 0, jnp.where(slot < b, a, jnp.where(slot < c, b, slot)))


class Square:
    def __init__(self, ways):
        self.ways = ways
        self.me = lax.axis_index("seq")
        self.square = ways == 4
        if self.square:
            self.x = self.me + 1 - 2 * lax.rem(self.me, 2)
            self.y = lax.rem(self.me + 2, 4)
            self.d = 3 - self.me

    def peer(self, p):
        return lax.rem(self.me + p, self.ways)

    def near(self):
        if self.square:
            return [self.x, self.y]
        return [self.peer(p) for p in range(1, self.ways)]

    def everyone(self):
        return [self.peer(p) for p in range(1, self.ways)]

    def order(self):
        if self.square:
            return [self.d, self.x, self.y, self.me]
        return self.everyone() + [self.me]


def greet(devices):
    barrier = pltpu.get_barrier_semaphore()
    for device in devices:
        pl.semaphore_signal(barrier, inc=1, device_id=device, device_id_type=MESH)
    pl.semaphore_wait(barrier, len(devices))


def to_seq(src, dst, send, recv, peer):
    return pltpu.make_async_remote_copy(
        src_ref=src, dst_ref=dst, send_sem=send, recv_sem=recv, device_id={"seq": peer}, device_id_type=MESH
    )


def to_dp(src, dst, send, recv, peer):
    return pltpu.make_async_remote_copy(
        src_ref=src, dst_ref=dst, send_sem=send, recv_sem=recv, device_id={"dp": peer}, device_id_type=MESH
    )


class Gather:
    def __init__(self, group, src, full, send, recv, own_sem):
        self.g, self.src, self.full, self.send, self.recv = group, src, full, send, recv
        self.rows = src.shape[0]
        self.own = pltpu.make_async_copy(src, self.chunk(group.me), own_sem)

    @staticmethod
    def sems(ways):
        return 6 if ways == 4 else ways - 1

    def chunk(self, index):
        return self.full.at[pl.ds(index * self.rows, self.rows)]

    def half(self, index, which):
        h = self.rows // 2
        return self.full.at[pl.ds(index * self.rows + which * h, h)]

    def cp(self, k, src, dst, peer):
        return to_seq(src, dst, self.send.at[k], self.recv.at[k], peer)

    def start(self):
        g, h = self.g, self.rows // 2
        if g.square:
            top, low = self.src.at[pl.ds(0, h)], self.src.at[pl.ds(h, h)]
            self.first = [
                self.cp(0, top, self.half(g.me, 0), g.x),
                self.cp(1, low, self.half(g.me, 1), g.y),
                self.cp(2, low, self.half(g.me, 1), g.x),
                self.cp(3, top, self.half(g.me, 0), g.y),
            ]
        else:
            self.first = [self.cp(p - 1, self.src, self.chunk(g.me), g.peer(p)) for p in range(1, g.ways)]
        for c in self.first:
            c.start()
        self.own.start()

    def relay(self):
        g = self.g
        if g.square:
            self.first[0].wait_recv()
            a = self.cp(4, self.half(g.x, 0), self.half(g.x, 0), g.y)
            a.start()
            self.first[1].wait_recv()
            b = self.cp(5, self.half(g.y, 1), self.half(g.y, 1), g.x)
            b.start()
            self.second = [a, b]
        else:
            self.second = []

    def arrive(self, k):
        g = self.g
        if k == 0:
            self.own.wait()
            return g.me
        if not g.square:
            self.first[k - 1].wait_recv()
            return lax.rem(g.me + g.ways - k, g.ways)
        if k < 3:
            self.first[k + 1].wait_recv()
            return (g.x, g.y)[k - 1]
        for c in self.second:
            c.wait_recv()
        return g.d

    def drain(self):
        for c in self.first + self.second:
            c.wait_send()


class Scatter:
    @staticmethod
    def buffers(ways, rows, width):
        if ways == 4:
            return [
                pltpu.VMEM((3, rows, width), BF16),
                pltpu.VMEM((2, rows, width), BF16),
                pltpu.VMEM((2, rows // 2, width), BF16),
            ]
        return [
            pltpu.VMEM((ways - 1, rows, width), BF16),
            pltpu.VMEM((ways - 1, rows, width), BF16),
            pltpu.VMEM((2, 16, width), BF16),
        ]

    def __init__(self, group, out, arrived, relayed, send, recv):
        self.g, self.out, self.arrived, self.relayed, self.send, self.recv = group, out, arrived, relayed, send, recv
        self.rows = out.shape[1]

    def cp(self, k, src, dst, peer):
        return to_seq(src, dst, self.send.at[k], self.recv.at[k], peer)

    def run(self, partial):
        g, h = self.g, self.rows // 2
        out, arrived, relayed = self.out, self.arrived, self.relayed
        if not g.square:
            self.sent = []
            for p in range(1, g.ways):
                partial(out.at[p - 1])
                c = self.cp(p - 1, out.at[p - 1], arrived.at[p - 1], g.peer(p))
                c.start()
                self.sent.append(c)
            return
        top, low = pl.ds(0, h), pl.ds(h, h)
        partial(out.at[2])
        c0 = self.cp(0, out.at[2, top], relayed.at[0], g.x)
        c1 = self.cp(1, out.at[2, low], relayed.at[1], g.y)
        c0.start()
        c1.start()
        partial(out.at[0])
        c2 = self.cp(2, out.at[0, top], arrived.at[0, top], g.x)
        c2.start()
        partial(out.at[1])
        c3 = self.cp(3, out.at[1, low], arrived.at[1, low], g.y)
        c3.start()
        self.sent = [c0, c1, c2, c3]

    def relay(self):
        g, h = self.g, self.rows // 2
        if not g.square:
            return
        out, arrived, relayed = self.out, self.arrived, self.relayed
        top, low = pl.ds(0, h), pl.ds(h, h)
        c0, c1, c2, c3 = self.sent
        step = tile_of(h, 64)

        def add(slot, base, which):
            def body(t, carry):
                rows = pl.ds(base + t * step, step)
                have = out[slot, rows, :].astype(F32)
                out[slot, rows, :] = (have + relayed[which, pl.ds(t * step, step), :].astype(F32)).astype(BF16)
                return carry

            lax.fori_loop(0, h // step, body, 0)

        c1.wait_recv()
        add(0, h, 1)
        c4 = self.cp(4, out.at[0, low], arrived.at[0, low], g.x)
        c4.start()
        c0.wait_recv()
        add(1, 0, 0)
        c5 = self.cp(5, out.at[1, top], arrived.at[1, top], g.y)
        c5.start()
        self.sent += [c4, c5]

    def finish(self):
        for c in self.sent[2:] if self.g.square else self.sent:
            c.wait_recv()

    def drain(self):
        for c in self.sent:
            c.wait_send()

    def total(self, own, rows):
        value = own[rows, :]
        for k in range(self.arrived.shape[0]):
            value = value + self.arrived[k, rows, :].astype(F32)
        return value


def remote_call(kernel, outs, in_specs, out_specs, scratch, collective_id, flops, nbytes):
    return pl.pallas_call(
        kernel,
        out_shape=outs,
        in_specs=in_specs,
        out_specs=out_specs,
        scratch_shapes=scratch,
        compiler_params=pltpu.CompilerParams(
            collective_id=collective_id, has_side_effects=True, vmem_limit_bytes=VMEM_BYTES
        ),
        cost_estimate=pl.CostEstimate(flops=0, bytes_accessed=nbytes, transcendentals=0),
    )


def sems(n):
    return [pltpu.SemaphoreType.DMA((n,)), pltpu.SemaphoreType.DMA((n,))]


def write_tables(lens_ref, cos_ref, sin_ref):
    count, head_width = cos_ref.shape
    half = head_width // 2
    step = tile_of(count, 256)
    bounds = bounds_of(lens_ref)
    lane = lax.broadcasted_iota(jnp.int32, (1, head_width), 1)
    folded = jnp.where(lane < half, lane, lane - half).astype(F32)
    frequency = jnp.exp(folded * (-2.0 / head_width * math.log(ROPE_BASE)))
    sign = jnp.where(lane < half, -1.0, 1.0)

    def body(t, carry):
        rows = pl.ds(pl.multiple_of(t * step, step), step)
        slots = t * step + lax.broadcasted_iota(jnp.int32, (step, head_width), 0)
        a, b, c = bounds
        begin = jnp.where(slots < a, 0, jnp.where(slots < b, a, jnp.where(slots < c, b, c)))
        angles = (slots - begin).astype(F32) * frequency
        cos_ref[rows, :] = jnp.cos(angles)
        sin_ref[rows, :] = jnp.sin(angles) * sign
        return carry

    lax.fori_loop(0, count // step, body, 0)


def enter_kernel(
    ways, dp_ways, lens_ref, x_ref, gain_ref, full_ref, gains_ref, cos_ref, sin_ref,
    send, recv, own_sem, gsend, grecv,
):
    g = Square(ways)
    dp_me = lax.axis_index("dp")
    dp_peers = [lax.rem(dp_me + p, dp_ways) for p in range(1, dp_ways)]
    greet([{"seq": q} for q in g.everyone()] + [{"dp": p} for p in dp_peers])
    ag = Gather(g, x_ref, full_ref, send, recv, own_sem.at[0])
    ag.start()

    gains_ref[g.me, dp_me] = gain_ref[...]
    first = [
        to_dp(gain_ref, gains_ref.at[g.me, dp_me], gsend.at[k], grecv.at[k], p) for k, p in enumerate(dp_peers)
    ]
    for c in first:
        c.start()
    write_tables(lens_ref, cos_ref, sin_ref)
    for c in first:
        c.wait_recv()
    base = dp_ways - 1
    second = [
        to_seq(gains_ref.at[g.me], gains_ref.at[g.me], gsend.at[base + k], grecv.at[base + k], q)
        for k, q in enumerate(g.everyone())
    ]
    for c in second:
        c.start()
    ag.relay()
    for c in second:
        c.wait_recv()
    for c in first + second:
        c.wait_send()
    for k in range(ways):
        ag.arrive(k)
    ag.drain()


def enter(ways, dp_ways, lens, x, gains):
    rows, width = x.shape
    count, head_width = ways * rows, width // HEADS
    table = jax.ShapeDtypeStruct((count, head_width), F32)
    return remote_call(
        functools.partial(enter_kernel, ways, dp_ways),
        (
            jax.ShapeDtypeStruct((count, width), BF16),
            jax.ShapeDtypeStruct((ways, dp_ways, 8, 128), F32),
            table,
            table,
        ),
        [pl.BlockSpec(memory_space=pltpu.SMEM), ANY, VM],
        (ANY, VM, VM, VM),
        sems(Gather.sems(ways))
        + [pltpu.SemaphoreType.DMA((1,))]
        + sems(dp_ways - 1 + ways - 1),
        0,
        0,
        1_000_000,
    )(lens, x, gains)


def exchange_rows(g, mine, arrived, send, recv):
    copies = [
        to_seq(mine, arrived.at[k], send.at[k], recv.at[k], q) for k, q in enumerate(g.everyone())
    ]
    for c in copies:
        c.start()
    for c in copies:
        c.wait_recv()
    total = mine[...]
    for k in range(g.ways - 1):
        total = total + arrived[k]
    for c in copies:
        c.wait_send()
    return total


class Columns:
    @staticmethod
    def sems(dp_ways):
        return sems(dp_ways - 1) + [pltpu.SemaphoreType.DMA((1,))]

    def __init__(self, dp_ways, src, full, send, recv, own_sem):
        self.ways, self.full, self.send, self.recv = dp_ways, full, send, recv
        self.me = lax.axis_index("dp")
        self.part = src.shape[1]
        self.chips = dp_ways // 2
        self.mate = self.me + 1 - 2 * lax.rem(self.me, 2)
        self.away = [lax.rem(self.me + 2 * k, dp_ways) for k in range(1, self.chips)]
        mine = self.block(self.me)
        self.own = pltpu.make_async_copy(src, mine, own_sem)
        self.outward = [to_dp(src, mine, send.at[k], recv.at[k], p) for k, p in enumerate([*self.away, self.mate])]

    def peers(self):
        return [*self.away, self.mate]

    def block(self, p):
        return self.full.at[:, pl.ds(pl.multiple_of(p * self.part, self.part), self.part)]

    def start(self):
        self.own.start()
        for c in self.outward:
            c.start()

    def relay(self):
        self.inward = []
        for k in range(1, self.chips):
            self.outward[k - 1].wait_recv()
            source = self.block(lax.rem(self.me + self.ways - 2 * k, self.ways))
            at = self.chips - 1 + k
            c = to_dp(source, source, self.send.at[at], self.recv.at[at], self.mate)
            c.start()
            self.inward.append(c)

    def finish(self):
        self.outward[self.chips - 1].wait_recv()
        for c in self.inward:
            c.wait_recv()
        for c in self.outward + self.inward:
            c.wait_send()
        self.own.wait()


def project_kernel(
    ways, dp_ways, x_ref, w_ref, wo_ref, gain_ref, cos_ref, sin_ref,
    q_ref, k_ref, v_ref, qn_ref, kn_ref, stat_ref, rows_ref,
    qf, kf, mine, arrived, send, recv, wsend, wrecv, own_sem, buffer, ready,
):
    g = Square(ways)
    count, width = x_ref.shape
    cols = q_ref.shape[1]
    step = buffer.shape[1]
    steps = count // step

    def fetch(i, slot):
        rows = pl.ds(pl.multiple_of(i * step, step), step)
        return pltpu.make_async_copy(x_ref.at[rows], buffer.at[slot], ready.at[slot])

    fetch(0, 0).start()
    across = Columns(dp_ways, wo_ref, rows_ref, wsend, wrecv, own_sem.at[0])
    greet([{"seq": q} for q in g.everyone()] + [{"dp": p} for p in across.peers()])
    across.start()
    mine[...] = jnp.zeros_like(mine)

    def project(i, carry):
        slot = lax.rem(i, 2)

        @pl.when(i + 1 < steps)
        def _():
            fetch(i + 1, 1 - slot).start()

        fetch(i, slot).wait()
        rows = pl.ds(pl.multiple_of(i * step, step), step)
        xs = buffer[slot]
        for part, ref in ((0, qf), (1, kf)):
            value = dot_nn(xs, w_ref[:, part * cols : (part + 1) * cols])
            ref[rows, :] = value
            mine[part : part + 1, rows] = row_sums(value * value)
        v_ref[rows, :] = dot_nn(xs, w_ref[:, 2 * cols : 3 * cols]).astype(BF16)
        return carry

    lax.fori_loop(0, steps, project, 0)
    stat_ref[...] = exchange_rows(g, mine, arrived, send, recv)
    small = tile_of(count, 256)

    def finish(i, carry):
        rows = pl.ds(pl.multiple_of(i * small, small), small)
        inverse = lax.rsqrt(as_columns(stat_ref[:, rows]) * (1.0 / width) + NORM_EPS)
        cosine, sine = cos_ref[rows, :], sin_ref[rows, :]
        for part, src, normed, out in ((0, qf, qn_ref, q_ref), (1, kf, kn_ref, k_ref)):
            scale = inverse[:, part : part + 1]
            for h in range(cols // 128):
                at = slice(h * 128, (h + 1) * 128)
                unit = src[rows, at] * scale
                normed[rows, at] = unit.astype(BF16)
                start = pl.multiple_of(g.me * cols + h * 128, 128)
                value = unit * gain_ref[part : part + 1, pl.ds(start, 128)]
                out[rows, at] = (value * cosine + pltpu.roll(value, 64, 1) * sine).astype(BF16)
        return carry

    lax.fori_loop(0, count // small, finish, 0)
    across.relay()
    across.finish()


def project(ways, dp_ways, x_full, w_qkv, w_out, gains, cosine, sine):
    count, width = x_full.shape
    cols = w_qkv.shape[1] // 3
    step = tile_of(count, 512)
    low = jax.ShapeDtypeStruct((count, cols), BF16)
    return remote_call(
        functools.partial(project_kernel, ways, dp_ways),
        (
            low, low, low, low, low, jax.ShapeDtypeStruct((8, count), F32),
            jax.ShapeDtypeStruct((w_out.shape[0], width), BF16),
        ),
        [ANY, VM, ANY, VM, VM, VM],
        (VM,) * 6 + (ANY,),
        [
            pltpu.VMEM((count, cols), F32),
            pltpu.VMEM((count, cols), F32),
            pltpu.VMEM((8, count), F32),
            pltpu.VMEM((ways - 1, 8, count), F32),
        ]
        + sems(ways - 1)
        + Columns.sems(dp_ways)
        + [pltpu.VMEM((2, step, width), BF16), pltpu.SemaphoreType.DMA((2,))],
        1,
        2 * count * width * 3 * cols,
        1_000_000,
    )(x_full, w_qkv, w_out, gains, cosine, sine)


def unproject_kernel(
    ways, gq_ref, gk_ref, gv_ref, q_ref, k_ref, qn_ref, kn_ref, stat_ref, gain_ref, cos_ref, sin_ref,
    out_ref, sums_ref, mine, arrived, total, send, recv,
):
    g = Square(ways)
    greet([{"seq": q} for q in g.everyone()])
    count, cols = gq_ref.shape
    width = gain_ref.shape[1]
    step = tile_of(count, 256)
    mine[...] = jnp.zeros_like(mine)

    def inner(i, carry):
        rows = pl.ds(pl.multiple_of(i * step, step), step)
        for part, grad, rot in ((0, gq_ref, q_ref), (1, gk_ref, k_ref)):
            both = grad[rows, :].astype(F32) * rot[rows, :].astype(F32)
            mine[part : part + 1, rows] = row_sums(both)
        out_ref[rows, 2 * cols : 3 * cols] = gv_ref[rows, :]
        return carry

    lax.fori_loop(0, count // step, inner, 0)
    total[...] = exchange_rows(g, mine, arrived, send, recv)
    sums_ref[...] = jnp.zeros_like(sums_ref)
    small = tile_of(count, 256)

    def finish(i, carry):
        rows = pl.ds(pl.multiple_of(i * small, small), small)
        inverse = lax.rsqrt(as_columns(stat_ref[:, rows]) * (1.0 / width) + NORM_EPS)
        mean = as_columns(total[:, rows]) * (1.0 / width)
        cosine, sine = cos_ref[rows, :], sin_ref[rows, :]
        for part, grad, normed in ((0, gq_ref, qn_ref), (1, gk_ref, kn_ref)):
            scale, centre = inverse[:, part : part + 1], mean[:, part : part + 1]
            for h in range(cols // 128):
                at = slice(h * 128, (h + 1) * 128)
                value = grad[rows, at].astype(F32)
                e = value * cosine - pltpu.roll(value, 64, 1) * sine
                unit = normed[rows, at].astype(F32)
                start = pl.multiple_of(g.me * cols + h * 128, 128)
                gain = gain_ref[part : part + 1, pl.ds(start, 128)]
                to = slice(part * cols + h * 128, part * cols + (h + 1) * 128)
                out_ref[rows, to] = (scale * (e * gain - unit * centre)).astype(BF16)
                sums_ref[part : part + 1, at] += jnp.sum(e * unit, axis=0, keepdims=True)
        return carry

    lax.fori_loop(0, count // small, finish, 0)


def unproject(ways, grads, q_low, k_low, qn, kn, stats, gains, cosine, sine):
    count, cols = q_low.shape
    return remote_call(
        functools.partial(unproject_kernel, ways),
        (jax.ShapeDtypeStruct((count, 3 * cols), BF16), jax.ShapeDtypeStruct((8, cols), F32)),
        [VM] * 11,
        (VM, VM),
        [
            pltpu.VMEM((8, count), F32),
            pltpu.VMEM((ways - 1, 8, count), F32),
            pltpu.VMEM((8, count), F32),
        ]
        + sems(ways - 1),
        2,
        0,
        1_000_000,
    )(*grads, q_low, k_low, qn, kn, stats, gains, cosine, sine)


def attend_kernel(head_width, lens_ref, q_ref, k_ref, v_ref, o_ref, lse_ref, acc, top, tot):
    block, cols = q_ref.shape
    heads = cols // head_width
    i = pl.program_id(0)
    bounds = bounds_of(lens_ref)
    slots = i * block + lax.broadcasted_iota(jnp.int32, (1, block), 1)
    begins = first_key(slots, bounds)
    factor = head_width ** (-0.5) * LOG2E

    def scores_of(kb, h):
        at = slice(h * head_width, (h + 1) * head_width)
        rows = pl.ds(pl.multiple_of(kb * block, block), block)
        keys = kb * block + lax.broadcasted_iota(jnp.int32, (block, block), 0)
        visible = (keys <= slots) & (keys >= begins)
        scores = dot_nt(k_ref[rows, at], q_ref[:, at]) * factor
        return jnp.where(visible, scores, MASKED), v_ref[rows, at], at

    for h in range(heads):
        scores, values, at = scores_of(i, h)
        largest = jnp.max(scores, axis=0, keepdims=True)
        weights = jnp.exp2(scores - largest)
        top[h : h + 1, :] = largest
        tot[h : h + 1, :] = jnp.sum(weights, axis=0, keepdims=True)
        acc[at, :] = dot_tn(values, weights.astype(BF16))

    def earlier(t, carry):
        kb = i - 1 - t
        for h in range(heads):
            scores, values, at = scores_of(kb, h)
            before = top[h : h + 1, :]
            largest = jnp.maximum(before, jnp.max(scores, axis=0, keepdims=True))
            weights = jnp.exp2(scores - largest)
            shrink = jnp.exp2(before - largest)
            top[h : h + 1, :] = largest
            tot[h : h + 1, :] = tot[h : h + 1, :] * shrink + jnp.sum(weights, axis=0, keepdims=True)
            acc[at, :] = acc[at, :] * shrink + dot_tn(values, weights.astype(BF16))
        return carry

    lowest = first_key(i * block, bounds) // block
    lax.fori_loop(0, i - lowest, earlier, 0)
    lse_ref[...] = jnp.zeros_like(lse_ref)
    for h in range(heads):
        at = slice(h * head_width, (h + 1) * head_width)
        total = tot[h : h + 1, :]
        o_ref[:, at] = jnp.transpose(acc[at, :] * (1.0 / total)).astype(BF16)
        lse_ref[h : h + 1, :] = top[h : h + 1, :] + jnp.log2(total)


def attend(lens, q_low, k_low, v_low, head_width):
    count, cols = q_low.shape
    block = tile_of(count, 256)
    tile = pl.BlockSpec((block, cols), lambda i, lens: (i, 0))
    whole = pl.BlockSpec((count, cols), lambda i, lens: (0, 0))
    line = pl.BlockSpec((8, block), lambda i, lens: (0, i))
    return pl.pallas_call(
        functools.partial(attend_kernel, head_width),
        out_shape=(jax.ShapeDtypeStruct((count, cols), BF16), jax.ShapeDtypeStruct((8, count), F32)),
        grid_spec=pltpu.PrefetchScalarGridSpec(
            num_scalar_prefetch=1,
            grid=(count // block,),
            in_specs=[tile, whole, whole],
            out_specs=(tile, line),
            scratch_shapes=[pltpu.VMEM((cols, block), F32), pltpu.VMEM((8, block), F32), pltpu.VMEM((8, block), F32)],
        ),
        compiler_params=pltpu.CompilerParams(dimension_semantics=("arbitrary",), vmem_limit_bytes=VMEM_BYTES),
        cost_estimate=pl.CostEstimate(flops=0, bytes_accessed=1_000_000, transcendentals=0),
    )(lens, q_low, k_low, v_low)


def attend_back_kernel(
    head_width, lens_ref, q_ref, g_ref, o_ref, lse_ref, k_ref, v_ref, gq_ref, gk_ref, gv_ref, qacc, kacc, vacc, centre
):
    block, cols = q_ref.shape
    heads = cols // head_width
    i = pl.program_id(0)
    bounds = bounds_of(lens_ref)
    slots = i * block + lax.broadcasted_iota(jnp.int32, (1, block), 1)
    begins = first_key(slots, bounds)
    root = head_width ** (-0.5)
    factor = root * LOG2E

    @pl.when(i == 0)
    def _():
        kacc[...] = jnp.zeros_like(kacc)
        vacc[...] = jnp.zeros_like(vacc)

    for h in range(heads):
        at = slice(h * head_width, (h + 1) * head_width)
        both = g_ref[:, at].astype(F32) * o_ref[:, at].astype(F32)
        centre[h : h + 1, :] = row_sums(both)
    qacc[...] = jnp.zeros_like(qacc)

    def keys_block(t, carry):
        kb = i - t
        rows = pl.ds(pl.multiple_of(kb * block, block), block)
        keys = kb * block + lax.broadcasted_iota(jnp.int32, (block, block), 0)
        visible = (keys <= slots) & (keys >= begins)
        for h in range(heads):
            at = slice(h * head_width, (h + 1) * head_width)
            keys_h, query, grad = k_ref[rows, at], q_ref[:, at], g_ref[:, at]
            scores = dot_nt(keys_h, query) * factor - lse_ref[h : h + 1, :]
            weights = jnp.where(visible, jnp.exp2(scores), 0.0)
            grad_probs = dot_nt(v_ref[rows, at], grad)
            grad_scores = (weights * (grad_probs - centre[h : h + 1, :])).astype(BF16)
            vacc[rows, at] += dot_nn(weights.astype(BF16), grad)
            kacc[rows, at] += dot_nn(grad_scores, query)
            qacc[:, at] += dot_tn(grad_scores, keys_h)
        return carry

    lowest = first_key(i * block, bounds) // block
    lax.fori_loop(0, i - lowest + 1, keys_block, 0)
    gq_ref[...] = (qacc[...] * root).astype(BF16)

    @pl.when(i == pl.num_programs(0) - 1)
    def _():
        gk_ref[...] = (kacc[...] * root).astype(BF16)
        gv_ref[...] = vacc[...].astype(BF16)


def attend_back(lens, q_low, grad, out, lse, k_low, v_low, head_width):
    count, cols = q_low.shape
    block = tile_of(count, 256)
    tile = pl.BlockSpec((block, cols), lambda i, lens: (i, 0))
    whole = pl.BlockSpec((count, cols), lambda i, lens: (0, 0))
    line = pl.BlockSpec((8, block), lambda i, lens: (0, i))
    low = jax.ShapeDtypeStruct((count, cols), BF16)
    return pl.pallas_call(
        functools.partial(attend_back_kernel, head_width),
        out_shape=(low, low, low),
        grid_spec=pltpu.PrefetchScalarGridSpec(
            num_scalar_prefetch=1,
            grid=(count // block,),
            in_specs=[tile, tile, tile, line, whole, whole],
            out_specs=(tile, whole, whole),
            scratch_shapes=[
                pltpu.VMEM((block, cols), F32),
                pltpu.VMEM((count, cols), F32),
                pltpu.VMEM((count, cols), F32),
                pltpu.VMEM((8, block), F32),
            ],
        ),
        compiler_params=pltpu.CompilerParams(dimension_semantics=("arbitrary",), vmem_limit_bytes=VMEM_BYTES),
        cost_estimate=pl.CostEstimate(flops=0, bytes_accessed=1_000_000, transcendentals=0),
    )(lens, q_low, grad, out, lse, k_low, v_low)


def matmul_tiles(ref, pairs, transposed, dtype):
    width = ref.shape[1]
    tile = tile_of(width, 512)

    def body(t, carry):
        at = pl.ds(pl.multiple_of(t * tile, tile), tile)
        value = None
        for lhs, rhs in pairs:
            term = dot_nt(lhs[...], rhs[at, :]) if transposed else dot_nn(lhs[...], rhs[:, at])
            value = term if value is None else value + term
        ref[:, at] = value.astype(dtype)
        return carry

    lax.fori_loop(0, width // tile, body, 0)


class Rows:
    def __init__(self, order, refs, buffer, ready):
        self.order, self.refs, self.buffer, self.ready = order, refs, buffer, ready
        self.turn = 0

    @staticmethod
    def scratch(n, rows, depth):
        return [pltpu.VMEM((2, n, rows, depth), BF16), pltpu.SemaphoreType.DMA((2, n))]

    def copies(self, turn):
        count = self.buffer.shape[2]
        rows = pl.ds(pl.multiple_of(self.order[turn] * count, count), count)
        slot = turn % 2
        return [
            pltpu.make_async_copy(ref.at[rows], self.buffer.at[slot, j], self.ready.at[slot, j])
            for j, ref in enumerate(self.refs)
        ]

    def start(self):
        for c in self.copies(0):
            c.start()

    def next(self):
        turn = self.turn
        self.turn += 1
        if turn + 1 < len(self.order):
            for c in self.copies(turn + 1):
                c.start()
        for c in self.copies(turn):
            c.wait()
        return [self.buffer.at[turn % 2, j] for j in range(len(self.refs))]


def fold8(value):
    return jnp.sum(value.reshape(value.shape[0] // 8, 8, value.shape[1]), axis=0)


def meet_kernel(ways, n_pairs, transposed, epilogue, n_extra, n_out, own_is_out, *refs):
    pairs = [(refs[2 * k], refs[2 * k + 1]) for k in range(n_pairs)]
    refs = refs[2 * n_pairs :]
    extra, outs, scratch = refs[:n_extra], refs[n_extra : n_extra + n_out], refs[n_extra + n_out :]
    own = outs[0] if own_is_out else scratch[0]
    scratch = scratch if own_is_out else scratch[1:]
    out, arrived, relayed, send, recv, buffer, ready = scratch
    g = Square(ways)
    left = Rows(g.order(), [lhs for lhs, _ in pairs], buffer, ready)
    left.start()
    greet([{"seq": q} for q in g.near()])
    count = own.shape[0]

    def terms(ref, dtype):
        matmul_tiles(ref, [(lhs, rhs) for lhs, (_, rhs) in zip(left.next(), pairs)], transposed, dtype)

    rs = Scatter(g, out, arrived, relayed, send, recv)
    rs.run(lambda ref: terms(ref, BF16))
    rs.relay()
    terms(own, F32)
    rs.finish()
    step = tile_of(count, 64)

    def body(t, carry):
        rows = pl.ds(pl.multiple_of(t * step, step), step)
        epilogue(rows, rs.total(own, rows), extra, outs, t)
        return carry

    lax.fori_loop(0, count // step, body, 0)
    rs.drain()


def meet(ways, pairs, transposed, epilogue, extra, outs, collective_id):
    count = pairs[0][0].shape[0]
    rhs = pairs[0][1]
    width = rhs.shape[0] if transposed else rhs.shape[1]
    rows = count // ways
    n = 6 if ways == 4 else ways - 1
    own_is_out = outs[0].dtype == F32
    scratch = [] if own_is_out else [pltpu.VMEM((rows, width), F32)]
    scratch += Scatter.buffers(ways, rows, width) + sems(n) + Rows.scratch(len(pairs), rows, pairs[0][0].shape[1])
    flops = sum(2 * count * width * (a.shape[1]) for a, _ in pairs)
    return remote_call(
        functools.partial(meet_kernel, ways, len(pairs), transposed, epilogue, len(extra), len(outs), own_is_out),
        tuple(outs),
        [ANY, VM] * len(pairs) + [VM] * len(extra),
        (VM,) * len(outs),
        scratch,
        collective_id,
        flops,
        1_000_000,
    )(*[ref for pair in pairs for ref in pair], *extra)


def after_attention(rows, branch, extra, outs, t):
    x_ref, gain_ref = extra
    hidden_ref, unit_ref, inv_ref, source = outs
    inverse = lax.rsqrt(jnp.mean(branch * branch, axis=1, keepdims=True) + NORM_EPS)
    unit = branch * inverse
    hidden = x_ref[rows, :].astype(F32) + unit * gain_ref[2:3, :]
    hidden_ref[rows, :] = hidden
    unit_ref[rows, :] = unit.astype(BF16)
    inv_ref[rows, :] = jnp.broadcast_to(inverse, (inverse.shape[0], 128))
    source[rows, :] = hidden.astype(BF16)


def after_ffn(rows, branch, extra, outs, t):
    hidden_ref, cot_ref, gain_ref = extra
    out_ref, sums_ref, source = outs
    gain = gain_ref[3:4, :]
    inverse = lax.rsqrt(jnp.mean(branch * branch, axis=1, keepdims=True) + NORM_EPS)
    unit = branch * inverse
    out_ref[rows, :] = (hidden_ref[rows, :] + unit * gain).astype(BF16)
    e = cot_ref[rows, :].astype(F32)
    term = fold8(e * unit)

    @pl.when(t == 0)
    def _():
        sums_ref[...] = term

    @pl.when(t > 0)
    def _():
        sums_ref[...] += term

    eg = e * gain
    mean = jnp.mean(eg * unit, axis=1, keepdims=True)
    source[rows, :] = (inverse * (eg - unit * mean)).astype(BF16)


def before_ffn(rows, terms, extra, outs, t):
    cot_ref, unit_ref, inv_ref, gain_ref = extra
    hidden_ref, sums_ref, source = outs
    e = cot_ref[rows, :].astype(F32) + terms
    hidden_ref[rows, :] = e
    unit = unit_ref[rows, :].astype(F32)
    term = fold8(e * unit)

    @pl.when(t == 0)
    def _():
        sums_ref[...] = term

    @pl.when(t > 0)
    def _():
        sums_ref[...] += term

    eg = e * gain_ref[2:3, :]
    mean = jnp.mean(eg * unit, axis=1, keepdims=True)
    source[rows, :] = (inv_ref[rows, 0:1] * (eg - unit * mean)).astype(BF16)


def leave_kernel(
    ways, dp_ways, d_ref, w_ref, hidden_ref, tiles_ref, grad_ref, gains_ref,
    own, out, arrived, relayed, send, recv, from_dp, partial, from_seq, gsend, grecv, buffer, ready,
):
    g = Square(ways)
    left = Rows(g.order(), [d_ref], buffer, ready)
    left.start()
    dp_me = lax.axis_index("dp")
    dp_peers = [lax.rem(dp_me + p, dp_ways) for p in range(1, dp_ways)]
    greet([{"seq": q} for q in g.everyone()] + [{"dp": p} for p in dp_peers])
    first = [
        to_dp(tiles_ref.at[p], from_dp.at[k], gsend.at[k], grecv.at[k], p) for k, p in enumerate(dp_peers)
    ]
    for c in first:
        c.start()
    count = own.shape[0]

    rs = Scatter(g, out, arrived, relayed, send, recv)
    rs.run(lambda ref: matmul_tiles(ref, [(left.next()[0], w_ref)], True, BF16))
    for c in first:
        c.wait_recv()
    value = tiles_ref[dp_me]
    for k in range(dp_ways - 1):
        value = value + from_dp[k]
    partial[...] = value
    base = dp_ways - 1
    second = [
        to_seq(partial.at[q], from_seq.at[k], gsend.at[base + k], grecv.at[base + k], q)
        for k, q in enumerate(g.everyone())
    ]
    for c in second:
        c.start()
    rs.relay()
    matmul_tiles(own, [(left.next()[0], w_ref)], True, F32)
    for c in second:
        c.wait_recv()
    value = partial[g.me]
    for k in range(ways - 1):
        value = value + from_seq[k]
    gains_ref[...] = value
    rs.finish()
    step = tile_of(count, 64)

    def body(t, carry):
        rows = pl.ds(pl.multiple_of(t * step, step), step)
        grad_ref[rows, :] = hidden_ref[rows, :] + rs.total(own, rows)
        return carry

    lax.fori_loop(0, count // step, body, 0)
    for c in first + second:
        c.wait_send()
    rs.drain()


def leave(ways, dp_ways, d_qkv, w_qkv, grad_hidden, tiles):
    count, depth = d_qkv.shape
    rows, width = grad_hidden.shape
    n = 6 if ways == 4 else ways - 1
    m = dp_ways - 1 + ways - 1
    return remote_call(
        functools.partial(leave_kernel, ways, dp_ways),
        (jax.ShapeDtypeStruct((rows, width), F32), jax.ShapeDtypeStruct((8, 128), F32)),
        [ANY, VM, VM, VM],
        (VM, VM),
        [pltpu.VMEM((rows, width), F32)]
        + Scatter.buffers(ways, rows, width)
        + sems(n)
        + [
            pltpu.VMEM((dp_ways - 1, ways, 8, 128), F32),
            pltpu.VMEM((ways, 8, 128), F32),
            pltpu.VMEM((ways - 1, 8, 128), F32),
        ]
        + sems(m)
        + Rows.scratch(1, rows, depth),
        6,
        2 * count * width * depth,
        1_000_000,
    )(d_qkv, w_qkv, grad_hidden, tiles)


def drain_stage(stage, slot, targets, done):
    for k, target in enumerate(targets):
        pltpu.make_async_copy(stage.at[slot, k], target, done.at[slot, k]).wait()


def expand_kernel(
    ways, src_ref, wg_hbm, wu_hbm, all_ref, gate_ref, up_ref, act_ref,
    full_ref, wg_ref, wu_ref, loaded, out_sem, stage, done, send, recv, own_sem,
):
    g = Square(ways)
    loads = [pltpu.make_async_copy(a, b, loaded.at[j]) for j, (a, b) in enumerate(((wg_hbm, wg_ref), (wu_hbm, wu_ref)))]
    greet([{"seq": q} for q in g.near()])
    ag = Gather(g, src_ref, full_ref, send, recv, own_sem.at[0])
    ag.start()
    for c in loads:
        c.start()
    for c in loads:
        c.wait()
    count = src_ref.shape[0]
    outgoing = []
    tile = stage.shape[3]
    tiles = wg_ref.shape[1] // tile
    results = (gate_ref, up_ref, act_ref)

    def targets(rows, t):
        at = pl.ds(pl.multiple_of(t * tile, tile), tile)
        return [ref.at[rows, at] for ref in results]

    for k in range(ways):
        index = ag.arrive(k)
        rows = pl.ds(pl.multiple_of(index * count, count), count)
        outgoing.append(pltpu.make_async_copy(full_ref.at[rows], all_ref.at[rows], out_sem.at[k]))
        outgoing[-1].start()

        def body(t, carry):
            slot = lax.rem(k * tiles + t, 2)
            at = pl.ds(pl.multiple_of(t * tile, tile), tile)
            value = full_ref[rows, :]
            gate = dot_nn(value, wg_ref[:, at])
            up = dot_nn(value, wu_ref[:, at])

            @pl.when(k * tiles + t >= 2)
            def _():
                drain_stage(stage, slot, targets(rows, t), done)

            stage[slot, 0] = gate.astype(BF16)
            stage[slot, 1] = up.astype(BF16)
            stage[slot, 2] = (gate * (1.0 / (1.0 + jnp.exp(-gate))) * up).astype(BF16)
            for j, target in enumerate(targets(rows, t)):
                pltpu.make_async_copy(stage.at[slot, j], target, done.at[slot, j]).start()
            return carry

        lax.fori_loop(0, tiles, body, 0)
        if k == 0:
            ag.relay()
    last = ways * tiles
    for u in range(max(0, last - 2), last):
        drain_stage(stage, u % 2, targets(pl.ds(0, count), 0), done)
    for c in outgoing:
        c.wait()
    ag.drain()


def expand(ways, hidden, w_gate, w_up):
    rows, width = hidden.shape
    units = w_gate.shape[1]
    count = ways * rows
    low = jax.ShapeDtypeStruct((count, units), BF16)
    tile = tile_of(units, 512)
    return remote_call(
        functools.partial(expand_kernel, ways),
        (jax.ShapeDtypeStruct((count, width), BF16), low, low, low),
        [VM, ANY, ANY],
        (ANY,) * 4,
        [
            pltpu.VMEM((count, width), BF16),
            pltpu.VMEM((width, units), BF16),
            pltpu.VMEM((width, units), BF16),
            pltpu.SemaphoreType.DMA((2,)),
            pltpu.SemaphoreType.DMA((ways,)),
            pltpu.VMEM((2, 3, rows, tile), BF16),
            pltpu.SemaphoreType.DMA((2, 3)),
        ]
        + sems(Gather.sems(ways))
        + [pltpu.SemaphoreType.DMA((1,))],
        7,
        4 * count * width * units,
        1_000_000,
    )(hidden, w_gate, w_up)


def expand_back_kernel(
    ways, src_ref, w_hbm, act_hbm, gate_ref, up_ref, dgate_ref, dup_ref, down_ref,
    full, acc, w_ref, act_ref, loaded, inputs, stage, ready, done, send, recv, own_sem,
):
    g = Square(ways)
    loads = [pltpu.make_async_copy(a, b, loaded.at[j]) for j, (a, b) in enumerate(((w_hbm, w_ref), (act_hbm, act_ref)))]
    greet([{"seq": q} for q in g.near()])
    ag = Gather(g, src_ref, full, send, recv, own_sem.at[0])
    ag.start()
    for c in loads:
        c.start()
    for c in loads:
        c.wait()
    count, width = src_ref.shape
    tile = stage.shape[3]
    units = w_ref.shape[0]
    tiles = units // tile
    wide = tile_of(width, 1024)

    def views(refs, rows, t):
        at = pl.ds(pl.multiple_of(t * tile, tile), tile)
        return [ref.at[rows, at] for ref in refs]

    for k in range(ways):
        index = ag.arrive(k)
        rows = pl.ds(pl.multiple_of(index * count, count), count)

        def load(slot, t):
            return [
                pltpu.make_async_copy(ref, inputs.at[slot, j], ready.at[slot, j])
                for j, ref in enumerate(views((gate_ref, up_ref), rows, t))
            ]

        for c in load((k * tiles) % 2, 0):
            c.start()

        def body(t, carry):
            slot = lax.rem(k * tiles + t, 2)
            at = pl.ds(pl.multiple_of(t * tile, tile), tile)

            @pl.when(t + 1 < tiles)
            def _():
                for c in load(1 - slot, t + 1):
                    c.start()

            grad = dot_nt(full[rows, :], w_ref[at, :])
            for c in load(slot, t):
                c.wait()
            gate = inputs[slot, 0].astype(F32)
            up = inputs[slot, 1].astype(F32)
            s = 1.0 / (1.0 + jnp.exp(-gate))
            part = grad * s

            @pl.when(k * tiles + t >= 2)
            def _():
                drain_stage(stage, slot, views((dgate_ref, dup_ref), rows, t), done)

            stage[slot, 0] = (part * up * (1.0 + gate * (1.0 - s))).astype(BF16)
            stage[slot, 1] = (part * gate).astype(BF16)
            for j, target in enumerate(views((dgate_ref, dup_ref), rows, t)):
                pltpu.make_async_copy(stage.at[slot, j], target, done.at[slot, j]).start()
            return carry

        lax.fori_loop(0, tiles, body, 0)

        def down(u, carry):
            own = pl.ds(pl.multiple_of(lax.rem(u, tiles) * tile, tile), tile)
            at = pl.ds(pl.multiple_of(u // tiles * wide, wide), wide)
            term = dot_tn(act_ref[rows, own], full[rows, at])
            if k == 0:
                acc[own, at] = term
            elif k < ways - 1:
                acc[own, at] += term
            else:
                down_ref[own, at] = (acc[own, at] + term).astype(BF16)
            return carry

        lax.fori_loop(0, tiles * (width // wide), down, 0)
        if k == 0:
            ag.relay()
    last = ways * tiles
    for u in range(max(0, last - 2), last):
        drain_stage(stage, u % 2, views((dgate_ref, dup_ref), pl.ds(0, count), 0), done)
    ag.drain()


def expand_back(ways, grad, w_down, act, gate, up):
    rows, width = grad.shape
    count, units = act.shape
    low = jax.ShapeDtypeStruct((count, units), BF16)
    tile = tile_of(units, 512)
    return remote_call(
        functools.partial(expand_back_kernel, ways),
        (low, low, jax.ShapeDtypeStruct((units, width), BF16)),
        [VM, ANY, ANY, ANY, ANY],
        (ANY, ANY, VM),
        [
            pltpu.VMEM((count, width), BF16),
            pltpu.VMEM((units, width), F32),
            pltpu.VMEM((units, width), BF16),
            pltpu.VMEM((count, units), BF16),
            pltpu.SemaphoreType.DMA((2,)),
            pltpu.VMEM((2, 2, rows, tile), BF16),
            pltpu.VMEM((2, 2, rows, tile), BF16),
            pltpu.SemaphoreType.DMA((2, 2)),
            pltpu.SemaphoreType.DMA((2, 2)),
        ]
        + sems(Gather.sems(ways))
        + [pltpu.SemaphoreType.DMA((1,))],
        8,
        4 * count * width * units,
        1_000_000,
    )(grad, w_down, act, gate, up)


def out_back_kernel(ways, src_ref, w_ref, attn_ref, grad_ref, rows_ref, full, acc, send, recv, own_sem):
    g = Square(ways)
    greet([{"seq": q} for q in g.near()])
    ag = Gather(g, src_ref, full, send, recv, own_sem.at[0])
    ag.start()
    count, width = src_ref.shape
    wide = tile_of(width, 1024)
    for k in range(ways):
        index = ag.arrive(k)
        rows = pl.ds(pl.multiple_of(index * count, count), count)
        grad_ref[rows, :] = dot_nt(full[rows, :], w_ref[...]).astype(BF16)

        def body(u, carry):
            at = pl.ds(pl.multiple_of(u * wide, wide), wide)
            term = dot_tn(attn_ref[rows, :], full[rows, at])
            if k == 0:
                acc[:, at] = term
            elif k < ways - 1:
                acc[:, at] += term
            else:
                rows_ref[:, at] = (acc[:, at] + term).astype(BF16)
            return carry

        lax.fori_loop(0, width // wide, body, 0)
        if k == 0:
            ag.relay()
    ag.drain()


def out_back(ways, grad, w_rows, attn):
    rows, width = grad.shape
    count, cols = attn.shape
    return remote_call(
        functools.partial(out_back_kernel, ways),
        (jax.ShapeDtypeStruct((count, cols), BF16), jax.ShapeDtypeStruct((cols, width), BF16)),
        [VM] * 3,
        (VM, VM),
        [pltpu.VMEM((count, width), BF16), pltpu.VMEM((cols, width), F32)]
        + sems(Gather.sems(ways))
        + [pltpu.SemaphoreType.DMA((1,))],
        9,
        4 * count * width * cols,
        1_000_000,
    )(grad, w_rows, attn)


def scatter_dp(terms, axis):
    return lax.psum_scatter(terms.astype(BF16), "dp", scatter_dimension=axis, tiled=True).astype(F32)


def gather_dp(weights, axis):
    return lax.all_gather(weights, "dp", axis=axis, tiled=True)


def local(
    layer_in, cotangent, lengths, w_query, w_key, w_value, w_out, w_gate, w_up, w_down,
    gain_query, gain_key, gain_attn, gain_ffn,
):
    rows, width = layer_in.shape
    ways, dp_ways = lax.axis_size("seq"), lax.axis_size("dp")
    count = rows * ways
    head_width = width // HEADS
    cols = width // ways
    part = gain_query.shape[0]
    lens = lengths[0]
    seq_me = lax.axis_index("seq")

    w_qkv = gather_dp(jnp.concatenate([w_query, w_key, w_value], axis=1), 0)
    all_gate, all_up, all_down = gather_dp(w_gate, 1), gather_dp(w_up, 1), gather_dp(w_down, 0)

    four = jnp.stack([gain_query, gain_key, gain_attn, gain_ffn]).astype(F32)
    x_full, gain_tiles, cosine, sine = enter(
        ways, dp_ways, lens, layer_in, jnp.pad(four, ((0, 4), (0, 128 - part)))
    )
    gains = gain_tiles[:, :, :4, :part].transpose(2, 1, 0, 3).reshape(4, width)

    q_low, k_low, v_low, qn, kn, stats, w_rows = project(ways, dp_ways, x_full, w_qkv, w_out, gains, cosine, sine)
    attn, lse = attend(lens, q_low, k_low, v_low, head_width)

    whole = jax.ShapeDtypeStruct((rows, width), F32)
    half = jax.ShapeDtypeStruct((rows, width), BF16)
    eight = jax.ShapeDtypeStruct((8, width), F32)
    hidden, unit_a, inv_a, hidden_low = meet(
        ways, [(attn, w_rows)], False, after_attention, (layer_in, gains),
        (whole, half, jax.ShapeDtypeStruct((rows, 128), F32), half), 3,
    )
    hidden_full, gate, up, act = expand(ways, hidden_low, all_gate, all_up)
    layer_out, sums_f, grad_m = meet(
        ways, [(act, all_down)], False, after_ffn, (hidden, cotangent, gains), (half, eight, half), 4
    )
    d_gate, d_up, grad_down = expand_back(ways, grad_m, all_down, act, gate, up)
    out_down = scatter_dp(grad_down, 0)
    grad_gate = dot_tn(hidden_full, d_gate).astype(BF16)
    d_gate, grad_gate = lax.optimization_barrier((d_gate, grad_gate))
    out_gate = scatter_dp(grad_gate, 1)
    grad_up = dot_tn(hidden_full, d_up).astype(BF16)
    d_gate, d_up, grad_up = lax.optimization_barrier((d_gate, d_up, grad_up))
    out_up = scatter_dp(grad_up, 1)
    grad_hidden, sums_a, grad_a = meet(
        ways, [(d_gate, all_gate), (d_up, all_up)], True, before_ffn, (cotangent, unit_a, inv_a, gains),
        (whole, eight, half), 5,
    )
    grad_a, out_down = lax.optimization_barrier((grad_a, out_down))
    grad_attn, grad_rows = out_back(ways, grad_a, w_rows, attn)
    grad_attn, out_gate = lax.optimization_barrier((grad_attn, out_gate))
    out_out = scatter_dp(grad_rows, 1)
    grads = attend_back(lens, q_low, grad_attn, attn, lse, k_low, v_low, head_width)
    d_qkv, sums_qk = unproject(ways, grads, q_low, k_low, qn, kn, stats, gains, cosine, sine)
    d_qkv, out_up = lax.optimization_barrier((d_qkv, out_up))
    grad_qkv = dot_tn(x_full, d_qkv).astype(BF16)
    d_qkv, grad_qkv = lax.optimization_barrier((d_qkv, grad_qkv))
    out_qkv = scatter_dp(grad_qkv, 0)

    own = lax.dynamic_update_slice(jnp.zeros((2, width), F32), sums_qk[:2], (0, seq_me * cols))
    norms = jnp.stack([jnp.sum(sums_a, axis=0), jnp.sum(sums_f, axis=0)])
    tiles = jnp.concatenate([own, norms]).reshape(4, dp_ways, ways, part).transpose(1, 2, 0, 3)
    tiles = jnp.pad(tiles, ((0, 0), (0, 0), (0, 4), (0, 128 - part)))
    grad_in, gain_sums = leave(ways, dp_ways, d_qkv, w_qkv, grad_hidden, tiles)
    return (
        layer_out,
        grad_in,
        out_qkv[:, :cols],
        out_qkv[:, cols : 2 * cols],
        out_qkv[:, 2 * cols :],
        out_out,
        out_gate,
        out_up,
        out_down,
        gain_sums[0, :part],
        gain_sums[1, :part],
        gain_sums[2, :part],
        gain_sums[3, :part],
    )


def solution(mesh):
    both = P(("dp", "seq"))
    rows = P(("dp", "seq"), None)
    columns = P(None, ("dp", "seq"))
    square = P("dp", "seq")
    in_specs = (
        rows, rows, P("dp", None), square, square, square, P("seq", "dp"), columns, columns, rows, both, both, both, both,
    )
    out_specs = (
        rows, rows, square, square, square, P("seq", "dp"), columns, columns, rows, both, both, both, both,
    )
    return jax.shard_map(local, mesh=mesh, in_specs=in_specs, out_specs=out_specs, check_vma=False)
```

```python
import functools
import math

import jax
import jax.numpy as jnp
from jax import lax
from jax.experimental import pallas as pl
from jax.experimental.pallas import tpu as pltpu
from jax.sharding import PartitionSpec as P

HEADS = 16
NORM_EPS = 1e-06
ROPE_BASE = 500000.0
MASKED = -1e30
LONGEST = 1024
LOG2E = 1.4426950408889634

F32 = jnp.float32
BF16 = jnp.bfloat16
MESH = pl.DeviceIdType.MESH
VMEM_BYTES = 60 * 1024 * 1024
ANY = pl.BlockSpec(memory_space=pl.ANY)
VM = pl.BlockSpec(memory_space=pltpu.VMEM)


def dot_nn(a, b):
    return lax.dot_general(a, b, (((1,), (0,)), ((), ())), preferred_element_type=F32)


def dot_nt(a, b):
    return lax.dot_general(a, b, (((1,), (1,)), ((), ())), preferred_element_type=F32)


def dot_tn(a, b):
    return lax.dot_general(a, b, (((0,), (0,)), ((), ())), preferred_element_type=F32)


def row_sums(values):
    folded = values[:, 0:128]
    for k in range(1, values.shape[1] // 128):
        folded = folded + values[:, k * 128 : (k + 1) * 128]
    return jnp.sum(jnp.transpose(folded), axis=0, keepdims=True)


def as_columns(rows8):
    return jnp.transpose(jnp.concatenate([rows8] * 16, axis=0))


def tile_of(extent, most):
    return most if extent % most == 0 else extent


def bounds_of(lens_ref):
    first = lens_ref[0]
    second = first + lens_ref[1]
    return first, second, second + lens_ref[2]


def first_key(slot, bounds):
    a, b, c = bounds
    return jnp.where(slot < a, 0, jnp.where(slot < b, a, jnp.where(slot < c, b, slot)))


class Square:
    def __init__(self, ways):
        self.ways = ways
        self.me = lax.axis_index("seq")
        self.square = ways == 4
        if self.square:
            self.x = self.me + 1 - 2 * lax.rem(self.me, 2)
            self.y = lax.rem(self.me + 2, 4)
            self.d = 3 - self.me

    def peer(self, p):
        return lax.rem(self.me + p, self.ways)

    def near(self):
        if self.square:
            return [self.x, self.y]
        return [self.peer(p) for p in range(1, self.ways)]

    def everyone(self):
        return [self.peer(p) for p in range(1, self.ways)]

    def order(self):
        if self.square:
            return [self.d, self.x, self.y, self.me]
        return self.everyone() + [self.me]


def greet(devices):
    barrier = pltpu.get_barrier_semaphore()
    for device in devices:
        pl.semaphore_signal(barrier, inc=1, device_id=device, device_id_type=MESH)
    pl.semaphore_wait(barrier, len(devices))


def to_seq(src, dst, send, recv, peer):
    return pltpu.make_async_remote_copy(
        src_ref=src, dst_ref=dst, send_sem=send, recv_sem=recv, device_id={"seq": peer}, device_id_type=MESH
    )


def to_dp(src, dst, send, recv, peer):
    return pltpu.make_async_remote_copy(
        src_ref=src, dst_ref=dst, send_sem=send, recv_sem=recv, device_id={"dp": peer}, device_id_type=MESH
    )


class Gather:
    def __init__(self, group, src, full, send, recv, own_sem):
        self.g, self.src, self.full, self.send, self.recv = group, src, full, send, recv
        self.rows = src.shape[0]
        self.own = pltpu.make_async_copy(src, self.chunk(group.me), own_sem)

    @staticmethod
    def sems(ways):
        return 6 if ways == 4 else ways - 1

    def chunk(self, index):
        return self.full.at[pl.ds(index * self.rows, self.rows)]

    def half(self, index, which):
        h = self.rows // 2
        return self.full.at[pl.ds(index * self.rows + which * h, h)]

    def cp(self, k, src, dst, peer):
        return to_seq(src, dst, self.send.at[k], self.recv.at[k], peer)

    def start(self):
        g, h = self.g, self.rows // 2
        if g.square:
            top, low = self.src.at[pl.ds(0, h)], self.src.at[pl.ds(h, h)]
            self.first = [
                self.cp(0, top, self.half(g.me, 0), g.x),
                self.cp(1, low, self.half(g.me, 1), g.y),
                self.cp(2, low, self.half(g.me, 1), g.x),
                self.cp(3, top, self.half(g.me, 0), g.y),
            ]
        else:
            self.first = [self.cp(p - 1, self.src, self.chunk(g.me), g.peer(p)) for p in range(1, g.ways)]
        for c in self.first:
            c.start()
        self.own.start()

    def relay(self):
        g = self.g
        if g.square:
            self.first[0].wait_recv()
            a = self.cp(4, self.half(g.x, 0), self.half(g.x, 0), g.y)
            a.start()
            self.first[1].wait_recv()
            b = self.cp(5, self.half(g.y, 1), self.half(g.y, 1), g.x)
            b.start()
            self.second = [a, b]
        else:
            self.second = []

    def arrive(self, k):
        g = self.g
        if k == 0:
            self.own.wait()
            return g.me
        if not g.square:
            self.first[k - 1].wait_recv()
            return lax.rem(g.me + g.ways - k, g.ways)
        if k < 3:
            self.first[k + 1].wait_recv()
            return (g.x, g.y)[k - 1]
        for c in self.second:
            c.wait_recv()
        return g.d

    def drain(self):
        for c in self.first + self.second:
            c.wait_send()


class Scatter:
    @staticmethod
    def buffers(ways, rows, width):
        if ways == 4:
            return [
                pltpu.VMEM((3, rows, width), BF16),
                pltpu.VMEM((2, rows, width), BF16),
                pltpu.VMEM((2, rows // 2, width), BF16),
            ]
        return [
            pltpu.VMEM((ways - 1, rows, width), BF16),
            pltpu.VMEM((ways - 1, rows, width), BF16),
            pltpu.VMEM((2, 16, width), BF16),
        ]

    def __init__(self, group, out, arrived, relayed, send, recv):
        self.g, self.out, self.arrived, self.relayed, self.send, self.recv = group, out, arrived, relayed, send, recv
        self.rows = out.shape[1]

    def cp(self, k, src, dst, peer):
        return to_seq(src, dst, self.send.at[k], self.recv.at[k], peer)

    def run(self, left, right, own):
        g, h = self.g, self.rows // 2
        out, arrived, relayed = self.out, self.arrived, self.relayed
        left.copy(1).start()
        if not g.square:
            self.sent = []
            for p in range(1, g.ways):
                right.product(left.get(p - 1), out.at[p - 1], BF16)
                if p + 1 < g.ways:
                    left.copy(p + 1).start()
                c = self.cp(p - 1, out.at[p - 1], arrived.at[p - 1], g.peer(p))
                c.start()
                self.sent.append(c)
            right.product(left.get(g.ways - 1), own, F32)
            return
        top, low = pl.ds(0, h), pl.ds(h, h)
        right.product(left.get(0, top), out.at[2, top], BF16)
        c0 = self.cp(0, out.at[2, top], relayed.at[0], g.x)
        c0.start()
        right.product(left.get(0, low), out.at[2, low], BF16)
        c1 = self.cp(1, out.at[2, low], relayed.at[1], g.y)
        c1.start()
        left.copy(2).start()
        right.product(left.get(1, top), out.at[0, top], BF16)
        c2 = self.cp(2, out.at[0, top], arrived.at[0, top], g.x)
        c2.start()
        right.product(left.get(2, low), out.at[1, low], BF16)
        c3 = self.cp(3, out.at[1, low], arrived.at[1, low], g.y)
        c3.start()
        right.product(left.get(1, low), out.at[0, low], BF16)
        left.copy(3).start()
        right.product(left.get(2, top), out.at[1, top], BF16)
        self.sent = [c0, c1, c2, c3]
        self.relay()
        right.product(left.get(3), own, F32)

    def relay(self):
        g, h = self.g, self.rows // 2
        out, arrived, relayed = self.out, self.arrived, self.relayed
        top, low = pl.ds(0, h), pl.ds(h, h)
        c0, c1, c2, c3 = self.sent
        step = tile_of(h, 64)

        def add(slot, base, which):
            def body(t, carry):
                rows = pl.ds(base + t * step, step)
                have = out[slot, rows, :].astype(F32)
                out[slot, rows, :] = (have + relayed[which, pl.ds(t * step, step), :].astype(F32)).astype(BF16)
                return carry

            lax.fori_loop(0, h // step, body, 0)

        c1.wait_recv()
        add(0, h, 1)
        c4 = self.cp(4, out.at[0, low], arrived.at[0, low], g.x)
        c4.start()
        c0.wait_recv()
        add(1, 0, 0)
        c5 = self.cp(5, out.at[1, top], arrived.at[1, top], g.y)
        c5.start()
        self.sent += [c4, c5]

    def finish(self):
        for c in self.sent[2:] if self.g.square else self.sent:
            c.wait_recv()

    def drain(self):
        for c in self.sent:
            c.wait_send()

    def total(self, own, rows):
        value = own[rows, :]
        for k in range(self.arrived.shape[0]):
            value = value + self.arrived[k, rows, :].astype(F32)
        return value


def remote_call(kernel, outs, in_specs, out_specs, scratch, collective_id, flops, nbytes):
    return pl.pallas_call(
        kernel,
        out_shape=outs,
        in_specs=in_specs,
        out_specs=out_specs,
        scratch_shapes=scratch,
        compiler_params=pltpu.CompilerParams(
            collective_id=collective_id, has_side_effects=True, vmem_limit_bytes=VMEM_BYTES
        ),
        cost_estimate=pl.CostEstimate(flops=0, bytes_accessed=nbytes, transcendentals=0),
    )


def sems(n):
    return [pltpu.SemaphoreType.DMA((n,)), pltpu.SemaphoreType.DMA((n,))]


def write_tables(lens_ref, cos_ref, sin_ref):
    count, head_width = cos_ref.shape
    half = head_width // 2
    step = tile_of(count, 256)
    bounds = bounds_of(lens_ref)
    lane = lax.broadcasted_iota(jnp.int32, (1, head_width), 1)
    folded = jnp.where(lane < half, lane, lane - half).astype(F32)
    frequency = jnp.exp(folded * (-2.0 / head_width * math.log(ROPE_BASE)))
    sign = jnp.where(lane < half, -1.0, 1.0)

    def body(t, carry):
        rows = pl.ds(pl.multiple_of(t * step, step), step)
        slots = t * step + lax.broadcasted_iota(jnp.int32, (step, head_width), 0)
        a, b, c = bounds
        begin = jnp.where(slots < a, 0, jnp.where(slots < b, a, jnp.where(slots < c, b, c)))
        angles = (slots - begin).astype(F32) * frequency
        cos_ref[rows, :] = jnp.cos(angles)
        sin_ref[rows, :] = jnp.sin(angles) * sign
        return carry

    lax.fori_loop(0, count // step, body, 0)


def enter_kernel(
    ways, dp_ways, lens_ref, x_ref, gain_ref, full_ref, gains_ref, cos_ref, sin_ref,
    send, recv, own_sem, gsend, grecv,
):
    g = Square(ways)
    dp_me = lax.axis_index("dp")
    dp_peers = [lax.rem(dp_me + p, dp_ways) for p in range(1, dp_ways)]
    greet([{"seq": q} for q in g.everyone()] + [{"dp": p} for p in dp_peers])
    ag = Gather(g, x_ref, full_ref, send, recv, own_sem.at[0])
    ag.start()

    gains_ref[g.me, dp_me] = gain_ref[...]
    first = [
        to_dp(gain_ref, gains_ref.at[g.me, dp_me], gsend.at[k], grecv.at[k], p) for k, p in enumerate(dp_peers)
    ]
    for c in first:
        c.start()
    write_tables(lens_ref, cos_ref, sin_ref)
    for c in first:
        c.wait_recv()
    base = dp_ways - 1
    second = [
        to_seq(gains_ref.at[g.me], gains_ref.at[g.me], gsend.at[base + k], grecv.at[base + k], q)
        for k, q in enumerate(g.everyone())
    ]
    for c in second:
        c.start()
    ag.relay()
    for c in second:
        c.wait_recv()
    for c in first + second:
        c.wait_send()
    for k in range(ways):
        ag.arrive(k)
    ag.drain()


def enter(ways, dp_ways, lens, x, gains):
    rows, width = x.shape
    count, head_width = ways * rows, width // HEADS
    table = jax.ShapeDtypeStruct((count, head_width), F32)
    return remote_call(
        functools.partial(enter_kernel, ways, dp_ways),
        (
            jax.ShapeDtypeStruct((count, width), BF16),
            jax.ShapeDtypeStruct((ways, dp_ways, 8, 128), F32),
            table,
            table,
        ),
        [pl.BlockSpec(memory_space=pltpu.SMEM), ANY, VM],
        (ANY, VM, VM, VM),
        sems(Gather.sems(ways))
        + [pltpu.SemaphoreType.DMA((1,))]
        + sems(dp_ways - 1 + ways - 1),
        0,
        0,
        1_000_000,
    )(lens, x, gains)


def exchange_rows(g, mine, arrived, send, recv):
    copies = [
        to_seq(mine, arrived.at[k], send.at[k], recv.at[k], q) for k, q in enumerate(g.everyone())
    ]
    for c in copies:
        c.start()
    for c in copies:
        c.wait_recv()
    total = mine[...]
    for k in range(g.ways - 1):
        total = total + arrived[k]
    for c in copies:
        c.wait_send()
    return total


def project_kernel(
    ways, x_ref, w_ref, gain_ref, cos_ref, sin_ref, q_ref, k_ref, v_ref, qn_ref, kn_ref, stat_ref,
    qf, kf, mine, arrived, send, recv, buffer, ready,
):
    g = Square(ways)
    count, width = x_ref.shape
    cols = q_ref.shape[1]
    step = buffer.shape[1]
    steps = count // step

    def fetch(i, slot):
        rows = pl.ds(pl.multiple_of(i * step, step), step)
        return pltpu.make_async_copy(x_ref.at[rows], buffer.at[slot], ready.at[slot])

    fetch(0, 0).start()
    greet([{"seq": q} for q in g.everyone()])
    mine[...] = jnp.zeros_like(mine)

    def project(i, carry):
        slot = lax.rem(i, 2)

        @pl.when(i + 1 < steps)
        def _():
            fetch(i + 1, 1 - slot).start()

        fetch(i, slot).wait()
        rows = pl.ds(pl.multiple_of(i * step, step), step)
        xs = buffer[slot]
        for part, ref in ((0, qf), (1, kf)):
            value = dot_nn(xs, w_ref[:, part * cols : (part + 1) * cols])
            ref[rows, :] = value
            mine[part : part + 1, rows] = row_sums(value * value)
        v_ref[rows, :] = dot_nn(xs, w_ref[:, 2 * cols : 3 * cols]).astype(BF16)
        return carry

    lax.fori_loop(0, steps, project, 0)
    stat_ref[...] = exchange_rows(g, mine, arrived, send, recv)
    small = tile_of(count, 256)

    def finish(i, carry):
        rows = pl.ds(pl.multiple_of(i * small, small), small)
        inverse = lax.rsqrt(as_columns(stat_ref[:, rows]) * (1.0 / width) + NORM_EPS)
        cosine, sine = cos_ref[rows, :], sin_ref[rows, :]
        for part, src, normed, out in ((0, qf, qn_ref, q_ref), (1, kf, kn_ref, k_ref)):
            scale = inverse[:, part : part + 1]
            for h in range(cols // 128):
                at = slice(h * 128, (h + 1) * 128)
                unit = src[rows, at] * scale
                normed[rows, at] = unit.astype(BF16)
                start = pl.multiple_of(g.me * cols + h * 128, 128)
                value = unit * gain_ref[part : part + 1, pl.ds(start, 128)]
                out[rows, at] = (value * cosine + pltpu.roll(value, 64, 1) * sine).astype(BF16)
        return carry

    lax.fori_loop(0, count // small, finish, 0)


def project(ways, x_full, w_all, gains, cosine, sine):
    count, width = x_full.shape
    cols = w_all.shape[1] // 4
    step = tile_of(count, 512)
    low = jax.ShapeDtypeStruct((count, cols), BF16)
    return remote_call(
        functools.partial(project_kernel, ways),
        (low, low, low, low, low, jax.ShapeDtypeStruct((8, count), F32)),
        [ANY, VM, VM, VM, VM],
        (VM,) * 6,
        [
            pltpu.VMEM((count, cols), F32),
            pltpu.VMEM((count, cols), F32),
            pltpu.VMEM((8, count), F32),
            pltpu.VMEM((ways - 1, 8, count), F32),
        ]
        + sems(ways - 1)
        + [pltpu.VMEM((2, step, width), BF16), pltpu.SemaphoreType.DMA((2,))],
        1,
        2 * count * width * 3 * cols,
        1_000_000,
    )(x_full, w_all, gains, cosine, sine)


def attend_kernel(head_width, lens_ref, q_ref, k_ref, v_ref, o_ref, lse_ref, acc, top, tot):
    block, cols = q_ref.shape
    heads = cols // head_width
    i = pl.program_id(0)
    bounds = bounds_of(lens_ref)
    slots = i * block + lax.broadcasted_iota(jnp.int32, (1, block), 1)
    begins = first_key(slots, bounds)
    factor = head_width ** (-0.5) * LOG2E

    def scores_of(kb, h):
        at = slice(h * head_width, (h + 1) * head_width)
        rows = pl.ds(pl.multiple_of(kb * block, block), block)
        keys = kb * block + lax.broadcasted_iota(jnp.int32, (block, block), 0)
        visible = (keys <= slots) & (keys >= begins)
        scores = dot_nt(k_ref[rows, at], q_ref[:, at]) * factor
        return jnp.where(visible, scores, MASKED), v_ref[rows, at], at

    for h in range(heads):
        scores, values, at = scores_of(i, h)
        largest = jnp.max(scores, axis=0, keepdims=True)
        weights = jnp.exp2(scores - largest)
        top[h : h + 1, :] = largest
        tot[h : h + 1, :] = jnp.sum(weights, axis=0, keepdims=True)
        acc[at, :] = dot_tn(values, weights.astype(BF16))

    def earlier(t, carry):
        kb = i - 1 - t
        for h in range(heads):
            scores, values, at = scores_of(kb, h)
            before = top[h : h + 1, :]
            largest = jnp.maximum(before, jnp.max(scores, axis=0, keepdims=True))
            weights = jnp.exp2(scores - largest)
            shrink = jnp.exp2(before - largest)
            top[h : h + 1, :] = largest
            tot[h : h + 1, :] = tot[h : h + 1, :] * shrink + jnp.sum(weights, axis=0, keepdims=True)
            acc[at, :] = acc[at, :] * shrink + dot_tn(values, weights.astype(BF16))
        return carry

    lowest = first_key(i * block, bounds) // block
    lax.fori_loop(0, i - lowest, earlier, 0)
    lse_ref[...] = jnp.zeros_like(lse_ref)
    for h in range(heads):
        at = slice(h * head_width, (h + 1) * head_width)
        total = tot[h : h + 1, :]
        o_ref[:, at] = jnp.transpose(acc[at, :] * (1.0 / total)).astype(BF16)
        lse_ref[h : h + 1, :] = top[h : h + 1, :] + jnp.log2(total)


def attend(lens, q_low, k_low, v_low, head_width):
    count, cols = q_low.shape
    block = tile_of(count, 512)
    tile = pl.BlockSpec((block, cols), lambda i, lens: (i, 0))
    whole = pl.BlockSpec((count, cols), lambda i, lens: (0, 0))
    line = pl.BlockSpec((8, block), lambda i, lens: (0, i))
    return pl.pallas_call(
        functools.partial(attend_kernel, head_width),
        out_shape=(jax.ShapeDtypeStruct((count, cols), BF16), jax.ShapeDtypeStruct((8, count), F32)),
        grid_spec=pltpu.PrefetchScalarGridSpec(
            num_scalar_prefetch=1,
            grid=(count // block,),
            in_specs=[tile, whole, whole],
            out_specs=(tile, line),
            scratch_shapes=[pltpu.VMEM((cols, block), F32), pltpu.VMEM((8, block), F32), pltpu.VMEM((8, block), F32)],
        ),
        compiler_params=pltpu.CompilerParams(dimension_semantics=("arbitrary",), vmem_limit_bytes=VMEM_BYTES),
        cost_estimate=pl.CostEstimate(flops=0, bytes_accessed=1_000_000, transcendentals=0),
    )(lens, q_low, k_low, v_low)


class Right:
    def __init__(self, src, ref, loaded, transposed, first_column):
        self.ref, self.transposed, self.loaded = ref, transposed, loaded
        self.width = ref.shape[0] if transposed else ref.shape[1]
        self.tile = self.width // self.tiles(self.width)
        self.src = src.at[:, pl.ds(first_column, ref.shape[1])] if transposed else src
        self.fresh = True

    @staticmethod
    def tiles(width):
        return width // tile_of(width, 512)

    @staticmethod
    def scratch(shape, transposed):
        width = shape[0] if transposed else shape[1]
        return [pltpu.VMEM(shape, BF16), pltpu.SemaphoreType.DMA((Right.tiles(width),))]

    def copy(self, t):
        at = pl.ds(pl.multiple_of(t * self.tile, self.tile), self.tile)
        if self.transposed:
            return pltpu.make_async_copy(self.src.at[at], self.ref.at[at], self.loaded.at[t])
        return pltpu.make_async_copy(self.src.at[:, at], self.ref.at[:, at], self.loaded.at[t])

    def start(self):
        for t in range(self.width // self.tile):
            self.copy(t).start()

    def product(self, lhs, out, dtype):
        fresh, self.fresh = self.fresh, False

        def body(t, carry):
            at = pl.ds(pl.multiple_of(t * self.tile, self.tile), self.tile)
            if fresh:
                self.copy(t).wait()
            value = dot_nt(lhs[...], self.ref[at, :]) if self.transposed else dot_nn(lhs[...], self.ref[:, at])
            out[:, at] = value.astype(dtype)
            return carry

        lax.fori_loop(0, self.width // self.tile, body, 0)


class Rows:
    def __init__(self, order, ref, buffer, ready):
        self.order, self.ref, self.buffer, self.ready = order, ref, buffer, ready
        self.waited = set()

    @staticmethod
    def scratch(rows, depth):
        return [pltpu.VMEM((2, rows, depth), BF16), pltpu.SemaphoreType.DMA((2,))]

    def copy(self, turn):
        count = self.buffer.shape[1]
        rows = pl.ds(pl.multiple_of(self.order[turn] * count, count), count)
        return pltpu.make_async_copy(self.ref.at[rows], self.buffer.at[turn % 2], self.ready.at[turn % 2])

    def get(self, turn, part=None):
        if turn not in self.waited:
            self.copy(turn).wait()
            self.waited.add(turn)
        return self.buffer.at[turn % 2] if part is None else self.buffer.at[turn % 2, part]


def fold8(value):
    return jnp.sum(value.reshape(value.shape[0] // 8, 8, value.shape[1]), axis=0)


def meet_kernel(ways, transposed, first_column, epilogue, n_extra, n_out, own_is_out, lhs, rhs, *refs):
    sources, outs, scratch = refs[:n_extra], refs[n_extra : n_extra + n_out], refs[n_extra + n_out :]
    own = outs[0] if own_is_out else scratch[0]
    scratch = scratch if own_is_out else scratch[1:]
    out, arrived, relayed, send, recv, buffer, ready, w_ref, loaded, fetched = scratch[:10]
    extra = scratch[10:]
    g = Square(ways)
    left = Rows(g.order(), lhs, buffer, ready)
    right = Right(rhs, w_ref, loaded, transposed, first_column)
    left.copy(0).start()
    right.start()
    fetches = [pltpu.make_async_copy(a, b, fetched.at[j]) for j, (a, b) in enumerate(zip(sources, extra))]
    greet([{"seq": q} for q in g.near()])
    count = own.shape[0]
    rs = Scatter(g, out, arrived, relayed, send, recv)
    for c in fetches:
        c.start()
    rs.run(left, right, own)
    for c in fetches:
        c.wait()
    rs.finish()
    step = tile_of(count, 64)

    def body(t, carry):
        rows = pl.ds(pl.multiple_of(t * step, step), step)
        epilogue(rows, rs.total(own, rows), extra, outs, t)
        return carry

    lax.fori_loop(0, count // step, body, 0)
    rs.drain()


def meet(ways, lhs, rhs, transposed, epilogue, extra, outs, collective_id, first_column=0):
    count, depth = lhs.shape
    width = rhs.shape[0] if transposed else rhs.shape[1]
    rows = count // ways
    n = 6 if ways == 4 else ways - 1
    own_is_out = outs[0].dtype == F32
    scratch = [] if own_is_out else [pltpu.VMEM((rows, width), F32)]
    scratch += Scatter.buffers(ways, rows, width) + sems(n) + Rows.scratch(rows, depth)
    scratch += Right.scratch((width, depth) if transposed else (depth, width), transposed)
    scratch += [pltpu.SemaphoreType.DMA((len(extra),))] + [pltpu.VMEM(e.shape, e.dtype) for e in extra]
    return remote_call(
        functools.partial(meet_kernel, ways, transposed, first_column, epilogue, len(extra), len(outs), own_is_out),
        tuple(outs),
        [ANY] * (2 + len(extra)),
        (VM,) * len(outs),
        scratch,
        collective_id,
        2 * count * width * depth,
        1_000_000,
    )(lhs, rhs, *extra)


def after_attention(rows, branch, extra, outs, t):
    x_ref, gain_ref = extra
    hidden_ref, unit_ref, inv_ref, source = outs
    inverse = lax.rsqrt(jnp.mean(branch * branch, axis=1, keepdims=True) + NORM_EPS)
    unit = branch * inverse
    hidden = x_ref[rows, :].astype(F32) + unit * gain_ref[2:3, :]
    hidden_ref[rows, :] = hidden
    unit_ref[rows, :] = unit.astype(BF16)
    inv_ref[rows, :] = jnp.broadcast_to(inverse, (inverse.shape[0], 128))
    source[rows, :] = hidden.astype(BF16)


def after_ffn(rows, branch, extra, outs, t):
    hidden_ref, cot_ref, gain_ref = extra
    out_ref, sums_ref, source = outs
    gain = gain_ref[3:4, :]
    inverse = lax.rsqrt(jnp.mean(branch * branch, axis=1, keepdims=True) + NORM_EPS)
    unit = branch * inverse
    out_ref[rows, :] = (hidden_ref[rows, :] + unit * gain).astype(BF16)
    e = cot_ref[rows, :].astype(F32)
    term = fold8(e * unit)

    @pl.when(t == 0)
    def _():
        sums_ref[...] = term

    @pl.when(t > 0)
    def _():
        sums_ref[...] += term

    eg = e * gain
    mean = jnp.mean(eg * unit, axis=1, keepdims=True)
    source[rows, :] = (inverse * (eg - unit * mean)).astype(BF16)


def before_ffn(rows, terms, extra, outs, t):
    cot_ref, unit_ref, inv_ref, gain_ref = extra
    hidden_ref, sums_ref, source = outs
    e = cot_ref[rows, :].astype(F32) + terms
    hidden_ref[rows, :] = e
    unit = unit_ref[rows, :].astype(F32)
    term = fold8(e * unit)

    @pl.when(t == 0)
    def _():
        sums_ref[...] = term

    @pl.when(t > 0)
    def _():
        sums_ref[...] += term

    eg = e * gain_ref[2:3, :]
    mean = jnp.mean(eg * unit, axis=1, keepdims=True)
    source[rows, :] = (inv_ref[rows, 0:1] * (eg - unit * mean)).astype(BF16)


def leave_kernel(
    ways, dp_ways, d_ref, w_hbm, hidden_hbm, tiles_ref, grad_ref, gains_ref,
    hidden_ref, out, arrived, relayed, send, recv, from_dp, partial, from_seq, gsend, grecv, buffer, ready,
    w_ref, loaded, fetched,
):
    g = Square(ways)
    left = Rows(g.order(), d_ref, buffer, ready)
    right = Right(w_hbm, w_ref, loaded, True, 0)
    left.copy(0).start()
    right.start()
    fetch = pltpu.make_async_copy(hidden_hbm, hidden_ref, fetched.at[0])
    dp_me = lax.axis_index("dp")
    dp_peers = [lax.rem(dp_me + p, dp_ways) for p in range(1, dp_ways)]
    greet([{"seq": q} for q in g.everyone()] + [{"dp": p} for p in dp_peers])
    first = [
        to_dp(tiles_ref.at[p], from_dp.at[k], gsend.at[k], grecv.at[k], p) for k, p in enumerate(dp_peers)
    ]
    for c in first:
        c.start()
    fetch.start()
    count = grad_ref.shape[0]
    rs = Scatter(g, out, arrived, relayed, send, recv)
    rs.run(left, right, grad_ref)
    for c in first:
        c.wait_recv()
    value = tiles_ref[dp_me]
    for k in range(dp_ways - 1):
        value = value + from_dp[k]
    partial[...] = value
    base = dp_ways - 1
    second = [
        to_seq(partial.at[q], from_seq.at[k], gsend.at[base + k], grecv.at[base + k], q)
        for k, q in enumerate(g.everyone())
    ]
    for c in second:
        c.start()
    for c in second:
        c.wait_recv()
    value = partial[g.me]
    for k in range(ways - 1):
        value = value + from_seq[k]
    gains_ref[...] = value
    fetch.wait()
    rs.finish()
    step = tile_of(count, 64)

    def body(t, carry):
        rows = pl.ds(pl.multiple_of(t * step, step), step)
        grad_ref[rows, :] = hidden_ref[rows, :] + rs.total(grad_ref, rows)
        return carry

    lax.fori_loop(0, count // step, body, 0)
    for c in first + second:
        c.wait_send()
    rs.drain()


def leave(ways, dp_ways, d_qkv, w_all, grad_hidden, tiles):
    count, depth = d_qkv.shape
    rows, width = grad_hidden.shape
    n = 6 if ways == 4 else ways - 1
    m = dp_ways - 1 + ways - 1
    return remote_call(
        functools.partial(leave_kernel, ways, dp_ways),
        (jax.ShapeDtypeStruct((rows, width), F32), jax.ShapeDtypeStruct((8, 128), F32)),
        [ANY, ANY, ANY, VM],
        (VM, VM),
        [pltpu.VMEM((rows, width), F32)]
        + Scatter.buffers(ways, rows, width)
        + sems(n)
        + [
            pltpu.VMEM((dp_ways - 1, ways, 8, 128), F32),
            pltpu.VMEM((ways, 8, 128), F32),
            pltpu.VMEM((ways - 1, 8, 128), F32),
        ]
        + sems(m)
        + Rows.scratch(rows, depth)
        + Right.scratch((width, depth), True)
        + [pltpu.SemaphoreType.DMA((1,))],
        6,
        2 * count * width * depth,
        1_000_000,
    )(d_qkv, w_all, grad_hidden, tiles)


def halves(unit, blocks):
    return [
        (slice(2 * j * unit, (2 * j + 1) * unit), slice((2 * j + 1) * unit, (2 * j + 2) * unit)) for j in range(blocks)
    ]


def expand_kernel(
    ways, unit, blocks, src_ref, w_hbm, all_ref, both_ref, act_ref,
    full_ref, w_ref, loaded, out_sem, stage, act_stage, done, send, recv, own_sem,
):
    g = Square(ways)
    load = pltpu.make_async_copy(w_hbm, w_ref, loaded.at[0])
    greet([{"seq": q} for q in g.near()])
    ag = Gather(g, src_ref, full_ref, send, recv, own_sem.at[0])
    ag.start()
    load.start()
    load.wait()
    count = src_ref.shape[0]
    outgoing = []
    tile = unit * blocks
    tiles = w_ref.shape[1] // (2 * tile)

    def results(slot, rows, t):
        wide = pl.ds(pl.multiple_of(t * 2 * tile, 2 * tile), 2 * tile)
        at = pl.ds(pl.multiple_of(t * tile, tile), tile)
        return [
            pltpu.make_async_copy(stage.at[slot], both_ref.at[rows, wide], done.at[slot, 0]),
            pltpu.make_async_copy(act_stage.at[slot], act_ref.at[rows, at], done.at[slot, 1]),
        ]

    for k in range(ways):
        index = ag.arrive(k)
        rows = pl.ds(pl.multiple_of(index * count, count), count)
        outgoing.append(pltpu.make_async_copy(full_ref.at[rows], all_ref.at[rows], out_sem.at[k]))
        outgoing[-1].start()

        def body(t, carry):
            slot = lax.rem(k * tiles + t, 2)
            both = dot_nn(full_ref[rows, :], w_ref[:, pl.ds(pl.multiple_of(t * 2 * tile, 2 * tile), 2 * tile)])

            @pl.when(k * tiles + t >= 2)
            def _():
                for c in results(slot, rows, t):
                    c.wait()

            stage[slot] = both.astype(BF16)
            for j, (first, second) in enumerate(halves(unit, blocks)):
                gate, up = both[:, first], both[:, second]
                value = gate * (1.0 / (1.0 + jnp.exp(-gate))) * up
                act_stage[slot, :, j * unit : (j + 1) * unit] = value.astype(BF16)
            for c in results(slot, rows, t):
                c.start()
            return carry

        lax.fori_loop(0, tiles, body, 0)
        if k == 0:
            ag.relay()
    last = ways * tiles
    for u in range(max(0, last - 2), last):
        for c in results(u % 2, pl.ds(0, count), 0):
            c.wait()
    for c in outgoing:
        c.wait()
    ag.drain()


def blocks_of(units, unit):
    return 2 if (units // unit) % 2 == 0 else 1


def expand(ways, hidden, w_both, unit):
    rows, width = hidden.shape
    units = w_both.shape[1] // 2
    count = ways * rows
    blocks = blocks_of(units, unit)
    tile = unit * blocks
    return remote_call(
        functools.partial(expand_kernel, ways, unit, blocks),
        (
            jax.ShapeDtypeStruct((count, width), BF16),
            jax.ShapeDtypeStruct((count, 2 * units), BF16),
            jax.ShapeDtypeStruct((count, units), BF16),
        ),
        [VM, ANY],
        (ANY,) * 3,
        [
            pltpu.VMEM((count, width), BF16),
            pltpu.VMEM((width, 2 * units), BF16),
            pltpu.SemaphoreType.DMA((1,)),
            pltpu.SemaphoreType.DMA((ways,)),
            pltpu.VMEM((2, rows, 2 * tile), BF16),
            pltpu.VMEM((2, rows, tile), BF16),
            pltpu.SemaphoreType.DMA((2, 2)),
        ]
        + sems(Gather.sems(ways))
        + [pltpu.SemaphoreType.DMA((1,))],
        7,
        4 * count * width * units,
        1_000_000,
    )(hidden, w_both)


def expand_back_kernel(
    ways, unit, blocks, src_ref, w_hbm, act_hbm, both_ref, dboth_ref, down_ref,
    full, acc, w_ref, act_ref, loaded, inputs, stage, ready, done, send, recv, own_sem,
):
    g = Square(ways)
    loads = [pltpu.make_async_copy(a, b, loaded.at[j]) for j, (a, b) in enumerate(((w_hbm, w_ref), (act_hbm, act_ref)))]
    greet([{"seq": q} for q in g.near()])
    ag = Gather(g, src_ref, full, send, recv, own_sem.at[0])
    ag.start()
    for c in loads:
        c.start()
    for c in loads:
        c.wait()
    count, width = src_ref.shape
    tile = unit * blocks
    units = w_ref.shape[0]
    tiles = units // tile
    wide = tile_of(width, 1024)

    def view(ref, rows, t):
        return ref.at[rows, pl.ds(pl.multiple_of(t * 2 * tile, 2 * tile), 2 * tile)]

    for k in range(ways):
        index = ag.arrive(k)
        rows = pl.ds(pl.multiple_of(index * count, count), count)

        def load(slot, t):
            return pltpu.make_async_copy(view(both_ref, rows, t), inputs.at[slot], ready.at[slot])

        def result(slot, t):
            return pltpu.make_async_copy(stage.at[slot], view(dboth_ref, rows, t), done.at[slot])

        load((k * tiles) % 2, 0).start()

        def body(t, carry):
            slot = lax.rem(k * tiles + t, 2)
            at = pl.ds(pl.multiple_of(t * tile, tile), tile)

            @pl.when(t + 1 < tiles)
            def _():
                load(1 - slot, t + 1).start()

            grads = dot_nt(full[rows, :], w_ref[at, :])
            load(slot, t).wait()

            @pl.when(k * tiles + t >= 2)
            def _():
                result(slot, t).wait()

            for j, (first, second) in enumerate(halves(unit, blocks)):
                grad = grads[:, j * unit : (j + 1) * unit]
                gate = inputs[slot, :, first].astype(F32)
                up = inputs[slot, :, second].astype(F32)
                s = 1.0 / (1.0 + jnp.exp(-gate))
                part = grad * s
                stage[slot, :, first] = (part * up * (1.0 + gate * (1.0 - s))).astype(BF16)
                stage[slot, :, second] = (part * gate).astype(BF16)
            result(slot, t).start()
            return carry

        lax.fori_loop(0, tiles, body, 0)

        def down(u, carry):
            own = pl.ds(pl.multiple_of(lax.rem(u, tiles) * tile, tile), tile)
            at = pl.ds(pl.multiple_of(u // tiles * wide, wide), wide)
            term = dot_tn(act_ref[rows, own], full[rows, at])
            if k == 0:
                acc[own, at] = term
            elif k < ways - 1:
                acc[own, at] += term
            else:
                down_ref[own, at] = (acc[own, at] + term).astype(BF16)
            return carry

        lax.fori_loop(0, tiles * (width // wide), down, 0)
        if k == 0:
            ag.relay()
    last = ways * tiles
    for u in range(max(0, last - 2), last):
        pltpu.make_async_copy(stage.at[u % 2], view(dboth_ref, pl.ds(0, count), 0), done.at[u % 2]).wait()
    ag.drain()


def expand_back(ways, grad, w_down, act, both, unit):
    rows, width = grad.shape
    count, units = act.shape
    blocks = blocks_of(units, unit)
    tile = unit * blocks
    return remote_call(
        functools.partial(expand_back_kernel, ways, unit, blocks),
        (jax.ShapeDtypeStruct((count, 2 * units), BF16), jax.ShapeDtypeStruct((units, width), BF16)),
        [VM, ANY, ANY, ANY],
        (ANY, VM),
        [
            pltpu.VMEM((count, width), BF16),
            pltpu.VMEM((units, width), F32),
            pltpu.VMEM((units, width), BF16),
            pltpu.VMEM((count, units), BF16),
            pltpu.SemaphoreType.DMA((2,)),
            pltpu.VMEM((2, rows, 2 * tile), BF16),
            pltpu.VMEM((2, rows, 2 * tile), BF16),
            pltpu.SemaphoreType.DMA((2,)),
            pltpu.SemaphoreType.DMA((2,)),
        ]
        + sems(Gather.sems(ways))
        + [pltpu.SemaphoreType.DMA((1,))],
        8,
        4 * count * width * units,
        1_000_000,
    )(grad, w_down, act, both)


def attention_back_kernel(
    ways, head_width, lens_ref, src_ref, w_hbm, attn_ref, q_ref, k_ref, v_ref, qn_ref, kn_ref, lse_ref, stat_ref,
    gain_ref, cos_ref, sin_ref, out_ref, sums_ref, all_ref,
    full, acc, w_ref, out_t, loaded, grad, gq, qacc, kacc, vacc, centre, mine, arrived, total,
    send, recv, own_sem, xsend, xrecv,
):
    g = Square(ways)
    load = pltpu.make_async_copy(w_hbm.at[:, pl.ds(3 * attn_ref.shape[1], attn_ref.shape[1])], w_ref, loaded.at[0])
    load.start()
    greet([{"seq": q} for q in g.everyone()])
    ag = Gather(g, src_ref, full, send, recv, own_sem.at[0])
    ag.start()
    kacc[...] = jnp.zeros_like(kacc)
    vacc[...] = jnp.zeros_like(vacc)
    mine[...] = jnp.zeros_like(mine)
    count, width = src_ref.shape
    cols = attn_ref.shape[1]
    heads = cols // head_width
    wide = tile_of(width, 1024)
    bounds = bounds_of(lens_ref)
    root = head_width ** (-0.5)
    factor = root * LOG2E
    back = (LONGEST - 1 + count - 1) // count
    load.wait()
    for k in range(ways):
        index = ag.arrive(k)
        rows = pl.ds(pl.multiple_of(index * count, count), count)
        grad[...] = dot_nn(full[rows, :], w_ref[...]).astype(BF16)

        def body(u, carry):
            at = pl.ds(pl.multiple_of(u * wide, wide), wide)
            term = dot_tn(full[rows, at], attn_ref[rows, :])
            if k == 0:
                acc[at, :] = term
            elif k < ways - 1:
                acc[at, :] += term
            else:
                out_t[at, :] = (acc[at, :] + term).astype(BF16)
            return carry

        lax.fori_loop(0, width // wide, body, 0)
        slots = index * count + lax.broadcasted_iota(jnp.int32, (1, count), 1)
        begins = first_key(slots, bounds)
        for h in range(heads):
            at = slice(h * head_width, (h + 1) * head_width)
            centre[h : h + 1, :] = row_sums(grad[:, at].astype(F32) * attn_ref[rows, at].astype(F32))
        qacc[...] = jnp.zeros_like(qacc)

        def keys_block(t, carry):
            kb = index - t
            there = pl.ds(pl.multiple_of(kb * count, count), count)
            keys = kb * count + lax.broadcasted_iota(jnp.int32, (count, count), 0)
            visible = (keys <= slots) & (keys >= begins)
            for h in range(heads):
                at = slice(h * head_width, (h + 1) * head_width)
                keys_h, query, grad_h = k_ref[there, at], q_ref[rows, at], grad[:, at]
                scores = dot_nt(keys_h, query) * factor - lse_ref[h : h + 1, rows]
                weights = jnp.where(visible, jnp.exp2(scores), 0.0)
                grad_probs = dot_nt(v_ref[there, at], grad_h)
                grad_scores = (weights * (grad_probs - centre[h : h + 1, :])).astype(BF16)
                vacc[there, at] += dot_nn(weights.astype(BF16), grad_h)
                kacc[there, at] += dot_nn(grad_scores, query)
                qacc[:, at] += dot_tn(grad_scores, keys_h)
            return carry

        lax.fori_loop(0, jnp.minimum(index, back) + 1, keys_block, 0)
        gq[rows, :] = (qacc[...] * root).astype(BF16)
        mine[0:1, rows] = row_sums(gq[rows, :].astype(F32) * q_ref[rows, :].astype(F32))
        if k == 0:
            ag.relay()
    ag.drain()
    written = pltpu.make_async_copy(out_t, all_ref.at[:, pl.ds(3 * cols, cols)], loaded.at[1])
    written.start()

    def key_grad(rows, at):
        return (kacc[rows, at] * root).astype(BF16).astype(F32)

    def inner(i, carry):
        rows = pl.ds(pl.multiple_of(i * count, count), count)
        mine[1:2, rows] = row_sums(key_grad(rows, slice(0, cols)) * k_ref[rows, :].astype(F32))
        out_ref[rows, 2 * cols : 3 * cols] = vacc[rows, :].astype(BF16)
        return carry

    lax.fori_loop(0, ways, inner, 0)
    total[...] = exchange_rows(g, mine, arrived, xsend, xrecv)
    sums_ref[...] = jnp.zeros_like(sums_ref)
    small = tile_of(count, 256)

    def finish(i, carry):
        rows = pl.ds(pl.multiple_of(i * small, small), small)
        inverse = lax.rsqrt(as_columns(stat_ref[:, rows]) * (1.0 / width) + NORM_EPS)
        mean = as_columns(total[:, rows]) * (1.0 / width)
        cosine, sine = cos_ref[rows, :], sin_ref[rows, :]
        for part, normed in ((0, qn_ref), (1, kn_ref)):
            scale, middle = inverse[:, part : part + 1], mean[:, part : part + 1]
            for h in range(heads):
                at = slice(h * head_width, (h + 1) * head_width)
                value = gq[rows, at].astype(F32) if part == 0 else key_grad(rows, at)
                e = value * cosine - pltpu.roll(value, head_width // 2, 1) * sine
                unit = normed[rows, at].astype(F32)
                start = pl.multiple_of(g.me * cols + h * head_width, head_width)
                gain = gain_ref[part : part + 1, pl.ds(start, head_width)]
                to = slice(part * cols + h * head_width, part * cols + (h + 1) * head_width)
                out_ref[rows, to] = (scale * (e * gain - unit * middle)).astype(BF16)
                sums_ref[part : part + 1, at] += jnp.sum(e * unit, axis=0, keepdims=True)
        return carry

    lax.fori_loop(0, ways * count // small, finish, 0)
    written.wait()


def attention_back(ways, lens, grad, w_all, attn, q_low, k_low, v_low, qn, kn, lse, stats, gains, cosine, sine):
    rows, width = grad.shape
    count, cols = attn.shape
    head_width = cosine.shape[1]
    return remote_call(
        functools.partial(attention_back_kernel, ways, head_width),
        (
            jax.ShapeDtypeStruct((count, 3 * cols), BF16),
            jax.ShapeDtypeStruct((8, cols), F32),
            jax.ShapeDtypeStruct((width, 4 * cols), BF16),
        ),
        [pl.BlockSpec(memory_space=pltpu.SMEM), VM, ANY] + [VM] * 11,
        (VM, VM, ANY),
        [
            pltpu.VMEM((count, width), BF16),
            pltpu.VMEM((width, cols), F32),
            pltpu.VMEM((width, cols), BF16),
            pltpu.VMEM((width, cols), BF16),
            pltpu.SemaphoreType.DMA((2,)),
            pltpu.VMEM((rows, cols), BF16),
            pltpu.VMEM((count, cols), BF16),
            pltpu.VMEM((rows, cols), F32),
            pltpu.VMEM((count, cols), F32),
            pltpu.VMEM((count, cols), F32),
            pltpu.VMEM((8, rows), F32),
            pltpu.VMEM((8, count), F32),
            pltpu.VMEM((ways - 1, 8, count), F32),
            pltpu.VMEM((8, count), F32),
        ]
        + sems(Gather.sems(ways))
        + [pltpu.SemaphoreType.DMA((1,))]
        + sems(ways - 1),
        9,
        4 * count * width * cols,
        1_000_000,
    )(lens, grad, w_all, attn, q_low, k_low, v_low, qn, kn, lse, stats, gains, cosine, sine)


def weight_grads_kernel(x_ref, d_ref, old_ref, out_ref):
    out_ref[...] = dot_tn(x_ref[...], d_ref[...]).astype(BF16)


def weight_grads(x_full, d_qkv, grads):
    count, width = x_full.shape
    depth = d_qkv.shape[1]
    tm, tn = tile_of(width, 512), tile_of(depth, 768)
    return pl.pallas_call(
        weight_grads_kernel,
        out_shape=jax.ShapeDtypeStruct(grads.shape, BF16),
        grid=(width // tm, depth // tn),
        in_specs=[
            pl.BlockSpec((count, tm), lambda i, j: (0, i)),
            pl.BlockSpec((count, tn), lambda i, j: (0, j)),
            ANY,
        ],
        out_specs=pl.BlockSpec((tm, tn), lambda i, j: (i, j)),
        input_output_aliases={2: 0},
        compiler_params=pltpu.CompilerParams(
            dimension_semantics=("arbitrary", "arbitrary"), vmem_limit_bytes=VMEM_BYTES
        ),
        cost_estimate=pl.CostEstimate(flops=0, bytes_accessed=1_000_000, transcendentals=0),
    )(x_full, d_qkv, grads)


def scatter_dp(terms, axis):
    return lax.psum_scatter(terms.astype(BF16), "dp", scatter_dimension=axis, tiled=True).astype(F32)


def gather_dp(weights, axis):
    return lax.all_gather(weights, "dp", axis=axis, tiled=True)


def interleave(gate, up, unit):
    rows = gate.shape[0]
    return jnp.stack([gate.reshape(rows, -1, unit), up.reshape(rows, -1, unit)], axis=2).reshape(rows, -1)


def local(
    layer_in, cotangent, lengths, w_query, w_key, w_value, w_out, w_gate, w_up, w_down,
    gain_query, gain_key, gain_attn, gain_ffn,
):
    rows, width = layer_in.shape
    ways, dp_ways = lax.axis_size("seq"), lax.axis_size("dp")
    count = rows * ways
    head_width = width // HEADS
    cols = width // ways
    part = gain_query.shape[0]
    lens = lengths[0]
    seq_me = lax.axis_index("seq")
    mine = w_gate.shape[1]
    joined = mine % 128 == 0
    unit = mine if joined else tile_of(mine * dp_ways, 256)

    w_all = gather_dp(jnp.concatenate([w_query, w_key, w_value, w_out.T], axis=1), 0)
    if joined:
        w_both = gather_dp(jnp.concatenate([w_gate, w_up], axis=1), 1)
    else:
        w_both = interleave(gather_dp(w_gate, 1), gather_dp(w_up, 1), unit)
    all_down = gather_dp(w_down, 0)

    four = jnp.stack([gain_query, gain_key, gain_attn, gain_ffn]).astype(F32)
    x_full, gain_tiles, cosine, sine = enter(
        ways, dp_ways, lens, layer_in, jnp.pad(four, ((0, 4), (0, 128 - part)))
    )
    gains = gain_tiles[:, :, :4, :part].transpose(2, 1, 0, 3).reshape(4, width)

    q_low, k_low, v_low, qn, kn, stats = project(ways, x_full, w_all, gains, cosine, sine)
    attn, lse = attend(lens, q_low, k_low, v_low, head_width)

    whole = jax.ShapeDtypeStruct((rows, width), F32)
    half = jax.ShapeDtypeStruct((rows, width), BF16)
    eight = jax.ShapeDtypeStruct((8, width), F32)
    hidden, unit_a, inv_a, hidden_low = meet(
        ways, attn, w_all, True, after_attention, (layer_in, gains),
        (whole, half, jax.ShapeDtypeStruct((rows, 128), F32), half), 3, 3 * cols,
    )
    hidden_full, both, act = expand(ways, hidden_low, w_both, unit)
    layer_out, sums_f, grad_m = meet(
        ways, act, all_down, False, after_ffn, (hidden, cotangent, gains), (half, eight, half), 4
    )
    d_both, grad_down = expand_back(ways, grad_m, all_down, act, both, unit)
    out_down = scatter_dp(grad_down, 0)
    grad_both = dot_tn(hidden_full, d_both).astype(BF16)
    d_both, grad_both = lax.optimization_barrier((d_both, grad_both))
    if joined:
        out_both = scatter_dp(grad_both, 1)
        out_gate, out_up = out_both[:, :mine], out_both[:, mine:]
    else:
        pieces = grad_both.reshape(width, -1, 2, unit)
        out_gate = scatter_dp(pieces[:, :, 0].reshape(width, -1), 1)
        out_up = scatter_dp(pieces[:, :, 1].reshape(width, -1), 1)
    grad_hidden, sums_a, grad_a = meet(
        ways, d_both, w_both, True, before_ffn, (cotangent, unit_a, inv_a, gains), (whole, eight, half), 5
    )
    grad_a, out_down = lax.optimization_barrier((grad_a, out_down))
    d_qkv, sums_qk, grad_all = attention_back(
        ways, lens, grad_a, w_all, attn, q_low, k_low, v_low, qn, kn, lse, stats, gains, cosine, sine
    )
    grad_all = weight_grads(x_full, d_qkv, grad_all)
    d_qkv, grad_all, out_gate, out_up = lax.optimization_barrier((d_qkv, grad_all, out_gate, out_up))
    out_all = scatter_dp(grad_all, 0)

    own = lax.dynamic_update_slice(jnp.zeros((2, width), F32), sums_qk[:2], (0, seq_me * cols))
    norms = jnp.stack([jnp.sum(sums_a, axis=0), jnp.sum(sums_f, axis=0)])
    tiles = jnp.concatenate([own, norms]).reshape(4, dp_ways, ways, part).transpose(1, 2, 0, 3)
    tiles = jnp.pad(tiles, ((0, 0), (0, 0), (0, 4), (0, 128 - part)))
    grad_in, gain_sums = leave(ways, dp_ways, d_qkv, w_all, grad_hidden, tiles)
    return (
        layer_out,
        grad_in,
        out_all[:, :cols],
        out_all[:, cols : 2 * cols],
        out_all[:, 2 * cols : 3 * cols],
        out_all[:, 3 * cols :].T,
        out_gate,
        out_up,
        out_down,
        gain_sums[0, :part],
        gain_sums[1, :part],
        gain_sums[2, :part],
        gain_sums[3, :part],
    )


def solution(mesh):
    both = P(("dp", "seq"))
    rows = P(("dp", "seq"), None)
    columns = P(None, ("dp", "seq"))
    square = P("dp", "seq")
    in_specs = (
        rows, rows, P("dp", None), square, square, square, P("seq", "dp"), columns, columns, rows, both, both, both, both,
    )
    out_specs = (
        rows, rows, square, square, square, P("seq", "dp"), columns, columns, rows, both, both, both, both,
    )
    return jax.shard_map(local, mesh=mesh, in_specs=in_specs, out_specs=out_specs, check_vma=False)
```

```python
import functools
import math

import jax
import jax.numpy as jnp
from jax import lax
from jax.experimental import pallas as pl
from jax.experimental.pallas import tpu as pltpu
from jax.sharding import PartitionSpec as P

HEADS = 16
NORM_EPS = 1e-06
ROPE_BASE = 500000.0
MASKED = -1e30
LONGEST = 1024
LOG2E = 1.4426950408889634

F32 = jnp.float32
BF16 = jnp.bfloat16
MESH = pl.DeviceIdType.MESH
VMEM_BYTES = 60 * 1024 * 1024
ANY = pl.BlockSpec(memory_space=pl.ANY)
VM = pl.BlockSpec(memory_space=pltpu.VMEM)


def dot_nn(a, b):
    return lax.dot_general(a, b, (((1,), (0,)), ((), ())), preferred_element_type=F32)


def dot_nt(a, b):
    return lax.dot_general(a, b, (((1,), (1,)), ((), ())), preferred_element_type=F32)


def dot_tn(a, b):
    return lax.dot_general(a, b, (((0,), (0,)), ((), ())), preferred_element_type=F32)


def row_sums(values):
    folded = values[:, 0:128]
    for k in range(1, values.shape[1] // 128):
        folded = folded + values[:, k * 128 : (k + 1) * 128]
    return jnp.sum(jnp.transpose(folded), axis=0, keepdims=True)


def as_columns(rows8):
    return jnp.transpose(jnp.concatenate([rows8] * 16, axis=0))


def tile_of(extent, most):
    return most if extent % most == 0 else extent


def bounds_of(lens_ref):
    first = lens_ref[0]
    second = first + lens_ref[1]
    return first, second, second + lens_ref[2]


def first_key(slot, bounds):
    a, b, c = bounds
    return jnp.where(slot < a, 0, jnp.where(slot < b, a, jnp.where(slot < c, b, slot)))


class Square:
    def __init__(self, ways):
        self.ways = ways
        self.me = lax.axis_index("seq")
        self.square = ways == 4
        if self.square:
            self.x = self.me + 1 - 2 * lax.rem(self.me, 2)
            self.y = lax.rem(self.me + 2, 4)
            self.d = 3 - self.me

    def peer(self, p):
        return lax.rem(self.me + p, self.ways)

    def near(self):
        if self.square:
            return [self.x, self.y]
        return [self.peer(p) for p in range(1, self.ways)]

    def everyone(self):
        return [self.peer(p) for p in range(1, self.ways)]

    def order(self):
        if self.square:
            return [self.d, self.x, self.y, self.me]
        return self.everyone() + [self.me]


def greet(devices):
    barrier = pltpu.get_barrier_semaphore()
    for device in devices:
        pl.semaphore_signal(barrier, inc=1, device_id=device, device_id_type=MESH)
    pl.semaphore_wait(barrier, len(devices))


def to_seq(src, dst, send, recv, peer):
    return pltpu.make_async_remote_copy(
        src_ref=src, dst_ref=dst, send_sem=send, recv_sem=recv, device_id={"seq": peer}, device_id_type=MESH
    )


def to_dp(src, dst, send, recv, peer):
    return pltpu.make_async_remote_copy(
        src_ref=src, dst_ref=dst, send_sem=send, recv_sem=recv, device_id={"dp": peer}, device_id_type=MESH
    )


class Gather:
    def __init__(self, group, src, full, send, recv, own_sem):
        self.g, self.src, self.full, self.send, self.recv = group, src, full, send, recv
        self.rows = src.shape[0]
        self.own = pltpu.make_async_copy(src, self.chunk(group.me), own_sem)
        self.seen = set()

    @staticmethod
    def sems(ways):
        return 12 if ways == 4 else ways - 1

    def chunk(self, index):
        return self.full.at[pl.ds(index * self.rows, self.rows)]

    def quarter(self, index, which):
        h = self.rows // 4
        return self.full.at[pl.ds(index * self.rows + which * h, h)]

    def cp(self, k, src, dst, peer):
        return to_seq(src, dst, self.send.at[k], self.recv.at[k], peer)

    def start(self):
        g, h = self.g, self.rows // 4
        if g.square:
            parts = [self.src.at[pl.ds(j * h, h)] for j in range(4)]
            self.over_x = {j: self.cp(k, parts[j], self.quarter(g.me, j), g.x) for k, j in enumerate((0, 2, 1, 3))}
            self.over_y = {j: self.cp(4 + k, parts[j], self.quarter(g.me, j), g.y) for k, j in enumerate((1, 3, 0, 2))}
            for j, k in ((0, 1), (2, 3), (1, 0), (3, 2)):
                self.over_x[j].start()
                self.over_y[k].start()
        else:
            self.first = [self.cp(p - 1, self.src, self.chunk(g.me), g.peer(p)) for p in range(1, g.ways)]
            for c in self.first:
                c.start()
        self.own.start()

    def relay(self):
        g = self.g
        if not g.square:
            return
        self.turned = {}
        for k, j in enumerate((0, 1, 2, 3)):
            here, there, copy = (g.x, g.y, self.over_x[j]) if j % 2 == 0 else (g.y, g.x, self.over_y[j])
            copy.wait_recv()
            self.turned[j] = self.cp(8 + k, self.quarter(here, j), self.quarter(here, j), there)
            self.turned[j].start()

    def arrive(self, k, halves=(0, 1)):
        g = self.g
        halves = [h for h in halves if (k, h) not in self.seen]
        self.seen.update((k, h) for h in halves)
        if k == 0:
            if 0 in halves:
                self.own.wait()
            return g.me
        if not g.square:
            if 0 in halves:
                self.first[k - 1].wait_recv()
            return lax.rem(g.me + g.ways - k, g.ways)
        for h in halves:
            if k == 1:
                self.over_x[2 * h + 1].wait_recv()
            elif k == 2:
                self.over_y[2 * h].wait_recv()
            else:
                self.turned[2 * h].wait_recv()
                self.turned[2 * h + 1].wait_recv()
        return (g.x, g.y, g.d)[k - 1]

    def drain(self):
        if self.g.square:
            for copies in (self.over_x, self.over_y, self.turned):
                for j in range(4):
                    copies[j].wait_send()
        else:
            for c in self.first:
                c.wait_send()


class Scatter:
    @staticmethod
    def buffers(ways, rows, width):
        if ways == 4:
            return [
                pltpu.VMEM((3, rows, width), BF16),
                pltpu.VMEM((2, rows, width), BF16),
                pltpu.VMEM((2, rows // 2, width), BF16),
            ]
        return [
            pltpu.VMEM((ways - 1, rows, width), BF16),
            pltpu.VMEM((ways - 1, rows, width), BF16),
            pltpu.VMEM((2, 16, width), BF16),
        ]

    def __init__(self, group, out, arrived, relayed, send, recv):
        self.g, self.out, self.arrived, self.relayed, self.send, self.recv = group, out, arrived, relayed, send, recv
        self.rows = out.shape[1]

    def cp(self, k, src, dst, peer):
        return to_seq(src, dst, self.send.at[k], self.recv.at[k], peer)

    def run(self, left, right, own):
        g, h = self.g, self.rows // 2
        out, arrived, relayed = self.out, self.arrived, self.relayed
        left.copy(1).start()
        if not g.square:
            self.sent = []
            for p in range(1, g.ways):
                right.product(left.get(p - 1), out.at[p - 1], BF16)
                if p + 1 < g.ways:
                    left.copy(p + 1).start()
                c = self.cp(p - 1, out.at[p - 1], arrived.at[p - 1], g.peer(p))
                c.start()
                self.sent.append(c)
            right.product(left.get(g.ways - 1), own, F32)
            return
        top, low = pl.ds(0, h), pl.ds(h, h)
        right.product(left.get(0, top), out.at[2, top], BF16)
        c0 = self.cp(0, out.at[2, top], relayed.at[0], g.x)
        c0.start()
        right.product(left.get(0, low), out.at[2, low], BF16)
        c1 = self.cp(1, out.at[2, low], relayed.at[1], g.y)
        c1.start()
        left.copy(2).start()
        right.product(left.get(1, top), out.at[0, top], BF16)
        c2 = self.cp(2, out.at[0, top], arrived.at[0, top], g.x)
        c2.start()
        right.product(left.get(2, low), out.at[1, low], BF16)
        c3 = self.cp(3, out.at[1, low], arrived.at[1, low], g.y)
        c3.start()
        right.product(left.get(1, low), out.at[0, low], BF16)
        left.copy(3).start()
        right.product(left.get(2, top), out.at[1, top], BF16)
        self.sent = [c0, c1, c2, c3]
        self.relay()
        right.product(left.get(3), own, F32)

    def relay(self):
        g, h = self.g, self.rows // 4
        out, arrived, relayed = self.out, self.arrived, self.relayed
        c0, c1, c2, c3 = self.sent
        step = tile_of(h, 64)

        def add(slot, base, which, offset):
            def body(t, carry):
                rows = pl.ds(base + t * step, step)
                have = out[slot, rows, :].astype(F32)
                more = relayed[which, pl.ds(offset + t * step, step), :].astype(F32)
                out[slot, rows, :] = (have + more).astype(BF16)
                return carry

            lax.fori_loop(0, h // step, body, 0)

        c1.wait_recv()
        self.last = [[], []]
        for j in range(2):
            add(0, 2 * h + j * h, 1, j * h)
            rows = pl.ds((2 + j) * h, h)
            c = self.cp(4 + j, out.at[0, rows], arrived.at[0, rows], g.x)
            c.start()
            self.last[j].append(c)
            if j == 0:
                c0.wait_recv()
            add(1, j * h, 0, j * h)
            rows = pl.ds(j * h, h)
            c = self.cp(6 + j, out.at[1, rows], arrived.at[1, rows], g.y)
            c.start()
            self.last[j].append(c)

    def results(self, step, handle, early=True):
        count = self.rows // step

        def run(first, n):
            def body(t, carry):
                handle(first + t)
                return carry

            lax.fori_loop(0, n, body, 0)

        if not early or not self.g.square or count % 4:
            self.finish()
            run(0, count)
            return
        for c in self.sent[2:]:
            c.wait_recv()
        for j in range(2):
            for c in self.last[j]:
                c.wait_recv()
            run(j * (count // 4), count // 4)
            run((2 + j) * (count // 4), count // 4)

    def finish(self):
        if self.g.square:
            for c in self.sent[2:] + self.last[0] + self.last[1]:
                c.wait_recv()
        else:
            for c in self.sent:
                c.wait_recv()

    def drain(self):
        for c in self.sent + (self.last[0] + self.last[1] if self.g.square else []):
            c.wait_send()

    def total(self, own, rows):
        value = own[rows, :]
        for k in range(self.arrived.shape[0]):
            value = value + self.arrived[k, rows, :].astype(F32)
        return value


def remote_call(kernel, outs, in_specs, out_specs, scratch, collective_id, flops, nbytes):
    return pl.pallas_call(
        kernel,
        out_shape=outs,
        in_specs=in_specs,
        out_specs=out_specs,
        scratch_shapes=scratch,
        compiler_params=pltpu.CompilerParams(
            collective_id=collective_id, has_side_effects=True, vmem_limit_bytes=VMEM_BYTES
        ),
        cost_estimate=pl.CostEstimate(flops=0, bytes_accessed=nbytes, transcendentals=0),
    )


def sems(n):
    return [pltpu.SemaphoreType.DMA((n,)), pltpu.SemaphoreType.DMA((n,))]


def write_tables(lens_ref, cos_ref, sin_ref):
    count, head_width = cos_ref.shape
    half = head_width // 2
    step = tile_of(count, 256)
    bounds = bounds_of(lens_ref)
    lane = lax.broadcasted_iota(jnp.int32, (1, head_width), 1)
    folded = jnp.where(lane < half, lane, lane - half).astype(F32)
    frequency = jnp.exp(folded * (-2.0 / head_width * math.log(ROPE_BASE)))
    sign = jnp.where(lane < half, -1.0, 1.0)

    def body(t, carry):
        rows = pl.ds(pl.multiple_of(t * step, step), step)
        slots = t * step + lax.broadcasted_iota(jnp.int32, (step, head_width), 0)
        a, b, c = bounds
        begin = jnp.where(slots < a, 0, jnp.where(slots < b, a, jnp.where(slots < c, b, c)))
        angles = (slots - begin).astype(F32) * frequency
        cos_ref[rows, :] = jnp.cos(angles)
        sin_ref[rows, :] = jnp.sin(angles) * sign
        return carry

    lax.fori_loop(0, count // step, body, 0)


def enter_kernel(
    ways, dp_ways, lens_ref, x_ref, gain_ref, full_ref, gains_ref, cos_ref, sin_ref,
    send, recv, own_sem, gsend, grecv,
):
    g = Square(ways)
    dp_me = lax.axis_index("dp")
    dp_peers = [lax.rem(dp_me + p, dp_ways) for p in range(1, dp_ways)]
    greet([{"seq": q} for q in g.everyone()] + [{"dp": p} for p in dp_peers])
    ag = Gather(g, x_ref, full_ref, send, recv, own_sem.at[0])
    ag.start()

    gains_ref[g.me, dp_me] = gain_ref[...]
    first = [
        to_dp(gain_ref, gains_ref.at[g.me, dp_me], gsend.at[k], grecv.at[k], p) for k, p in enumerate(dp_peers)
    ]
    for c in first:
        c.start()
    write_tables(lens_ref, cos_ref, sin_ref)
    for c in first:
        c.wait_recv()
    base = dp_ways - 1
    second = [
        to_seq(gains_ref.at[g.me], gains_ref.at[g.me], gsend.at[base + k], grecv.at[base + k], q)
        for k, q in enumerate(g.everyone())
    ]
    for c in second:
        c.start()
    ag.relay()
    for c in second:
        c.wait_recv()
    for c in first + second:
        c.wait_send()
    for k in range(ways):
        ag.arrive(k)
    ag.drain()


def enter(ways, dp_ways, lens, x, gains):
    rows, width = x.shape
    count, head_width = ways * rows, width // HEADS
    table = jax.ShapeDtypeStruct((count, head_width), F32)
    return remote_call(
        functools.partial(enter_kernel, ways, dp_ways),
        (
            jax.ShapeDtypeStruct((count, width), BF16),
            jax.ShapeDtypeStruct((ways, dp_ways, 8, 128), F32),
            table,
            table,
        ),
        [pl.BlockSpec(memory_space=pltpu.SMEM), ANY, VM],
        (ANY, VM, VM, VM),
        sems(Gather.sems(ways))
        + [pltpu.SemaphoreType.DMA((1,))]
        + sems(dp_ways - 1 + ways - 1),
        0,
        0,
        1_000_000,
    )(lens, x, gains)


def exchange_rows(g, mine, arrived, send, recv):
    copies = [
        to_seq(mine, arrived.at[k], send.at[k], recv.at[k], q) for k, q in enumerate(g.everyone())
    ]
    for c in copies:
        c.start()
    for c in copies:
        c.wait_recv()
    total = mine[...]
    for k in range(g.ways - 1):
        total = total + arrived[k]
    for c in copies:
        c.wait_send()
    return total


def project_kernel(
    ways, x_ref, w_ref, gain_ref, cos_ref, sin_ref, q_ref, k_ref, v_ref, qn_ref, kn_ref, stat_ref,
    qf, kf, mine, arrived, send, recv, buffer, ready,
):
    g = Square(ways)
    count, width = x_ref.shape
    cols = q_ref.shape[1]
    step = buffer.shape[1]
    steps = count // step

    def fetch(i, slot):
        rows = pl.ds(pl.multiple_of(i * step, step), step)
        return pltpu.make_async_copy(x_ref.at[rows], buffer.at[slot], ready.at[slot])

    fetch(0, 0).start()
    greet([{"seq": q} for q in g.everyone()])
    mine[...] = jnp.zeros_like(mine)

    def project(i, carry):
        slot = lax.rem(i, 2)

        @pl.when(i + 1 < steps)
        def _():
            fetch(i + 1, 1 - slot).start()

        fetch(i, slot).wait()
        rows = pl.ds(pl.multiple_of(i * step, step), step)
        xs = buffer[slot]
        for part, ref in ((0, qf), (1, kf)):
            value = dot_nn(xs, w_ref[:, part * cols : (part + 1) * cols])
            ref[rows, :] = value
            mine[part : part + 1, rows] = row_sums(value * value)
        v_ref[rows, :] = dot_nn(xs, w_ref[:, 2 * cols : 3 * cols]).astype(BF16)
        return carry

    lax.fori_loop(0, steps, project, 0)
    stat_ref[...] = exchange_rows(g, mine, arrived, send, recv)
    small = tile_of(count, 256)

    def finish(i, carry):
        rows = pl.ds(pl.multiple_of(i * small, small), small)
        inverse = lax.rsqrt(as_columns(stat_ref[:, rows]) * (1.0 / width) + NORM_EPS)
        cosine, sine = cos_ref[rows, :], sin_ref[rows, :]
        for part, src, normed, out in ((0, qf, qn_ref, q_ref), (1, kf, kn_ref, k_ref)):
            scale = inverse[:, part : part + 1]
            for h in range(cols // 128):
                at = slice(h * 128, (h + 1) * 128)
                unit = src[rows, at] * scale
                normed[rows, at] = unit.astype(BF16)
                start = pl.multiple_of(g.me * cols + h * 128, 128)
                value = unit * gain_ref[part : part + 1, pl.ds(start, 128)]
                out[rows, at] = (value * cosine + pltpu.roll(value, 64, 1) * sine).astype(BF16)
        return carry

    lax.fori_loop(0, count // small, finish, 0)


def project(ways, x_full, w_all, gains, cosine, sine):
    count, width = x_full.shape
    cols = w_all.shape[1] // 4
    step = tile_of(count, 512)
    low = jax.ShapeDtypeStruct((count, cols), BF16)
    return remote_call(
        functools.partial(project_kernel, ways),
        (low, low, low, low, low, jax.ShapeDtypeStruct((8, count), F32)),
        [ANY, VM, VM, VM, VM],
        (VM,) * 6,
        [
            pltpu.VMEM((count, cols), F32),
            pltpu.VMEM((count, cols), F32),
            pltpu.VMEM((8, count), F32),
            pltpu.VMEM((ways - 1, 8, count), F32),
        ]
        + sems(ways - 1)
        + [pltpu.VMEM((2, step, width), BF16), pltpu.SemaphoreType.DMA((2,))],
        1,
        2 * count * width * 3 * cols,
        1_000_000,
    )(x_full, w_all, gains, cosine, sine)


def attend_kernel(head_width, lens_ref, q_ref, k_ref, v_ref, o_ref, lse_ref, acc, top, tot):
    block, cols = q_ref.shape
    heads = cols // head_width
    i = pl.program_id(0)
    bounds = bounds_of(lens_ref)
    slots = i * block + lax.broadcasted_iota(jnp.int32, (1, block), 1)
    begins = first_key(slots, bounds)
    factor = head_width ** (-0.5) * LOG2E

    def scores_of(kb, h):
        at = slice(h * head_width, (h + 1) * head_width)
        rows = pl.ds(pl.multiple_of(kb * block, block), block)
        keys = kb * block + lax.broadcasted_iota(jnp.int32, (block, block), 0)
        visible = (keys <= slots) & (keys >= begins)
        scores = dot_nt(k_ref[rows, at], q_ref[:, at]) * factor
        return jnp.where(visible, scores, MASKED), v_ref[rows, at], at

    for h in range(heads):
        scores, values, at = scores_of(i, h)
        largest = jnp.max(scores, axis=0, keepdims=True)
        weights = jnp.exp2(scores - largest)
        top[h : h + 1, :] = largest
        tot[h : h + 1, :] = jnp.sum(weights, axis=0, keepdims=True)
        acc[at, :] = dot_tn(values, weights.astype(BF16))

    def earlier(t, carry):
        kb = i - 1 - t
        for h in range(heads):
            scores, values, at = scores_of(kb, h)
            before = top[h : h + 1, :]
            largest = jnp.maximum(before, jnp.max(scores, axis=0, keepdims=True))
            weights = jnp.exp2(scores - largest)
            shrink = jnp.exp2(before - largest)
            top[h : h + 1, :] = largest
            tot[h : h + 1, :] = tot[h : h + 1, :] * shrink + jnp.sum(weights, axis=0, keepdims=True)
            acc[at, :] = acc[at, :] * shrink + dot_tn(values, weights.astype(BF16))
        return carry

    lowest = first_key(i * block, bounds) // block
    lax.fori_loop(0, i - lowest, earlier, 0)
    lse_ref[...] = jnp.zeros_like(lse_ref)
    for h in range(heads):
        at = slice(h * head_width, (h + 1) * head_width)
        total = tot[h : h + 1, :]
        o_ref[:, at] = jnp.transpose(acc[at, :] * (1.0 / total)).astype(BF16)
        lse_ref[h : h + 1, :] = top[h : h + 1, :] + jnp.log2(total)


def attend(lens, q_low, k_low, v_low, head_width):
    count, cols = q_low.shape
    block = tile_of(count, 512)
    tile = pl.BlockSpec((block, cols), lambda i, lens: (i, 0))
    whole = pl.BlockSpec((count, cols), lambda i, lens: (0, 0))
    line = pl.BlockSpec((8, block), lambda i, lens: (0, i))
    return pl.pallas_call(
        functools.partial(attend_kernel, head_width),
        out_shape=(jax.ShapeDtypeStruct((count, cols), BF16), jax.ShapeDtypeStruct((8, count), F32)),
        grid_spec=pltpu.PrefetchScalarGridSpec(
            num_scalar_prefetch=1,
            grid=(count // block,),
            in_specs=[tile, whole, whole],
            out_specs=(tile, line),
            scratch_shapes=[pltpu.VMEM((cols, block), F32), pltpu.VMEM((8, block), F32), pltpu.VMEM((8, block), F32)],
        ),
        compiler_params=pltpu.CompilerParams(dimension_semantics=("arbitrary",), vmem_limit_bytes=VMEM_BYTES),
        cost_estimate=pl.CostEstimate(flops=0, bytes_accessed=1_000_000, transcendentals=0),
    )(lens, q_low, k_low, v_low)


class Right:
    def __init__(self, src, ref, loaded, transposed, first_column):
        self.ref, self.transposed, self.loaded = ref, transposed, loaded
        self.width = ref.shape[0] if transposed else ref.shape[1]
        self.tile = self.width // self.tiles(self.width)
        self.src = src.at[:, pl.ds(first_column, ref.shape[1])] if transposed else src
        self.fresh = True

    @staticmethod
    def tiles(width):
        return width // tile_of(width, 512)

    @staticmethod
    def scratch(shape, transposed):
        width = shape[0] if transposed else shape[1]
        return [pltpu.VMEM(shape, BF16), pltpu.SemaphoreType.DMA((Right.tiles(width),))]

    def copy(self, t):
        at = pl.ds(pl.multiple_of(t * self.tile, self.tile), self.tile)
        if self.transposed:
            return pltpu.make_async_copy(self.src.at[at], self.ref.at[at], self.loaded.at[t])
        return pltpu.make_async_copy(self.src.at[:, at], self.ref.at[:, at], self.loaded.at[t])

    def start(self):
        for t in range(self.width // self.tile):
            self.copy(t).start()

    def product(self, lhs, out, dtype):
        fresh, self.fresh = self.fresh, False

        def body(t, carry):
            at = pl.ds(pl.multiple_of(t * self.tile, self.tile), self.tile)
            if fresh:
                self.copy(t).wait()
            value = dot_nt(lhs[...], self.ref[at, :]) if self.transposed else dot_nn(lhs[...], self.ref[:, at])
            out[:, at] = value.astype(dtype)
            return carry

        lax.fori_loop(0, self.width // self.tile, body, 0)


class Rows:
    def __init__(self, order, ref, buffer, ready):
        self.order, self.ref, self.buffer, self.ready = order, ref, buffer, ready
        self.waited = set()

    @staticmethod
    def scratch(rows, depth):
        return [pltpu.VMEM((2, rows, depth), BF16), pltpu.SemaphoreType.DMA((2,))]

    def copy(self, turn):
        count = self.buffer.shape[1]
        rows = pl.ds(pl.multiple_of(self.order[turn] * count, count), count)
        return pltpu.make_async_copy(self.ref.at[rows], self.buffer.at[turn % 2], self.ready.at[turn % 2])

    def get(self, turn, part=None):
        if turn not in self.waited:
            self.copy(turn).wait()
            self.waited.add(turn)
        return self.buffer.at[turn % 2] if part is None else self.buffer.at[turn % 2, part]


def fold8(value):
    return jnp.sum(value.reshape(value.shape[0] // 8, 8, value.shape[1]), axis=0)


def meet_kernel(ways, transposed, first_column, epilogue, n_extra, n_out, own_is_out, lhs, rhs, *refs):
    sources, outs, scratch = refs[:n_extra], refs[n_extra : n_extra + n_out], refs[n_extra + n_out :]
    own = outs[0] if own_is_out else scratch[0]
    scratch = scratch if own_is_out else scratch[1:]
    out, arrived, relayed, send, recv, buffer, ready, w_ref, loaded, fetched = scratch[:10]
    extra = scratch[10:]
    g = Square(ways)
    left = Rows(g.order(), lhs, buffer, ready)
    right = Right(rhs, w_ref, loaded, transposed, first_column)
    left.copy(0).start()
    right.start()
    fetches = [pltpu.make_async_copy(a, b, fetched.at[j]) for j, (a, b) in enumerate(zip(sources, extra))]
    greet([{"seq": q} for q in g.near()])
    count = own.shape[0]
    rs = Scatter(g, out, arrived, relayed, send, recv)
    for c in fetches:
        c.start()
    rs.run(left, right, own)
    for c in fetches:
        c.wait()
    step = tile_of(count, 64)

    def handle(t):
        rows = pl.ds(pl.multiple_of(t * step, step), step)
        epilogue(rows, rs.total(own, rows), extra, outs, t)

    rs.results(step, handle, transposed)
    rs.drain()


def meet(ways, lhs, rhs, transposed, epilogue, extra, outs, collective_id, first_column=0):
    count, depth = lhs.shape
    width = rhs.shape[0] if transposed else rhs.shape[1]
    rows = count // ways
    n = 8 if ways == 4 else ways - 1
    own_is_out = outs[0].dtype == F32
    scratch = [] if own_is_out else [pltpu.VMEM((rows, width), F32)]
    scratch += Scatter.buffers(ways, rows, width) + sems(n) + Rows.scratch(rows, depth)
    scratch += Right.scratch((width, depth) if transposed else (depth, width), transposed)
    scratch += [pltpu.SemaphoreType.DMA((len(extra),))] + [pltpu.VMEM(e.shape, e.dtype) for e in extra]
    return remote_call(
        functools.partial(meet_kernel, ways, transposed, first_column, epilogue, len(extra), len(outs), own_is_out),
        tuple(outs),
        [ANY] * (2 + len(extra)),
        (VM,) * len(outs),
        scratch,
        collective_id,
        2 * count * width * depth,
        1_000_000,
    )(lhs, rhs, *extra)


def after_attention(rows, branch, extra, outs, t):
    x_ref, gain_ref = extra
    hidden_ref, unit_ref, inv_ref, source = outs
    inverse = lax.rsqrt(jnp.mean(branch * branch, axis=1, keepdims=True) + NORM_EPS)
    unit = branch * inverse
    hidden = x_ref[rows, :].astype(F32) + unit * gain_ref[2:3, :]
    hidden_ref[rows, :] = hidden
    unit_ref[rows, :] = unit.astype(BF16)
    inv_ref[rows, :] = jnp.broadcast_to(inverse, (inverse.shape[0], 128))
    source[rows, :] = hidden.astype(BF16)


def after_ffn(rows, branch, extra, outs, t):
    hidden_ref, cot_ref, gain_ref = extra
    out_ref, sums_ref, source = outs
    gain = gain_ref[3:4, :]
    inverse = lax.rsqrt(jnp.mean(branch * branch, axis=1, keepdims=True) + NORM_EPS)
    unit = branch * inverse
    out_ref[rows, :] = (hidden_ref[rows, :] + unit * gain).astype(BF16)
    e = cot_ref[rows, :].astype(F32)
    term = fold8(e * unit)

    @pl.when(t == 0)
    def _():
        sums_ref[...] = term

    @pl.when(t > 0)
    def _():
        sums_ref[...] += term

    eg = e * gain
    mean = jnp.mean(eg * unit, axis=1, keepdims=True)
    source[rows, :] = (inverse * (eg - unit * mean)).astype(BF16)


def before_ffn(rows, terms, extra, outs, t):
    cot_ref, unit_ref, inv_ref, gain_ref = extra
    hidden_ref, sums_ref, source = outs
    e = cot_ref[rows, :].astype(F32) + terms
    hidden_ref[rows, :] = e
    unit = unit_ref[rows, :].astype(F32)
    term = fold8(e * unit)

    @pl.when(t == 0)
    def _():
        sums_ref[...] = term

    @pl.when(t > 0)
    def _():
        sums_ref[...] += term

    eg = e * gain_ref[2:3, :]
    mean = jnp.mean(eg * unit, axis=1, keepdims=True)
    source[rows, :] = (inv_ref[rows, 0:1] * (eg - unit * mean)).astype(BF16)


def leave_kernel(
    ways, dp_ways, d_ref, w_hbm, hidden_hbm, tiles_ref, grad_ref, gains_ref,
    hidden_ref, out, arrived, relayed, send, recv, from_dp, partial, from_seq, gsend, grecv, buffer, ready,
    w_ref, loaded, fetched,
):
    g = Square(ways)
    left = Rows(g.order(), d_ref, buffer, ready)
    right = Right(w_hbm, w_ref, loaded, True, 0)
    left.copy(0).start()
    right.start()
    fetch = pltpu.make_async_copy(hidden_hbm, hidden_ref, fetched.at[0])
    dp_me = lax.axis_index("dp")
    dp_peers = [lax.rem(dp_me + p, dp_ways) for p in range(1, dp_ways)]
    greet([{"seq": q} for q in g.everyone()] + [{"dp": p} for p in dp_peers])
    first = [
        to_dp(tiles_ref.at[p], from_dp.at[k], gsend.at[k], grecv.at[k], p) for k, p in enumerate(dp_peers)
    ]
    for c in first:
        c.start()
    fetch.start()
    count = grad_ref.shape[0]
    rs = Scatter(g, out, arrived, relayed, send, recv)
    rs.run(left, right, grad_ref)
    for c in first:
        c.wait_recv()
    value = tiles_ref[dp_me]
    for k in range(dp_ways - 1):
        value = value + from_dp[k]
    partial[...] = value
    base = dp_ways - 1
    second = [
        to_seq(partial.at[q], from_seq.at[k], gsend.at[base + k], grecv.at[base + k], q)
        for k, q in enumerate(g.everyone())
    ]
    for c in second:
        c.start()
    for c in second:
        c.wait_recv()
    value = partial[g.me]
    for k in range(ways - 1):
        value = value + from_seq[k]
    gains_ref[...] = value
    fetch.wait()
    step = tile_of(count, 64)

    def handle(t):
        rows = pl.ds(pl.multiple_of(t * step, step), step)
        grad_ref[rows, :] = hidden_ref[rows, :] + rs.total(grad_ref, rows)

    rs.results(step, handle)
    for c in first + second:
        c.wait_send()
    rs.drain()


def leave(ways, dp_ways, d_qkv, w_all, grad_hidden, tiles):
    count, depth = d_qkv.shape
    rows, width = grad_hidden.shape
    n = 8 if ways == 4 else ways - 1
    m = dp_ways - 1 + ways - 1
    return remote_call(
        functools.partial(leave_kernel, ways, dp_ways),
        (jax.ShapeDtypeStruct((rows, width), F32), jax.ShapeDtypeStruct((8, 128), F32)),
        [ANY, ANY, ANY, VM],
        (VM, VM),
        [pltpu.VMEM((rows, width), F32)]
        + Scatter.buffers(ways, rows, width)
        + sems(n)
        + [
            pltpu.VMEM((dp_ways - 1, ways, 8, 128), F32),
            pltpu.VMEM((ways, 8, 128), F32),
            pltpu.VMEM((ways - 1, 8, 128), F32),
        ]
        + sems(m)
        + Rows.scratch(rows, depth)
        + Right.scratch((width, depth), True)
        + [pltpu.SemaphoreType.DMA((1,))],
        6,
        2 * count * width * depth,
        1_000_000,
    )(d_qkv, w_all, grad_hidden, tiles)


def sigmoid(v):
    return 1.0 / (1.0 + jnp.exp(-v))


def halves(unit, blocks):
    return [
        (slice(2 * j * unit, (2 * j + 1) * unit), slice((2 * j + 1) * unit, (2 * j + 2) * unit)) for j in range(blocks)
    ]


def expand_kernel(
    ways, unit, blocks, src_ref, w_hbm, all_ref, both_ref, act_ref,
    full_ref, w_ref, loaded, out_sem, stage, act_stage, done, send, recv, own_sem,
):
    g = Square(ways)
    load = pltpu.make_async_copy(w_hbm, w_ref, loaded.at[0])
    greet([{"seq": q} for q in g.near()])
    ag = Gather(g, src_ref, full_ref, send, recv, own_sem.at[0])
    ag.start()
    load.start()
    load.wait()
    count = src_ref.shape[0]
    outgoing = []
    tile = unit * blocks
    tiles = w_ref.shape[1] // (2 * tile)

    def results(slot, rows, t):
        wide = pl.ds(pl.multiple_of(t * 2 * tile, 2 * tile), 2 * tile)
        at = pl.ds(pl.multiple_of(t * tile, tile), tile)
        return [
            pltpu.make_async_copy(stage.at[slot], both_ref.at[rows, wide], done.at[slot, 0]),
            pltpu.make_async_copy(act_stage.at[slot], act_ref.at[rows, at], done.at[slot, 1]),
        ]

    half = count // 2
    turns = []

    def part(k, h):
        index = ag.arrive(k, (h,))
        rows = pl.ds(pl.multiple_of(index * count + h * half, half), half)
        turn = len(turns)
        turns.append((k, h))
        outgoing.append(pltpu.make_async_copy(full_ref.at[rows], all_ref.at[rows], out_sem.at[turn]))
        outgoing[-1].start()

        def body(t, carry):
            slot = lax.rem(turn * tiles + t, 2)
            both = dot_nn(full_ref[rows, :], w_ref[:, pl.ds(pl.multiple_of(t * 2 * tile, 2 * tile), 2 * tile)])

            @pl.when(turn * tiles + t >= 2)
            def _():
                for c in results(slot, rows, t):
                    c.wait()

            stage[slot] = both.astype(BF16)
            for j, (first, second) in enumerate(halves(unit, blocks)):
                gate, up = both[:, first], both[:, second]
                value = gate * sigmoid(gate) * up
                act_stage[slot, :, j * unit : (j + 1) * unit] = value.astype(BF16)
            for c in results(slot, rows, t):
                c.start()
            return carry

        lax.fori_loop(0, tiles, body, 0)

    part(0, 0)
    part(0, 1)
    ag.relay()
    for k in range(1, ways - 1, 2):
        for h in range(2):
            for j in (k, k + 1):
                if j < ways - 1:
                    part(j, h)
    part(ways - 1, 0)
    part(ways - 1, 1)
    last = len(turns) * tiles
    for u in range(max(0, last - 2), last):
        for c in results(u % 2, pl.ds(0, half), 0):
            c.wait()
    for c in outgoing:
        c.wait()
    ag.drain()


def blocks_of(units, unit):
    return 2 if (units // unit) % 2 == 0 else 1


def expand(ways, hidden, w_both, unit):
    rows, width = hidden.shape
    units = w_both.shape[1] // 2
    count = ways * rows
    blocks = blocks_of(units, unit)
    tile = unit * blocks
    return remote_call(
        functools.partial(expand_kernel, ways, unit, blocks),
        (
            jax.ShapeDtypeStruct((count, width), BF16),
            jax.ShapeDtypeStruct((count, 2 * units), BF16),
            jax.ShapeDtypeStruct((count, units), BF16),
        ),
        [VM, ANY],
        (ANY,) * 3,
        [
            pltpu.VMEM((count, width), BF16),
            pltpu.VMEM((width, 2 * units), BF16),
            pltpu.SemaphoreType.DMA((1,)),
            pltpu.SemaphoreType.DMA((2 * ways,)),
            pltpu.VMEM((2, rows // 2, 2 * tile), BF16),
            pltpu.VMEM((2, rows // 2, tile), BF16),
            pltpu.SemaphoreType.DMA((2, 2)),
        ]
        + sems(Gather.sems(ways))
        + [pltpu.SemaphoreType.DMA((1,))],
        7,
        4 * count * width * units,
        1_000_000,
    )(hidden, w_both)


def expand_back_kernel(
    ways, unit, blocks, src_ref, w_hbm, act_hbm, both_ref, dboth_ref, down_hbm,
    full, acc, down_ref, w_ref, act_ref, loaded, out_sem, inputs, stage, ready, done, send, recv, own_sem,
):
    g = Square(ways)
    loads = [pltpu.make_async_copy(a, b, loaded.at[j]) for j, (a, b) in enumerate(((w_hbm, w_ref), (act_hbm, act_ref)))]
    greet([{"seq": q} for q in g.near()])
    ag = Gather(g, src_ref, full, send, recv, own_sem.at[0])
    ag.start()
    for c in loads:
        c.start()
    for c in loads:
        c.wait()
    count, width = src_ref.shape
    half = count // 2
    tile = unit * blocks
    units = w_ref.shape[0]
    tiles = units // tile
    wide = tile_of(width, 1024)
    across = width // wide

    def view(ref, rows, t):
        return ref.at[rows, pl.ds(pl.multiple_of(t * 2 * tile, 2 * tile), 2 * tile)]

    turns = []

    def back(k, h):
        index = ag.arrive(k, (h,))
        rows = pl.ds(pl.multiple_of(index * count + h * half, half), half)
        turn = len(turns)
        turns.append((k, h))

        def load(slot, t):
            return pltpu.make_async_copy(view(both_ref, rows, t), inputs.at[slot], ready.at[slot])

        def result(slot, t):
            return pltpu.make_async_copy(stage.at[slot], view(dboth_ref, rows, t), done.at[slot])

        load((turn * tiles) % 2, 0).start()

        def body(t, carry):
            slot = lax.rem(turn * tiles + t, 2)
            at = pl.ds(pl.multiple_of(t * tile, tile), tile)

            @pl.when(t + 1 < tiles)
            def _():
                load(1 - slot, t + 1).start()

            grads = dot_nt(full[rows, :], w_ref[at, :])
            load(slot, t).wait()

            @pl.when(turn * tiles + t >= 2)
            def _():
                result(slot, t).wait()

            for j, (first, second) in enumerate(halves(unit, blocks)):
                grad = grads[:, j * unit : (j + 1) * unit]
                gate = inputs[slot, :, first].astype(F32)
                up = inputs[slot, :, second].astype(F32)
                s = sigmoid(gate)
                part = grad * s
                stage[slot, :, first] = (part * up * (1.0 + gate * (1.0 - s))).astype(BF16)
                stage[slot, :, second] = (part * gate).astype(BF16)
            result(slot, t).start()
            return carry

        lax.fori_loop(0, tiles, body, 0)

    def written(u):
        own = pl.ds(pl.multiple_of(lax.rem(u, tiles) * tile, tile), tile)
        at = pl.ds(pl.multiple_of(u // tiles * wide, wide), wide)
        return pltpu.make_async_copy(down_ref.at[own, at], down_hbm.at[own, at], out_sem.at[u])

    def down(k, first, rows, last=False):
        index = ag.arrive(k, ())
        those = pl.ds(pl.multiple_of(index * count + first, rows), rows)

        def body(u, carry):
            own = pl.ds(pl.multiple_of(lax.rem(u, tiles) * tile, tile), tile)
            at = pl.ds(pl.multiple_of(u // tiles * wide, wide), wide)
            term = dot_tn(act_ref[those, own], full[those, at])
            if k == 0:
                acc[own, at] = term
            elif not last:
                acc[own, at] += term
            else:
                down_ref[own, at] = (acc[own, at] + term).astype(BF16)
                written(u).start()
            return carry

        lax.fori_loop(0, tiles * across, body, 0)

    back(0, 0)
    back(0, 1)
    down(0, 0, count)
    ag.relay()
    for k in range(1, ways - 1, 2):
        pair = [j for j in (k, k + 1) if j < ways - 1]
        for h in range(2):
            for j in pair:
                back(j, h)
        for j in pair:
            down(j, 0, count)
    back(ways - 1, 0)
    down(ways - 1, 0, half)
    back(ways - 1, 1)
    down(ways - 1, half, half, last=True)
    last = len(turns) * tiles
    for u in range(max(0, last - 2), last):
        pltpu.make_async_copy(stage.at[u % 2], view(dboth_ref, pl.ds(0, half), 0), done.at[u % 2]).wait()
    for u in range(tiles * across):
        written(u).wait()
    ag.drain()


def expand_back(ways, grad, w_down, act, both, unit):
    rows, width = grad.shape
    count, units = act.shape
    blocks = blocks_of(units, unit)
    tile = unit * blocks
    return remote_call(
        functools.partial(expand_back_kernel, ways, unit, blocks),
        (jax.ShapeDtypeStruct((count, 2 * units), BF16), jax.ShapeDtypeStruct((units, width), BF16)),
        [VM, ANY, ANY, ANY],
        (ANY, ANY),
        [
            pltpu.VMEM((count, width), BF16),
            pltpu.VMEM((units, width), F32),
            pltpu.VMEM((units, width), BF16),
            pltpu.VMEM((units, width), BF16),
            pltpu.VMEM((count, units), BF16),
            pltpu.SemaphoreType.DMA((2,)),
            pltpu.SemaphoreType.DMA((units // tile * (width // tile_of(width, 1024)),)),
            pltpu.VMEM((2, rows // 2, 2 * tile), BF16),
            pltpu.VMEM((2, rows // 2, 2 * tile), BF16),
            pltpu.SemaphoreType.DMA((2,)),
            pltpu.SemaphoreType.DMA((2,)),
        ]
        + sems(Gather.sems(ways))
        + [pltpu.SemaphoreType.DMA((1,))],
        8,
        4 * count * width * units,
        1_000_000,
    )(grad, w_down, act, both)


def attention_back_kernel(
    ways, head_width, lens_ref, src_ref, w_hbm, attn_ref, q_ref, k_ref, v_ref, qn_ref, kn_ref, lse_ref, stat_ref,
    gain_ref, cos_ref, sin_ref, out_ref, sums_ref, all_ref,
    full, acc, w_ref, out_t, loaded, grad, gq, qacc, kacc, vacc, centre, mine, arrived, total,
    send, recv, own_sem, xsend, xrecv,
):
    g = Square(ways)
    load = pltpu.make_async_copy(w_hbm.at[:, pl.ds(3 * attn_ref.shape[1], attn_ref.shape[1])], w_ref, loaded.at[0])
    load.start()
    greet([{"seq": q} for q in g.everyone()])
    ag = Gather(g, src_ref, full, send, recv, own_sem.at[0])
    ag.start()
    kacc[...] = jnp.zeros_like(kacc)
    vacc[...] = jnp.zeros_like(vacc)
    mine[...] = jnp.zeros_like(mine)
    count, width = src_ref.shape
    cols = attn_ref.shape[1]
    heads = cols // head_width
    wide = tile_of(width, 1024)
    bounds = bounds_of(lens_ref)
    root = head_width ** (-0.5)
    factor = root * LOG2E
    back = (LONGEST - 1 + count - 1) // count
    load.wait()
    for k in range(ways):
        index = ag.arrive(k)
        rows = pl.ds(pl.multiple_of(index * count, count), count)
        grad[...] = dot_nn(full[rows, :], w_ref[...]).astype(BF16)

        def body(u, carry):
            at = pl.ds(pl.multiple_of(u * wide, wide), wide)
            term = dot_tn(full[rows, at], attn_ref[rows, :])
            if k == 0:
                acc[at, :] = term
            elif k < ways - 1:
                acc[at, :] += term
            else:
                out_t[at, :] = (acc[at, :] + term).astype(BF16)
            return carry

        lax.fori_loop(0, width // wide, body, 0)
        slots = index * count + lax.broadcasted_iota(jnp.int32, (1, count), 1)
        begins = first_key(slots, bounds)
        for h in range(heads):
            at = slice(h * head_width, (h + 1) * head_width)
            centre[h : h + 1, :] = row_sums(grad[:, at].astype(F32) * attn_ref[rows, at].astype(F32))
        qacc[...] = jnp.zeros_like(qacc)

        def keys_block(t, carry):
            kb = index - t
            there = pl.ds(pl.multiple_of(kb * count, count), count)
            keys = kb * count + lax.broadcasted_iota(jnp.int32, (count, count), 0)
            visible = (keys <= slots) & (keys >= begins)
            for h in range(heads):
                at = slice(h * head_width, (h + 1) * head_width)
                keys_h, query, grad_h = k_ref[there, at], q_ref[rows, at], grad[:, at]
                scores = dot_nt(keys_h, query) * factor - lse_ref[h : h + 1, rows]
                weights = jnp.where(visible, jnp.exp2(scores), 0.0)
                grad_probs = dot_nt(v_ref[there, at], grad_h)
                grad_scores = (weights * (grad_probs - centre[h : h + 1, :])).astype(BF16)
                vacc[there, at] += dot_nn(weights.astype(BF16), grad_h)
                kacc[there, at] += dot_nn(grad_scores, query)
                qacc[:, at] += dot_tn(grad_scores, keys_h)
            return carry

        lax.fori_loop(0, jnp.minimum(index, back) + 1, keys_block, 0)
        gq[rows, :] = (qacc[...] * root).astype(BF16)
        mine[0:1, rows] = row_sums(gq[rows, :].astype(F32) * q_ref[rows, :].astype(F32))
        if k == 0:
            ag.relay()
    ag.drain()
    written = pltpu.make_async_copy(out_t, all_ref.at[:, pl.ds(3 * cols, cols)], loaded.at[1])
    written.start()

    def key_grad(rows, at):
        return (kacc[rows, at] * root).astype(BF16).astype(F32)

    def inner(i, carry):
        rows = pl.ds(pl.multiple_of(i * count, count), count)
        mine[1:2, rows] = row_sums(key_grad(rows, slice(0, cols)) * k_ref[rows, :].astype(F32))
        out_ref[rows, 2 * cols : 3 * cols] = vacc[rows, :].astype(BF16)
        return carry

    lax.fori_loop(0, ways, inner, 0)
    total[...] = exchange_rows(g, mine, arrived, xsend, xrecv)
    sums_ref[...] = jnp.zeros_like(sums_ref)
    small = tile_of(count, 256)

    def finish(i, carry):
        rows = pl.ds(pl.multiple_of(i * small, small), small)
        inverse = lax.rsqrt(as_columns(stat_ref[:, rows]) * (1.0 / width) + NORM_EPS)
        mean = as_columns(total[:, rows]) * (1.0 / width)
        cosine, sine = cos_ref[rows, :], sin_ref[rows, :]
        for part, normed in ((0, qn_ref), (1, kn_ref)):
            scale, middle = inverse[:, part : part + 1], mean[:, part : part + 1]
            for h in range(heads):
                at = slice(h * head_width, (h + 1) * head_width)
                value = gq[rows, at].astype(F32) if part == 0 else key_grad(rows, at)
                e = value * cosine - pltpu.roll(value, head_width // 2, 1) * sine
                unit = normed[rows, at].astype(F32)
                start = pl.multiple_of(g.me * cols + h * head_width, head_width)
                gain = gain_ref[part : part + 1, pl.ds(start, head_width)]
                to = slice(part * cols + h * head_width, part * cols + (h + 1) * head_width)
                out_ref[rows, to] = (scale * (e * gain - unit * middle)).astype(BF16)
                sums_ref[part : part + 1, at] += jnp.sum(e * unit, axis=0, keepdims=True)
        return carry

    lax.fori_loop(0, ways * count // small, finish, 0)
    written.wait()


def attention_back(ways, lens, grad, w_all, attn, q_low, k_low, v_low, qn, kn, lse, stats, gains, cosine, sine):
    rows, width = grad.shape
    count, cols = attn.shape
    head_width = cosine.shape[1]
    return remote_call(
        functools.partial(attention_back_kernel, ways, head_width),
        (
            jax.ShapeDtypeStruct((count, 3 * cols), BF16),
            jax.ShapeDtypeStruct((8, cols), F32),
            jax.ShapeDtypeStruct((width, 4 * cols), BF16),
        ),
        [pl.BlockSpec(memory_space=pltpu.SMEM), VM, ANY] + [VM] * 11,
        (VM, VM, ANY),
        [
            pltpu.VMEM((count, width), BF16),
            pltpu.VMEM((width, cols), F32),
            pltpu.VMEM((width, cols), BF16),
            pltpu.VMEM((width, cols), BF16),
            pltpu.SemaphoreType.DMA((2,)),
            pltpu.VMEM((rows, cols), BF16),
            pltpu.VMEM((count, cols), BF16),
            pltpu.VMEM((rows, cols), F32),
            pltpu.VMEM((count, cols), F32),
            pltpu.VMEM((count, cols), F32),
            pltpu.VMEM((8, rows), F32),
            pltpu.VMEM((8, count), F32),
            pltpu.VMEM((ways - 1, 8, count), F32),
            pltpu.VMEM((8, count), F32),
        ]
        + sems(Gather.sems(ways))
        + [pltpu.SemaphoreType.DMA((1,))]
        + sems(ways - 1),
        9,
        4 * count * width * cols,
        1_000_000,
    )(lens, grad, w_all, attn, q_low, k_low, v_low, qn, kn, lse, stats, gains, cosine, sine)


def weight_grads_kernel(x_ref, d_ref, old_ref, out_ref):
    out_ref[...] = dot_tn(x_ref[...], d_ref[...]).astype(BF16)


def weight_grads(x_full, d_qkv, grads):
    count, width = x_full.shape
    depth = d_qkv.shape[1]
    tm, tn = tile_of(width, 512), tile_of(depth, 768)
    return pl.pallas_call(
        weight_grads_kernel,
        out_shape=jax.ShapeDtypeStruct(grads.shape, BF16),
        grid=(width // tm, depth // tn),
        in_specs=[
            pl.BlockSpec((count, tm), lambda i, j: (0, i)),
            pl.BlockSpec((count, tn), lambda i, j: (0, j)),
            ANY,
        ],
        out_specs=pl.BlockSpec((tm, tn), lambda i, j: (i, j)),
        input_output_aliases={2: 0},
        compiler_params=pltpu.CompilerParams(
            dimension_semantics=("arbitrary", "arbitrary"), vmem_limit_bytes=VMEM_BYTES
        ),
        cost_estimate=pl.CostEstimate(flops=0, bytes_accessed=1_000_000, transcendentals=0),
    )(x_full, d_qkv, grads)


def scatter_dp(terms, axis):
    return lax.psum_scatter(terms.astype(BF16), "dp", scatter_dimension=axis, tiled=True)


def gather_dp(weights, axis):
    return lax.all_gather(weights, "dp", axis=axis, tiled=True)


def interleave(gate, up, unit):
    rows = gate.shape[0]
    return jnp.stack([gate.reshape(rows, -1, unit), up.reshape(rows, -1, unit)], axis=2).reshape(rows, -1)


def local(
    layer_in, cotangent, lengths, w_query, w_key, w_value, w_out, w_gate, w_up, w_down,
    gain_query, gain_key, gain_attn, gain_ffn,
):
    rows, width = layer_in.shape
    ways, dp_ways = lax.axis_size("seq"), lax.axis_size("dp")
    count = rows * ways
    head_width = width // HEADS
    cols = width // ways
    part = gain_query.shape[0]
    lens = lengths[0]
    seq_me = lax.axis_index("seq")
    mine = w_gate.shape[1]
    joined = mine % 128 == 0
    unit = mine if joined else tile_of(mine * dp_ways, 256)

    w_all = gather_dp(jnp.concatenate([w_query, w_key, w_value, w_out.T], axis=1), 0)
    if joined:
        w_both = gather_dp(jnp.concatenate([w_gate, w_up], axis=1), 1)
    else:
        w_both = interleave(gather_dp(w_gate, 1), gather_dp(w_up, 1), unit)
    all_down = gather_dp(w_down, 0)

    four = jnp.stack([gain_query, gain_key, gain_attn, gain_ffn]).astype(F32)
    x_full, gain_tiles, cosine, sine = enter(
        ways, dp_ways, lens, layer_in, jnp.pad(four, ((0, 4), (0, 128 - part)))
    )
    gains = gain_tiles[:, :, :4, :part].transpose(2, 1, 0, 3).reshape(4, width)

    q_low, k_low, v_low, qn, kn, stats = project(ways, x_full, w_all, gains, cosine, sine)
    attn, lse = attend(lens, q_low, k_low, v_low, head_width)

    whole = jax.ShapeDtypeStruct((rows, width), F32)
    half = jax.ShapeDtypeStruct((rows, width), BF16)
    eight = jax.ShapeDtypeStruct((8, width), F32)
    hidden, unit_a, inv_a, hidden_low = meet(
        ways, attn, w_all, True, after_attention, (layer_in, gains),
        (whole, half, jax.ShapeDtypeStruct((rows, 128), F32), half), 3, 3 * cols,
    )
    hidden_full, both, act = expand(ways, hidden_low, w_both, unit)
    layer_out, sums_f, grad_m = meet(
        ways, act, all_down, False, after_ffn, (hidden, cotangent, gains), (half, eight, half), 4
    )
    d_both, grad_down = expand_back(ways, grad_m, all_down, act, both, unit)
    out_down = scatter_dp(grad_down, 0)
    grad_both = dot_tn(hidden_full, d_both).astype(BF16)
    d_both, grad_both = lax.optimization_barrier((d_both, grad_both))
    if joined:
        out_both = [scatter_dp(grad_both, 1)]
    else:
        pieces = grad_both.reshape(width, -1, 2, unit)
        out_both = [scatter_dp(pieces[:, :, j].reshape(width, -1), 1) for j in range(2)]
    grad_hidden, sums_a, grad_a = meet(
        ways, d_both, w_both, True, before_ffn, (cotangent, unit_a, inv_a, gains), (whole, eight, half), 5
    )
    grad_a, out_down = lax.optimization_barrier((grad_a, out_down))
    d_qkv, sums_qk, grad_all = attention_back(
        ways, lens, grad_a, w_all, attn, q_low, k_low, v_low, qn, kn, lse, stats, gains, cosine, sine
    )
    grad_all = weight_grads(x_full, d_qkv, grad_all)
    d_qkv, grad_all, out_both = lax.optimization_barrier((d_qkv, grad_all, out_both))
    out_all = scatter_dp(grad_all, 0).astype(F32)
    out_gate, out_up = (out_both[0][:, :mine], out_both[0][:, mine:]) if joined else out_both

    own = lax.dynamic_update_slice(jnp.zeros((2, width), F32), sums_qk[:2], (0, seq_me * cols))
    norms = jnp.stack([jnp.sum(sums_a, axis=0), jnp.sum(sums_f, axis=0)])
    tiles = jnp.concatenate([own, norms]).reshape(4, dp_ways, ways, part).transpose(1, 2, 0, 3)
    tiles = jnp.pad(tiles, ((0, 0), (0, 0), (0, 4), (0, 128 - part)))
    grad_in, gain_sums = leave(ways, dp_ways, d_qkv, w_all, grad_hidden, tiles)
    return (
        layer_out,
        grad_in,
        out_all[:, :cols],
        out_all[:, cols : 2 * cols],
        out_all[:, 2 * cols : 3 * cols],
        out_all[:, 3 * cols :].T,
        out_gate.astype(F32),
        out_up.astype(F32),
        out_down.astype(F32),
        gain_sums[0, :part],
        gain_sums[1, :part],
        gain_sums[2, :part],
        gain_sums[3, :part],
    )


def solution(mesh):
    both = P(("dp", "seq"))
    rows = P(("dp", "seq"), None)
    columns = P(None, ("dp", "seq"))
    square = P("dp", "seq")
    in_specs = (
        rows, rows, P("dp", None), square, square, square, P("seq", "dp"), columns, columns, rows, both, both, both, both,
    )
    out_specs = (
        rows, rows, square, square, square, P("seq", "dp"), columns, columns, rows, both, both, both, both,
    )
    return jax.shard_map(local, mesh=mesh, in_specs=in_specs, out_specs=out_specs, check_vma=False)
```

```python
import functools
import math

import jax
import jax.numpy as jnp
from jax import lax
from jax.experimental import pallas as pl
from jax.experimental.pallas import tpu as pltpu
from jax.sharding import PartitionSpec as P

HEADS = 16
NORM_EPS = 1e-06
ROPE_BASE = 500000.0
MASKED = -1e30
LONGEST = 1024
LOG2E = 1.4426950408889634

F32 = jnp.float32
BF16 = jnp.bfloat16
MESH = pl.DeviceIdType.MESH
VMEM_BYTES = 60 * 1024 * 1024
ANY = pl.BlockSpec(memory_space=pl.ANY)
VM = pl.BlockSpec(memory_space=pltpu.VMEM)


def dot_nn(a, b):
    return lax.dot_general(a, b, (((1,), (0,)), ((), ())), preferred_element_type=F32)


def dot_nt(a, b):
    return lax.dot_general(a, b, (((1,), (1,)), ((), ())), preferred_element_type=F32)


def dot_tn(a, b):
    return lax.dot_general(a, b, (((0,), (0,)), ((), ())), preferred_element_type=F32)


def row_sums(values):
    folded = values[:, 0:128]
    for k in range(1, values.shape[1] // 128):
        folded = folded + values[:, k * 128 : (k + 1) * 128]
    return jnp.sum(jnp.transpose(folded), axis=0, keepdims=True)


def as_columns(rows8):
    return jnp.transpose(jnp.concatenate([rows8] * 16, axis=0))


def tile_of(extent, most):
    return most if extent % most == 0 else extent


def bounds_of(lens_ref):
    first = lens_ref[0]
    second = first + lens_ref[1]
    return first, second, second + lens_ref[2]


def first_key(slot, bounds):
    a, b, c = bounds
    return jnp.where(slot < a, 0, jnp.where(slot < b, a, jnp.where(slot < c, b, slot)))


class Square:
    def __init__(self, ways):
        self.ways = ways
        self.me = lax.axis_index("seq")
        self.square = ways == 4
        if self.square:
            self.x = self.me + 1 - 2 * lax.rem(self.me, 2)
            self.y = lax.rem(self.me + 2, 4)
            self.d = 3 - self.me

    def peer(self, p):
        return lax.rem(self.me + p, self.ways)

    def near(self):
        if self.square:
            return [self.x, self.y]
        return [self.peer(p) for p in range(1, self.ways)]

    def everyone(self):
        return [self.peer(p) for p in range(1, self.ways)]

    def order(self):
        if self.square:
            return [self.d, self.x, self.y, self.me]
        return self.everyone() + [self.me]


def greet(devices):
    barrier = pltpu.get_barrier_semaphore()
    for device in devices:
        pl.semaphore_signal(barrier, inc=1, device_id=device, device_id_type=MESH)
    pl.semaphore_wait(barrier, len(devices))


def to_seq(src, dst, send, recv, peer):
    return pltpu.make_async_remote_copy(
        src_ref=src, dst_ref=dst, send_sem=send, recv_sem=recv, device_id={"seq": peer}, device_id_type=MESH
    )


def to_dp(src, dst, send, recv, peer):
    return pltpu.make_async_remote_copy(
        src_ref=src, dst_ref=dst, send_sem=send, recv_sem=recv, device_id={"dp": peer}, device_id_type=MESH
    )


class Gather:
    def __init__(self, group, src, full, send, recv, own_sem):
        self.g, self.src, self.full, self.send, self.recv = group, src, full, send, recv
        self.rows = src.shape[0]
        self.own = pltpu.make_async_copy(src, self.chunk(group.me), own_sem)
        self.seen = set()
        self.turned = {}

    @staticmethod
    def sems(ways):
        return 12 if ways == 4 else ways - 1

    def chunk(self, index):
        return self.full.at[pl.ds(index * self.rows, self.rows)]

    def quarter(self, index, which):
        h = self.rows // 4
        return self.full.at[pl.ds(index * self.rows + which * h, h)]

    def cp(self, k, src, dst, peer):
        return to_seq(src, dst, self.send.at[k], self.recv.at[k], peer)

    def start(self):
        g, h = self.g, self.rows // 4
        if g.square:
            parts = [self.src.at[pl.ds(j * h, h)] for j in range(4)]
            self.over_x = {j: self.cp(k, parts[j], self.quarter(g.me, j), g.x) for k, j in enumerate((0, 1, 2, 3))}
            self.over_y = {j: self.cp(4 + k, parts[j], self.quarter(g.me, j), g.y) for k, j in enumerate((1, 0, 3, 2))}
            for j, k in ((0, 1), (1, 0), (2, 3), (3, 2)):
                self.over_x[j].start()
                self.over_y[k].start()
        else:
            self.first = [self.cp(p - 1, self.src, self.chunk(g.me), g.peer(p)) for p in range(1, g.ways)]
            for c in self.first:
                c.start()
        self.own.start()

    def relay(self, quarters=(0, 1, 2, 3)):
        g = self.g
        if not g.square:
            return
        for j in quarters:
            here, there, copy = (g.x, g.y, self.over_x[j]) if j % 2 == 0 else (g.y, g.x, self.over_y[j])
            copy.wait_recv()
            self.turned[j] = self.cp(8 + j, self.quarter(here, j), self.quarter(here, j), there)
            self.turned[j].start()

    def arrive(self, k, halves=(0, 1)):
        g = self.g
        halves = [h for h in halves if (k, h) not in self.seen]
        self.seen.update((k, h) for h in halves)
        if k == 0:
            if 0 in halves:
                self.own.wait()
            return g.me
        if not g.square:
            if 0 in halves:
                self.first[k - 1].wait_recv()
            return lax.rem(g.me + g.ways - k, g.ways)
        for h in halves:
            if k == 1:
                self.over_x[2 * h + 1].wait_recv()
            elif k == 2:
                self.over_y[2 * h].wait_recv()
            else:
                self.turned[2 * h].wait_recv()
                self.turned[2 * h + 1].wait_recv()
        return (g.x, g.y, g.d)[k - 1]

    def drain(self):
        if self.g.square:
            for copies in (self.over_x, self.over_y, self.turned):
                for j in range(4):
                    copies[j].wait_send()
        else:
            for c in self.first:
                c.wait_send()


class Scatter:
    @staticmethod
    def buffers(ways, rows, width):
        if ways == 4:
            return [
                pltpu.VMEM((3, rows, width), BF16),
                pltpu.VMEM((2, rows, width), BF16),
                pltpu.VMEM((2, rows // 2, width), BF16),
            ]
        return [
            pltpu.VMEM((ways - 1, rows, width), BF16),
            pltpu.VMEM((ways - 1, rows, width), BF16),
            pltpu.VMEM((2, 16, width), BF16),
        ]

    def __init__(self, group, out, arrived, relayed, send, recv):
        self.g, self.out, self.arrived, self.relayed, self.send, self.recv = group, out, arrived, relayed, send, recv
        self.rows = out.shape[1]

    def cp(self, k, src, dst, peer):
        return to_seq(src, dst, self.send.at[k], self.recv.at[k], peer)

    def run(self, left, right, own):
        g, h = self.g, self.rows // 2
        out, arrived, relayed = self.out, self.arrived, self.relayed
        left.copy(1).start()
        if not g.square:
            self.sent = []
            for p in range(1, g.ways):
                right.product(left.get(p - 1), out.at[p - 1], BF16)
                if p + 1 < g.ways:
                    left.copy(p + 1).start()
                c = self.cp(p - 1, out.at[p - 1], arrived.at[p - 1], g.peer(p))
                c.start()
                self.sent.append(c)
            right.product(left.get(g.ways - 1), own, F32)
            return
        top, low = pl.ds(0, h), pl.ds(h, h)
        right.product(left.get(0, top), out.at[2, top], BF16)
        c0 = self.cp(0, out.at[2, top], relayed.at[0], g.x)
        c0.start()
        right.product(left.get(0, low), out.at[2, low], BF16)
        c1 = self.cp(1, out.at[2, low], relayed.at[1], g.y)
        c1.start()
        left.copy(2).start()
        right.product(left.get(1, top), out.at[0, top], BF16)
        c2 = self.cp(2, out.at[0, top], arrived.at[0, top], g.x)
        c2.start()
        right.product(left.get(2, low), out.at[1, low], BF16)
        c3 = self.cp(3, out.at[1, low], arrived.at[1, low], g.y)
        c3.start()
        right.product(left.get(1, low), out.at[0, low], BF16)
        left.copy(3).start()
        right.product(left.get(2, top), out.at[1, top], BF16)
        self.sent = [c0, c1, c2, c3]
        self.relay()
        right.product(left.get(3), own, F32)

    def relay(self):
        g, h = self.g, self.rows // 4
        out, arrived, relayed = self.out, self.arrived, self.relayed
        c0, c1, c2, c3 = self.sent
        step = tile_of(h, 64)

        def add(slot, base, which, offset):
            def body(t, carry):
                rows = pl.ds(base + t * step, step)
                have = out[slot, rows, :].astype(F32)
                more = relayed[which, pl.ds(offset + t * step, step), :].astype(F32)
                out[slot, rows, :] = (have + more).astype(BF16)
                return carry

            lax.fori_loop(0, h // step, body, 0)

        c1.wait_recv()
        self.last = [[], []]
        for j in range(2):
            add(0, 2 * h + j * h, 1, j * h)
            rows = pl.ds((2 + j) * h, h)
            c = self.cp(4 + j, out.at[0, rows], arrived.at[0, rows], g.x)
            c.start()
            self.last[j].append(c)
            if j == 0:
                c0.wait_recv()
            add(1, j * h, 0, j * h)
            rows = pl.ds(j * h, h)
            c = self.cp(6 + j, out.at[1, rows], arrived.at[1, rows], g.y)
            c.start()
            self.last[j].append(c)

    def results(self, step, handle, early=True):
        count = self.rows // step

        def run(first, n):
            def body(t, carry):
                handle(first + t)
                return carry

            lax.fori_loop(0, n, body, 0)

        if not early or not self.g.square or count % 4:
            self.finish()
            run(0, count)
            return
        for c in self.sent[2:]:
            c.wait_recv()
        for j in range(2):
            for c in self.last[j]:
                c.wait_recv()
            run(j * (count // 4), count // 4)
            run((2 + j) * (count // 4), count // 4)

    def finish(self):
        if self.g.square:
            for c in self.sent[2:] + self.last[0] + self.last[1]:
                c.wait_recv()
        else:
            for c in self.sent:
                c.wait_recv()

    def drain(self):
        for c in self.sent + (self.last[0] + self.last[1] if self.g.square else []):
            c.wait_send()

    def total(self, own, rows):
        value = own[rows, :]
        for k in range(self.arrived.shape[0]):
            value = value + self.arrived[k, rows, :].astype(F32)
        return value


def remote_call(kernel, outs, in_specs, out_specs, scratch, collective_id, flops, nbytes):
    return pl.pallas_call(
        kernel,
        out_shape=outs,
        in_specs=in_specs,
        out_specs=out_specs,
        scratch_shapes=scratch,
        compiler_params=pltpu.CompilerParams(
            collective_id=collective_id, has_side_effects=True, vmem_limit_bytes=VMEM_BYTES
        ),
        cost_estimate=pl.CostEstimate(flops=0, bytes_accessed=nbytes, transcendentals=0),
    )


def sems(n):
    return [pltpu.SemaphoreType.DMA((n,)), pltpu.SemaphoreType.DMA((n,))]


def write_tables(lens_ref, cos_ref, sin_ref):
    count, head_width = cos_ref.shape
    half = head_width // 2
    step = tile_of(count, 256)
    bounds = bounds_of(lens_ref)
    lane = lax.broadcasted_iota(jnp.int32, (1, head_width), 1)
    folded = jnp.where(lane < half, lane, lane - half).astype(F32)
    frequency = jnp.exp(folded * (-2.0 / head_width * math.log(ROPE_BASE)))
    sign = jnp.where(lane < half, -1.0, 1.0)

    def body(t, carry):
        rows = pl.ds(pl.multiple_of(t * step, step), step)
        slots = t * step + lax.broadcasted_iota(jnp.int32, (step, head_width), 0)
        a, b, c = bounds
        begin = jnp.where(slots < a, 0, jnp.where(slots < b, a, jnp.where(slots < c, b, c)))
        angles = (slots - begin).astype(F32) * frequency
        cos_ref[rows, :] = jnp.cos(angles)
        sin_ref[rows, :] = jnp.sin(angles) * sign
        return carry

    lax.fori_loop(0, count // step, body, 0)


def enter_kernel(
    ways, dp_ways, lens_ref, x_ref, gain_ref, full_ref, gains_ref, cos_ref, sin_ref,
    send, recv, own_sem, gsend, grecv,
):
    g = Square(ways)
    dp_me = lax.axis_index("dp")
    dp_peers = [lax.rem(dp_me + p, dp_ways) for p in range(1, dp_ways)]
    greet([{"seq": q} for q in g.everyone()] + [{"dp": p} for p in dp_peers])
    ag = Gather(g, x_ref, full_ref, send, recv, own_sem.at[0])
    ag.start()

    gains_ref[g.me, dp_me] = gain_ref[...]
    first = [
        to_dp(gain_ref, gains_ref.at[g.me, dp_me], gsend.at[k], grecv.at[k], p) for k, p in enumerate(dp_peers)
    ]
    for c in first:
        c.start()
    write_tables(lens_ref, cos_ref, sin_ref)
    for c in first:
        c.wait_recv()
    base = dp_ways - 1
    second = [
        to_seq(gains_ref.at[g.me], gains_ref.at[g.me], gsend.at[base + k], grecv.at[base + k], q)
        for k, q in enumerate(g.everyone())
    ]
    for c in second:
        c.start()
    ag.relay()
    for c in second:
        c.wait_recv()
    for c in first + second:
        c.wait_send()
    for k in range(ways):
        ag.arrive(k)
    ag.drain()


def enter(ways, dp_ways, lens, x, gains):
    rows, width = x.shape
    count, head_width = ways * rows, width // HEADS
    table = jax.ShapeDtypeStruct((count, head_width), F32)
    return remote_call(
        functools.partial(enter_kernel, ways, dp_ways),
        (
            jax.ShapeDtypeStruct((count, width), BF16),
            jax.ShapeDtypeStruct((ways, dp_ways, 8, 128), F32),
            table,
            table,
        ),
        [pl.BlockSpec(memory_space=pltpu.SMEM), ANY, VM],
        (ANY, VM, VM, VM),
        sems(Gather.sems(ways))
        + [pltpu.SemaphoreType.DMA((1,))]
        + sems(dp_ways - 1 + ways - 1),
        0,
        0,
        1_000_000,
    )(lens, x, gains)


def exchange_rows(g, mine, arrived, send, recv):
    copies = [
        to_seq(mine, arrived.at[k], send.at[k], recv.at[k], q) for k, q in enumerate(g.everyone())
    ]
    for c in copies:
        c.start()
    for c in copies:
        c.wait_recv()
    total = mine[...]
    for k in range(g.ways - 1):
        total = total + arrived[k]
    for c in copies:
        c.wait_send()
    return total


def project_kernel(
    ways, x_ref, w_ref, gain_ref, cos_ref, sin_ref, q_ref, k_ref, v_ref, qn_ref, kn_ref, stat_ref,
    qf, kf, mine, arrived, send, recv, buffer, ready,
):
    g = Square(ways)
    count, width = x_ref.shape
    cols = q_ref.shape[1]
    step = buffer.shape[1]
    steps = count // step

    def fetch(i, slot):
        rows = pl.ds(pl.multiple_of(i * step, step), step)
        return pltpu.make_async_copy(x_ref.at[rows], buffer.at[slot], ready.at[slot])

    fetch(0, 0).start()
    greet([{"seq": q} for q in g.everyone()])
    mine[...] = jnp.zeros_like(mine)

    def project(i, carry):
        slot = lax.rem(i, 2)

        @pl.when(i + 1 < steps)
        def _():
            fetch(i + 1, 1 - slot).start()

        fetch(i, slot).wait()
        rows = pl.ds(pl.multiple_of(i * step, step), step)
        xs = buffer[slot]
        for part, ref in ((0, qf), (1, kf)):
            value = dot_nn(xs, w_ref[:, part * cols : (part + 1) * cols])
            ref[rows, :] = value
            mine[part : part + 1, rows] = row_sums(value * value)
        v_ref[rows, :] = dot_nn(xs, w_ref[:, 2 * cols : 3 * cols]).astype(BF16)
        return carry

    lax.fori_loop(0, steps, project, 0)
    stat_ref[...] = exchange_rows(g, mine, arrived, send, recv)
    small = tile_of(count, 256)

    def finish(i, carry):
        rows = pl.ds(pl.multiple_of(i * small, small), small)
        inverse = lax.rsqrt(as_columns(stat_ref[:, rows]) * (1.0 / width) + NORM_EPS)
        cosine, sine = cos_ref[rows, :], sin_ref[rows, :]
        for part, src, normed, out in ((0, qf, qn_ref, q_ref), (1, kf, kn_ref, k_ref)):
            scale = inverse[:, part : part + 1]
            for h in range(cols // 128):
                at = slice(h * 128, (h + 1) * 128)
                unit = src[rows, at] * scale
                normed[rows, at] = unit.astype(BF16)
                start = pl.multiple_of(g.me * cols + h * 128, 128)
                value = unit * gain_ref[part : part + 1, pl.ds(start, 128)]
                out[rows, at] = (value * cosine + pltpu.roll(value, 64, 1) * sine).astype(BF16)
        return carry

    lax.fori_loop(0, count // small, finish, 0)


def project(ways, x_full, w_all, gains, cosine, sine):
    count, width = x_full.shape
    cols = w_all.shape[1] // 4
    step = tile_of(count, 512)
    low = jax.ShapeDtypeStruct((count, cols), BF16)
    return remote_call(
        functools.partial(project_kernel, ways),
        (low, low, low, low, low, jax.ShapeDtypeStruct((8, count), F32)),
        [ANY, VM, VM, VM, VM],
        (VM,) * 6,
        [
            pltpu.VMEM((count, cols), F32),
            pltpu.VMEM((count, cols), F32),
            pltpu.VMEM((8, count), F32),
            pltpu.VMEM((ways - 1, 8, count), F32),
        ]
        + sems(ways - 1)
        + [pltpu.VMEM((2, step, width), BF16), pltpu.SemaphoreType.DMA((2,))],
        1,
        2 * count * width * 3 * cols,
        1_000_000,
    )(x_full, w_all, gains, cosine, sine)


def attend_kernel(head_width, lens_ref, q_ref, k_ref, v_ref, o_ref, lse_ref, acc, top, tot):
    block, cols = q_ref.shape
    heads = cols // head_width
    i = pl.program_id(0)
    bounds = bounds_of(lens_ref)
    slots = i * block + lax.broadcasted_iota(jnp.int32, (1, block), 1)
    begins = first_key(slots, bounds)
    factor = head_width ** (-0.5) * LOG2E

    def scores_of(kb, h):
        at = slice(h * head_width, (h + 1) * head_width)
        rows = pl.ds(pl.multiple_of(kb * block, block), block)
        keys = kb * block + lax.broadcasted_iota(jnp.int32, (block, block), 0)
        visible = (keys <= slots) & (keys >= begins)
        scores = dot_nt(k_ref[rows, at], q_ref[:, at]) * factor
        return jnp.where(visible, scores, MASKED), v_ref[rows, at], at

    for h in range(heads):
        scores, values, at = scores_of(i, h)
        largest = jnp.max(scores, axis=0, keepdims=True)
        weights = jnp.exp2(scores - largest)
        top[h : h + 1, :] = largest
        tot[h : h + 1, :] = jnp.sum(weights, axis=0, keepdims=True)
        acc[at, :] = dot_tn(values, weights.astype(BF16))

    def earlier(t, carry):
        kb = i - 1 - t
        for h in range(heads):
            scores, values, at = scores_of(kb, h)
            before = top[h : h + 1, :]
            largest = jnp.maximum(before, jnp.max(scores, axis=0, keepdims=True))
            weights = jnp.exp2(scores - largest)
            shrink = jnp.exp2(before - largest)
            top[h : h + 1, :] = largest
            tot[h : h + 1, :] = tot[h : h + 1, :] * shrink + jnp.sum(weights, axis=0, keepdims=True)
            acc[at, :] = acc[at, :] * shrink + dot_tn(values, weights.astype(BF16))
        return carry

    lowest = first_key(i * block, bounds) // block
    lax.fori_loop(0, i - lowest, earlier, 0)
    lse_ref[...] = jnp.zeros_like(lse_ref)
    for h in range(heads):
        at = slice(h * head_width, (h + 1) * head_width)
        total = tot[h : h + 1, :]
        o_ref[:, at] = jnp.transpose(acc[at, :] * (1.0 / total)).astype(BF16)
        lse_ref[h : h + 1, :] = top[h : h + 1, :] + jnp.log2(total)


def attend(lens, q_low, k_low, v_low, head_width):
    count, cols = q_low.shape
    block = tile_of(count, 512)
    tile = pl.BlockSpec((block, cols), lambda i, lens: (i, 0))
    whole = pl.BlockSpec((count, cols), lambda i, lens: (0, 0))
    line = pl.BlockSpec((8, block), lambda i, lens: (0, i))
    return pl.pallas_call(
        functools.partial(attend_kernel, head_width),
        out_shape=(jax.ShapeDtypeStruct((count, cols), BF16), jax.ShapeDtypeStruct((8, count), F32)),
        grid_spec=pltpu.PrefetchScalarGridSpec(
            num_scalar_prefetch=1,
            grid=(count // block,),
            in_specs=[tile, whole, whole],
            out_specs=(tile, line),
            scratch_shapes=[pltpu.VMEM((cols, block), F32), pltpu.VMEM((8, block), F32), pltpu.VMEM((8, block), F32)],
        ),
        compiler_params=pltpu.CompilerParams(dimension_semantics=("arbitrary",), vmem_limit_bytes=VMEM_BYTES),
        cost_estimate=pl.CostEstimate(flops=0, bytes_accessed=1_000_000, transcendentals=0),
    )(lens, q_low, k_low, v_low)


class Right:
    def __init__(self, src, ref, loaded, transposed, first_column):
        self.ref, self.transposed, self.loaded = ref, transposed, loaded
        self.width = ref.shape[0] if transposed else ref.shape[1]
        self.tile = self.width // self.tiles(self.width)
        self.src = src.at[:, pl.ds(first_column, ref.shape[1])] if transposed else src
        self.fresh = True

    @staticmethod
    def tiles(width):
        return width // tile_of(width, 512)

    @staticmethod
    def scratch(shape, transposed):
        width = shape[0] if transposed else shape[1]
        return [pltpu.VMEM(shape, BF16), pltpu.SemaphoreType.DMA((Right.tiles(width),))]

    def copy(self, t):
        at = pl.ds(pl.multiple_of(t * self.tile, self.tile), self.tile)
        if self.transposed:
            return pltpu.make_async_copy(self.src.at[at], self.ref.at[at], self.loaded.at[t])
        return pltpu.make_async_copy(self.src.at[:, at], self.ref.at[:, at], self.loaded.at[t])

    def start(self):
        for t in range(self.width // self.tile):
            self.copy(t).start()

    def product(self, lhs, out, dtype):
        fresh, self.fresh = self.fresh, False

        def body(t, carry):
            at = pl.ds(pl.multiple_of(t * self.tile, self.tile), self.tile)
            if fresh:
                self.copy(t).wait()
            value = dot_nt(lhs[...], self.ref[at, :]) if self.transposed else dot_nn(lhs[...], self.ref[:, at])
            out[:, at] = value.astype(dtype)
            return carry

        lax.fori_loop(0, self.width // self.tile, body, 0)


class Rows:
    def __init__(self, order, ref, buffer, ready):
        self.order, self.ref, self.buffer, self.ready = order, ref, buffer, ready
        self.waited = set()

    @staticmethod
    def scratch(rows, depth):
        return [pltpu.VMEM((2, rows, depth), BF16), pltpu.SemaphoreType.DMA((2,))]

    def copy(self, turn):
        count = self.buffer.shape[1]
        rows = pl.ds(pl.multiple_of(self.order[turn] * count, count), count)
        return pltpu.make_async_copy(self.ref.at[rows], self.buffer.at[turn % 2], self.ready.at[turn % 2])

    def get(self, turn, part=None):
        if turn not in self.waited:
            self.copy(turn).wait()
            self.waited.add(turn)
        return self.buffer.at[turn % 2] if part is None else self.buffer.at[turn % 2, part]


def fold8(value):
    return jnp.sum(value.reshape(value.shape[0] // 8, 8, value.shape[1]), axis=0)


def meet_kernel(ways, transposed, first_column, epilogue, n_extra, n_out, own_is_out, lhs, rhs, *refs):
    sources, outs, scratch = refs[:n_extra], refs[n_extra : n_extra + n_out], refs[n_extra + n_out :]
    own = outs[0] if own_is_out else scratch[0]
    scratch = scratch if own_is_out else scratch[1:]
    out, arrived, relayed, send, recv, buffer, ready, w_ref, loaded, fetched = scratch[:10]
    extra = scratch[10:]
    g = Square(ways)
    left = Rows(g.order(), lhs, buffer, ready)
    right = Right(rhs, w_ref, loaded, transposed, first_column)
    left.copy(0).start()
    right.start()
    fetches = [pltpu.make_async_copy(a, b, fetched.at[j]) for j, (a, b) in enumerate(zip(sources, extra))]
    greet([{"seq": q} for q in g.near()])
    count = own.shape[0]
    rs = Scatter(g, out, arrived, relayed, send, recv)
    for c in fetches:
        c.start()
    rs.run(left, right, own)
    for c in fetches:
        c.wait()
    step = tile_of(count, 64)

    def handle(t):
        rows = pl.ds(pl.multiple_of(t * step, step), step)
        epilogue(rows, rs.total(own, rows), extra, outs, t)

    rs.results(step, handle, transposed)
    rs.drain()


def meet(ways, lhs, rhs, transposed, epilogue, extra, outs, collective_id, first_column=0):
    count, depth = lhs.shape
    width = rhs.shape[0] if transposed else rhs.shape[1]
    rows = count // ways
    n = 8 if ways == 4 else ways - 1
    own_is_out = outs[0].dtype == F32
    scratch = [] if own_is_out else [pltpu.VMEM((rows, width), F32)]
    scratch += Scatter.buffers(ways, rows, width) + sems(n) + Rows.scratch(rows, depth)
    scratch += Right.scratch((width, depth) if transposed else (depth, width), transposed)
    scratch += [pltpu.SemaphoreType.DMA((len(extra),))] + [pltpu.VMEM(e.shape, e.dtype) for e in extra]
    return remote_call(
        functools.partial(meet_kernel, ways, transposed, first_column, epilogue, len(extra), len(outs), own_is_out),
        tuple(outs),
        [ANY] * (2 + len(extra)),
        (VM,) * len(outs),
        scratch,
        collective_id,
        2 * count * width * depth,
        1_000_000,
    )(lhs, rhs, *extra)


def after_attention(rows, branch, extra, outs, t):
    x_ref, gain_ref = extra
    hidden_ref, unit_ref, inv_ref, source = outs
    inverse = lax.rsqrt(jnp.mean(branch * branch, axis=1, keepdims=True) + NORM_EPS)
    unit = branch * inverse
    hidden = x_ref[rows, :].astype(F32) + unit * gain_ref[2:3, :]
    hidden_ref[rows, :] = hidden
    unit_ref[rows, :] = unit.astype(BF16)
    inv_ref[rows, :] = jnp.broadcast_to(inverse, (inverse.shape[0], 128))
    source[rows, :] = hidden.astype(BF16)


def after_ffn(rows, branch, extra, outs, t):
    hidden_ref, cot_ref, gain_ref = extra
    out_ref, sums_ref, source = outs
    gain = gain_ref[3:4, :]
    inverse = lax.rsqrt(jnp.mean(branch * branch, axis=1, keepdims=True) + NORM_EPS)
    unit = branch * inverse
    out_ref[rows, :] = (hidden_ref[rows, :] + unit * gain).astype(BF16)
    e = cot_ref[rows, :].astype(F32)
    term = fold8(e * unit)

    @pl.when(t == 0)
    def _():
        sums_ref[...] = term

    @pl.when(t > 0)
    def _():
        sums_ref[...] += term

    eg = e * gain
    mean = jnp.mean(eg * unit, axis=1, keepdims=True)
    source[rows, :] = (inverse * (eg - unit * mean)).astype(BF16)


def before_ffn(rows, terms, extra, outs, t):
    cot_ref, unit_ref, inv_ref, gain_ref = extra
    hidden_ref, sums_ref, source = outs
    e = cot_ref[rows, :].astype(F32) + terms
    hidden_ref[rows, :] = e
    unit = unit_ref[rows, :].astype(F32)
    term = fold8(e * unit)

    @pl.when(t == 0)
    def _():
        sums_ref[...] = term

    @pl.when(t > 0)
    def _():
        sums_ref[...] += term

    eg = e * gain_ref[2:3, :]
    mean = jnp.mean(eg * unit, axis=1, keepdims=True)
    source[rows, :] = (inv_ref[rows, 0:1] * (eg - unit * mean)).astype(BF16)


def leave_kernel(
    ways, dp_ways, d_ref, w_hbm, hidden_hbm, tiles_ref, grad_ref, gains_ref,
    hidden_ref, out, arrived, relayed, send, recv, from_dp, partial, from_seq, gsend, grecv, buffer, ready,
    w_ref, loaded, fetched,
):
    g = Square(ways)
    left = Rows(g.order(), d_ref, buffer, ready)
    right = Right(w_hbm, w_ref, loaded, True, 0)
    left.copy(0).start()
    right.start()
    fetch = pltpu.make_async_copy(hidden_hbm, hidden_ref, fetched.at[0])
    dp_me = lax.axis_index("dp")
    dp_peers = [lax.rem(dp_me + p, dp_ways) for p in range(1, dp_ways)]
    greet([{"seq": q} for q in g.everyone()] + [{"dp": p} for p in dp_peers])
    first = [
        to_dp(tiles_ref.at[p], from_dp.at[k], gsend.at[k], grecv.at[k], p) for k, p in enumerate(dp_peers)
    ]
    for c in first:
        c.start()
    fetch.start()
    count = grad_ref.shape[0]
    rs = Scatter(g, out, arrived, relayed, send, recv)
    rs.run(left, right, grad_ref)
    for c in first:
        c.wait_recv()
    value = tiles_ref[dp_me]
    for k in range(dp_ways - 1):
        value = value + from_dp[k]
    partial[...] = value
    base = dp_ways - 1
    second = [
        to_seq(partial.at[q], from_seq.at[k], gsend.at[base + k], grecv.at[base + k], q)
        for k, q in enumerate(g.everyone())
    ]
    for c in second:
        c.start()
    for c in second:
        c.wait_recv()
    value = partial[g.me]
    for k in range(ways - 1):
        value = value + from_seq[k]
    gains_ref[...] = value
    fetch.wait()
    step = tile_of(count, 64)

    def handle(t):
        rows = pl.ds(pl.multiple_of(t * step, step), step)
        grad_ref[rows, :] = hidden_ref[rows, :] + rs.total(grad_ref, rows)

    rs.results(step, handle)
    for c in first + second:
        c.wait_send()
    rs.drain()


def leave(ways, dp_ways, d_qkv, w_all, grad_hidden, tiles):
    count, depth = d_qkv.shape
    rows, width = grad_hidden.shape
    n = 8 if ways == 4 else ways - 1
    m = dp_ways - 1 + ways - 1
    return remote_call(
        functools.partial(leave_kernel, ways, dp_ways),
        (jax.ShapeDtypeStruct((rows, width), F32), jax.ShapeDtypeStruct((8, 128), F32)),
        [ANY, ANY, ANY, VM],
        (VM, VM),
        [pltpu.VMEM((rows, width), F32)]
        + Scatter.buffers(ways, rows, width)
        + sems(n)
        + [
            pltpu.VMEM((dp_ways - 1, ways, 8, 128), F32),
            pltpu.VMEM((ways, 8, 128), F32),
            pltpu.VMEM((ways - 1, 8, 128), F32),
        ]
        + sems(m)
        + Rows.scratch(rows, depth)
        + Right.scratch((width, depth), True)
        + [pltpu.SemaphoreType.DMA((1,))],
        6,
        2 * count * width * depth,
        1_000_000,
    )(d_qkv, w_all, grad_hidden, tiles)


def sigmoid(v):
    return 1.0 / (1.0 + jnp.exp(-v))


def halves(unit, blocks):
    return [
        (slice(2 * j * unit, (2 * j + 1) * unit), slice((2 * j + 1) * unit, (2 * j + 2) * unit)) for j in range(blocks)
    ]


def expand_kernel(
    ways, unit, blocks, src_ref, w_hbm, all_ref, both_ref, act_ref,
    full_ref, w_ref, loaded, out_sem, stage, act_stage, done, send, recv, own_sem,
):
    g = Square(ways)
    load = pltpu.make_async_copy(w_hbm, w_ref, loaded.at[0])
    greet([{"seq": q} for q in g.near()])
    ag = Gather(g, src_ref, full_ref, send, recv, own_sem.at[0])
    ag.start()
    load.start()
    load.wait()
    count = src_ref.shape[0]
    outgoing = []
    tile = unit * blocks
    tiles = w_ref.shape[1] // (2 * tile)

    def results(slot, rows, t):
        wide = pl.ds(pl.multiple_of(t * 2 * tile, 2 * tile), 2 * tile)
        at = pl.ds(pl.multiple_of(t * tile, tile), tile)
        return [
            pltpu.make_async_copy(stage.at[slot], both_ref.at[rows, wide], done.at[slot, 0]),
            pltpu.make_async_copy(act_stage.at[slot], act_ref.at[rows, at], done.at[slot, 1]),
        ]

    half = count // 2
    turns = []

    def part(k, h):
        index = ag.arrive(k, (h,))
        rows = pl.ds(pl.multiple_of(index * count + h * half, half), half)
        turn = len(turns)
        turns.append((k, h))
        outgoing.append(pltpu.make_async_copy(full_ref.at[rows], all_ref.at[rows], out_sem.at[turn]))
        outgoing[-1].start()

        def body(t, carry):
            slot = lax.rem(turn * tiles + t, 2)
            both = dot_nn(full_ref[rows, :], w_ref[:, pl.ds(pl.multiple_of(t * 2 * tile, 2 * tile), 2 * tile)])

            @pl.when(turn * tiles + t >= 2)
            def _():
                for c in results(slot, rows, t):
                    c.wait()

            stage[slot] = both.astype(BF16)
            for j, (first, second) in enumerate(halves(unit, blocks)):
                gate, up = both[:, first], both[:, second]
                value = gate * sigmoid(gate) * up
                act_stage[slot, :, j * unit : (j + 1) * unit] = value.astype(BF16)
            for c in results(slot, rows, t):
                c.start()
            return carry

        lax.fori_loop(0, tiles, body, 0)

    part(0, 0)
    part(0, 1)
    ag.relay()
    for k in range(1, ways - 1, 2):
        for h in range(2):
            for j in (k, k + 1):
                if j < ways - 1:
                    part(j, h)
    part(ways - 1, 0)
    part(ways - 1, 1)
    last = len(turns) * tiles
    for u in range(max(0, last - 2), last):
        for c in results(u % 2, pl.ds(0, half), 0):
            c.wait()
    for c in outgoing:
        c.wait()
    ag.drain()


def blocks_of(units, unit):
    return 2 if (units // unit) % 2 == 0 else 1


def expand(ways, hidden, w_both, unit):
    rows, width = hidden.shape
    units = w_both.shape[1] // 2
    count = ways * rows
    blocks = blocks_of(units, unit)
    tile = unit * blocks
    return remote_call(
        functools.partial(expand_kernel, ways, unit, blocks),
        (
            jax.ShapeDtypeStruct((count, width), BF16),
            jax.ShapeDtypeStruct((count, 2 * units), BF16),
            jax.ShapeDtypeStruct((count, units), BF16),
        ),
        [VM, ANY],
        (ANY,) * 3,
        [
            pltpu.VMEM((count, width), BF16),
            pltpu.VMEM((width, 2 * units), BF16),
            pltpu.SemaphoreType.DMA((1,)),
            pltpu.SemaphoreType.DMA((2 * ways,)),
            pltpu.VMEM((2, rows // 2, 2 * tile), BF16),
            pltpu.VMEM((2, rows // 2, tile), BF16),
            pltpu.SemaphoreType.DMA((2, 2)),
        ]
        + sems(Gather.sems(ways))
        + [pltpu.SemaphoreType.DMA((1,))],
        7,
        4 * count * width * units,
        1_000_000,
    )(hidden, w_both)


def expand_back_kernel(
    ways, unit, blocks, src_ref, w_hbm, act_hbm, both_ref, dboth_ref, down_hbm,
    full, acc, down_ref, w_ref, act_ref, loaded, out_sem, inputs, stage, ready, done, send, recv, own_sem,
):
    g = Square(ways)
    loads = [pltpu.make_async_copy(a, b, loaded.at[j]) for j, (a, b) in enumerate(((w_hbm, w_ref), (act_hbm, act_ref)))]
    greet([{"seq": q} for q in g.near()])
    ag = Gather(g, src_ref, full, send, recv, own_sem.at[0])
    ag.start()
    for c in loads:
        c.start()
    for c in loads:
        c.wait()
    count, width = src_ref.shape
    half = count // 2
    tile = unit * blocks
    units = w_ref.shape[0]
    tiles = units // tile
    wide = tile_of(width, 1024)
    across = width // wide

    def view(ref, rows, t):
        return ref.at[rows, pl.ds(pl.multiple_of(t * 2 * tile, 2 * tile), 2 * tile)]

    turns = []

    def back(k, h):
        index = ag.arrive(k, (h,))
        rows = pl.ds(pl.multiple_of(index * count + h * half, half), half)
        turn = len(turns)
        turns.append((k, h))

        def load(slot, t):
            return pltpu.make_async_copy(view(both_ref, rows, t), inputs.at[slot], ready.at[slot])

        def result(slot, t):
            return pltpu.make_async_copy(stage.at[slot], view(dboth_ref, rows, t), done.at[slot])

        load((turn * tiles) % 2, 0).start()

        def body(t, carry):
            slot = lax.rem(turn * tiles + t, 2)
            at = pl.ds(pl.multiple_of(t * tile, tile), tile)

            @pl.when(t + 1 < tiles)
            def _():
                load(1 - slot, t + 1).start()

            grads = dot_nt(full[rows, :], w_ref[at, :])
            load(slot, t).wait()

            @pl.when(turn * tiles + t >= 2)
            def _():
                result(slot, t).wait()

            for j, (first, second) in enumerate(halves(unit, blocks)):
                grad = grads[:, j * unit : (j + 1) * unit]
                gate = inputs[slot, :, first].astype(F32)
                up = inputs[slot, :, second].astype(F32)
                s = sigmoid(gate)
                part = grad * s
                stage[slot, :, first] = (part * up * (1.0 + gate * (1.0 - s))).astype(BF16)
                stage[slot, :, second] = (part * gate).astype(BF16)
            result(slot, t).start()
            return carry

        lax.fori_loop(0, tiles, body, 0)

    def written(u):
        own = pl.ds(pl.multiple_of(lax.rem(u, tiles) * tile, tile), tile)
        at = pl.ds(pl.multiple_of(u // tiles * wide, wide), wide)
        return pltpu.make_async_copy(down_ref.at[own, at], down_hbm.at[own, at], out_sem.at[u])

    def down(k, first, rows, last=False):
        index = ag.arrive(k, ())
        those = pl.ds(pl.multiple_of(index * count + first, rows), rows)

        def body(u, carry):
            own = pl.ds(pl.multiple_of(lax.rem(u, tiles) * tile, tile), tile)
            at = pl.ds(pl.multiple_of(u // tiles * wide, wide), wide)
            term = dot_tn(act_ref[those, own], full[those, at])
            if k == 0:
                acc[own, at] = term
            elif not last:
                acc[own, at] += term
            else:
                down_ref[own, at] = (acc[own, at] + term).astype(BF16)
                written(u).start()
            return carry

        lax.fori_loop(0, tiles * across, body, 0)

    back(0, 0)
    back(0, 1)
    down(0, 0, count)
    ag.relay((0, 1))
    for k in range(1, ways - 1, 2):
        pair = [j for j in (k, k + 1) if j < ways - 1]
        for h in range(2):
            for j in pair:
                back(j, h)
            if k == 1 and h == 0:
                down(1, 0, half)
                ag.relay((2, 3))
        for j in pair:
            if j == 1:
                down(1, half, half)
            else:
                down(j, 0, count)
    back(ways - 1, 0)
    down(ways - 1, 0, half)
    back(ways - 1, 1)
    down(ways - 1, half, half, last=True)
    last = len(turns) * tiles
    for u in range(max(0, last - 2), last):
        pltpu.make_async_copy(stage.at[u % 2], view(dboth_ref, pl.ds(0, half), 0), done.at[u % 2]).wait()
    for u in range(tiles * across):
        written(u).wait()
    ag.drain()


def expand_back(ways, grad, w_down, act, both, unit):
    rows, width = grad.shape
    count, units = act.shape
    blocks = blocks_of(units, unit)
    tile = unit * blocks
    return remote_call(
        functools.partial(expand_back_kernel, ways, unit, blocks),
        (jax.ShapeDtypeStruct((count, 2 * units), BF16), jax.ShapeDtypeStruct((units, width), BF16)),
        [VM, ANY, ANY, ANY],
        (ANY, ANY),
        [
            pltpu.VMEM((count, width), BF16),
            pltpu.VMEM((units, width), F32),
            pltpu.VMEM((units, width), BF16),
            pltpu.VMEM((units, width), BF16),
            pltpu.VMEM((count, units), BF16),
            pltpu.SemaphoreType.DMA((2,)),
            pltpu.SemaphoreType.DMA((units // tile * (width // tile_of(width, 1024)),)),
            pltpu.VMEM((2, rows // 2, 2 * tile), BF16),
            pltpu.VMEM((2, rows // 2, 2 * tile), BF16),
            pltpu.SemaphoreType.DMA((2,)),
            pltpu.SemaphoreType.DMA((2,)),
        ]
        + sems(Gather.sems(ways))
        + [pltpu.SemaphoreType.DMA((1,))],
        8,
        4 * count * width * units,
        1_000_000,
    )(grad, w_down, act, both)


def attention_back_kernel(
    ways, head_width, lens_ref, src_ref, w_hbm, attn_hbm, q_hbm, k_hbm, v_hbm, qn_hbm, kn_hbm, cos_hbm, sin_hbm,
    lse_ref, stat_ref, gain_ref, out_ref, sums_ref, all_ref,
    attn_ref, q_ref, k_ref, v_ref, qn_ref, kn_ref, cos_ref, sin_ref, fetched, full, acc, w_ref, out_t, loaded, grad, gq, qacc, kacc, vacc, centre, mine, arrived, total,
    send, recv, own_sem, xsend, xrecv,
):
    g = Square(ways)
    load = pltpu.make_async_copy(w_hbm.at[:, pl.ds(3 * w_ref.shape[1], w_ref.shape[1])], w_ref, loaded.at[0])
    load.start()
    greet([{"seq": q} for q in g.everyone()])
    ag = Gather(g, src_ref, full, send, recv, own_sem.at[0])
    ag.start()
    fetches = [
        pltpu.make_async_copy(a, b, fetched.at[j])
        for j, (a, b) in enumerate(
            (
                (attn_hbm, attn_ref), (q_hbm, q_ref), (k_hbm, k_ref), (v_hbm, v_ref),
                (qn_hbm, qn_ref), (kn_hbm, kn_ref), (cos_hbm, cos_ref), (sin_hbm, sin_ref),
            )
        )
    ]
    for c in fetches:
        c.start()
    kacc[...] = jnp.zeros_like(kacc)
    vacc[...] = jnp.zeros_like(vacc)
    mine[...] = jnp.zeros_like(mine)
    count, width = src_ref.shape
    cols = attn_ref.shape[1]
    heads = cols // head_width
    wide = tile_of(width, 1024)
    bounds = bounds_of(lens_ref)
    root = head_width ** (-0.5)
    factor = root * LOG2E
    back = (LONGEST - 1 + count - 1) // count
    load.wait()
    for c in fetches[:4]:
        c.wait()
    for k in range(ways):
        index = ag.arrive(k)
        rows = pl.ds(pl.multiple_of(index * count, count), count)
        grad[...] = dot_nn(full[rows, :], w_ref[...]).astype(BF16)

        def body(u, carry):
            at = pl.ds(pl.multiple_of(u * wide, wide), wide)
            term = dot_tn(full[rows, at], attn_ref[rows, :])
            if k == 0:
                acc[at, :] = term
            elif k < ways - 1:
                acc[at, :] += term
            else:
                out_t[at, :] = (acc[at, :] + term).astype(BF16)
            return carry

        lax.fori_loop(0, width // wide, body, 0)
        slots = index * count + lax.broadcasted_iota(jnp.int32, (1, count), 1)
        begins = first_key(slots, bounds)
        for h in range(heads):
            at = slice(h * head_width, (h + 1) * head_width)
            centre[h : h + 1, :] = row_sums(grad[:, at].astype(F32) * attn_ref[rows, at].astype(F32))
        qacc[...] = jnp.zeros_like(qacc)

        def keys_block(t, carry):
            kb = index - t
            there = pl.ds(pl.multiple_of(kb * count, count), count)
            keys = kb * count + lax.broadcasted_iota(jnp.int32, (count, count), 0)
            visible = (keys <= slots) & (keys >= begins)
            for h in range(heads):
                at = slice(h * head_width, (h + 1) * head_width)
                keys_h, query, grad_h = k_ref[there, at], q_ref[rows, at], grad[:, at]
                scores = dot_nt(keys_h, query) * factor - lse_ref[h : h + 1, rows]
                weights = jnp.where(visible, jnp.exp2(scores), 0.0)
                grad_probs = dot_nt(v_ref[there, at], grad_h)
                grad_scores = (weights * (grad_probs - centre[h : h + 1, :])).astype(BF16)
                vacc[there, at] += dot_nn(weights.astype(BF16), grad_h)
                kacc[there, at] += dot_nn(grad_scores, query)
                qacc[:, at] += dot_tn(grad_scores, keys_h)
            return carry

        lax.fori_loop(0, jnp.minimum(index, back) + 1, keys_block, 0)
        gq[rows, :] = (qacc[...] * root).astype(BF16)
        mine[0:1, rows] = row_sums(gq[rows, :].astype(F32) * q_ref[rows, :].astype(F32))
        if k == 0:
            ag.relay()
    ag.drain()
    written = pltpu.make_async_copy(out_t, all_ref.at[:, pl.ds(3 * cols, cols)], loaded.at[1])
    written.start()

    for c in fetches[4:]:
        c.wait()

    def key_grad(rows, at):
        return (kacc[rows, at] * root).astype(BF16).astype(F32)

    def inner(i, carry):
        rows = pl.ds(pl.multiple_of(i * count, count), count)
        mine[1:2, rows] = row_sums(key_grad(rows, slice(0, cols)) * k_ref[rows, :].astype(F32))
        out_ref[rows, 2 * cols : 3 * cols] = vacc[rows, :].astype(BF16)
        return carry

    lax.fori_loop(0, ways, inner, 0)
    total[...] = exchange_rows(g, mine, arrived, xsend, xrecv)
    sums_ref[...] = jnp.zeros_like(sums_ref)
    small = tile_of(count, 256)

    def finish(i, carry):
        rows = pl.ds(pl.multiple_of(i * small, small), small)
        inverse = lax.rsqrt(as_columns(stat_ref[:, rows]) * (1.0 / width) + NORM_EPS)
        mean = as_columns(total[:, rows]) * (1.0 / width)
        cosine, sine = cos_ref[rows, :], sin_ref[rows, :]
        for part, normed in ((0, qn_ref), (1, kn_ref)):
            scale, middle = inverse[:, part : part + 1], mean[:, part : part + 1]
            for h in range(heads):
                at = slice(h * head_width, (h + 1) * head_width)
                value = gq[rows, at].astype(F32) if part == 0 else key_grad(rows, at)
                e = value * cosine - pltpu.roll(value, head_width // 2, 1) * sine
                unit = normed[rows, at].astype(F32)
                start = pl.multiple_of(g.me * cols + h * head_width, head_width)
                gain = gain_ref[part : part + 1, pl.ds(start, head_width)]
                to = slice(part * cols + h * head_width, part * cols + (h + 1) * head_width)
                out_ref[rows, to] = (scale * (e * gain - unit * middle)).astype(BF16)
                sums_ref[part : part + 1, at] += jnp.sum(e * unit, axis=0, keepdims=True)
        return carry

    lax.fori_loop(0, ways * count // small, finish, 0)
    written.wait()


def attention_back(ways, lens, grad, w_all, attn, q_low, k_low, v_low, qn, kn, lse, stats, gains, cosine, sine):
    rows, width = grad.shape
    count, cols = attn.shape
    head_width = cosine.shape[1]
    return remote_call(
        functools.partial(attention_back_kernel, ways, head_width),
        (
            jax.ShapeDtypeStruct((count, 3 * cols), BF16),
            jax.ShapeDtypeStruct((8, cols), F32),
            jax.ShapeDtypeStruct((width, 4 * cols), BF16),
        ),
        [pl.BlockSpec(memory_space=pltpu.SMEM), VM] + [ANY] * 9 + [VM] * 3,
        (VM, VM, ANY),
        [pltpu.VMEM((count, cols), BF16)] * 6
        + [pltpu.VMEM((count, head_width), F32)] * 2
        + [
            pltpu.SemaphoreType.DMA((8,)),
            pltpu.VMEM((count, width), BF16),
            pltpu.VMEM((width, cols), F32),
            pltpu.VMEM((width, cols), BF16),
            pltpu.VMEM((width, cols), BF16),
            pltpu.SemaphoreType.DMA((2,)),
            pltpu.VMEM((rows, cols), BF16),
            pltpu.VMEM((count, cols), BF16),
            pltpu.VMEM((rows, cols), F32),
            pltpu.VMEM((count, cols), F32),
            pltpu.VMEM((count, cols), F32),
            pltpu.VMEM((8, rows), F32),
            pltpu.VMEM((8, count), F32),
            pltpu.VMEM((ways - 1, 8, count), F32),
            pltpu.VMEM((8, count), F32),
        ]
        + sems(Gather.sems(ways))
        + [pltpu.SemaphoreType.DMA((1,))]
        + sems(ways - 1),
        9,
        4 * count * width * cols,
        1_000_000,
    )(lens, grad, w_all, attn, q_low, k_low, v_low, qn, kn, cosine, sine, lse, stats, gains)


def weight_grads_kernel(x_ref, d_ref, old_ref, out_ref):
    out_ref[...] = dot_tn(x_ref[...], d_ref[...]).astype(BF16)


def weight_grads(x_full, d_qkv, grads):
    count, width = x_full.shape
    depth = d_qkv.shape[1]
    tm, tn = tile_of(width, 512), depth
    return pl.pallas_call(
        weight_grads_kernel,
        out_shape=jax.ShapeDtypeStruct(grads.shape, BF16),
        grid=(width // tm, depth // tn),
        in_specs=[
            pl.BlockSpec((count, tm), lambda i, j: (0, i)),
            pl.BlockSpec((count, tn), lambda i, j: (0, j)),
            ANY,
        ],
        out_specs=pl.BlockSpec((tm, tn), lambda i, j: (i, j)),
        input_output_aliases={2: 0},
        compiler_params=pltpu.CompilerParams(
            dimension_semantics=("arbitrary", "arbitrary"), vmem_limit_bytes=VMEM_BYTES
        ),
        cost_estimate=pl.CostEstimate(flops=0, bytes_accessed=1_000_000, transcendentals=0),
    )(x_full, d_qkv, grads)


def scatter_dp(terms, axis):
    return lax.psum_scatter(terms.astype(BF16), "dp", scatter_dimension=axis, tiled=True)


def gather_dp(weights, axis):
    return lax.all_gather(weights, "dp", axis=axis, tiled=True)


def interleave(gate, up, unit):
    rows = gate.shape[0]
    return jnp.stack([gate.reshape(rows, -1, unit), up.reshape(rows, -1, unit)], axis=2).reshape(rows, -1)


def local(
    layer_in, cotangent, lengths, w_query, w_key, w_value, w_out, w_gate, w_up, w_down,
    gain_query, gain_key, gain_attn, gain_ffn,
):
    rows, width = layer_in.shape
    ways, dp_ways = lax.axis_size("seq"), lax.axis_size("dp")
    count = rows * ways
    head_width = width // HEADS
    cols = width // ways
    part = gain_query.shape[0]
    lens = lengths[0]
    seq_me = lax.axis_index("seq")
    mine = w_gate.shape[1]
    joined = mine % 128 == 0
    unit = mine if joined else tile_of(mine * dp_ways, 256)

    w_all = gather_dp(jnp.concatenate([w_query, w_key, w_value, w_out.T], axis=1), 0)
    if joined:
        w_both = gather_dp(jnp.concatenate([w_gate, w_up], axis=1), 1)
    else:
        w_both = interleave(gather_dp(w_gate, 1), gather_dp(w_up, 1), unit)
    all_down = gather_dp(w_down, 0)

    four = jnp.stack([gain_query, gain_key, gain_attn, gain_ffn]).astype(F32)
    x_full, gain_tiles, cosine, sine = enter(
        ways, dp_ways, lens, layer_in, jnp.pad(four, ((0, 4), (0, 128 - part)))
    )
    gains = gain_tiles[:, :, :4, :part].transpose(2, 1, 0, 3).reshape(4, width)

    q_low, k_low, v_low, qn, kn, stats = project(ways, x_full, w_all, gains, cosine, sine)
    attn, lse = attend(lens, q_low, k_low, v_low, head_width)

    whole = jax.ShapeDtypeStruct((rows, width), F32)
    half = jax.ShapeDtypeStruct((rows, width), BF16)
    eight = jax.ShapeDtypeStruct((8, width), F32)
    hidden, unit_a, inv_a, hidden_low = meet(
        ways, attn, w_all, True, after_attention, (layer_in, gains),
        (whole, half, jax.ShapeDtypeStruct((rows, 128), F32), half), 3, 3 * cols,
    )
    hidden_full, both, act = expand(ways, hidden_low, w_both, unit)
    layer_out, sums_f, grad_m = meet(
        ways, act, all_down, False, after_ffn, (hidden, cotangent, gains), (half, eight, half), 4
    )
    d_both, grad_down = expand_back(ways, grad_m, all_down, act, both, unit)
    out_down = scatter_dp(grad_down, 0)
    grad_both = dot_tn(hidden_full, d_both).astype(BF16)
    d_both, grad_both = lax.optimization_barrier((d_both, grad_both))
    if joined:
        out_both = [scatter_dp(grad_both, 1)]
    else:
        pieces = grad_both.reshape(width, -1, 2, unit)
        out_both = [scatter_dp(pieces[:, :, j].reshape(width, -1), 1) for j in range(2)]
    grad_hidden, sums_a, grad_a = meet(
        ways, d_both, w_both, True, before_ffn, (cotangent, unit_a, inv_a, gains), (whole, eight, half), 5
    )
    grad_a, out_down = lax.optimization_barrier((grad_a, out_down))
    d_qkv, sums_qk, grad_all = attention_back(
        ways, lens, grad_a, w_all, attn, q_low, k_low, v_low, qn, kn, lse, stats, gains, cosine, sine
    )
    grad_all = weight_grads(x_full, d_qkv, grad_all)
    d_qkv, grad_all, out_both = lax.optimization_barrier((d_qkv, grad_all, out_both))
    out_all = scatter_dp(grad_all, 0).astype(F32)
    out_gate, out_up = (out_both[0][:, :mine], out_both[0][:, mine:]) if joined else out_both

    own = lax.dynamic_update_slice(jnp.zeros((2, width), F32), sums_qk[:2], (0, seq_me * cols))
    norms = jnp.stack([jnp.sum(sums_a, axis=0), jnp.sum(sums_f, axis=0)])
    tiles = jnp.concatenate([own, norms]).reshape(4, dp_ways, ways, part).transpose(1, 2, 0, 3)
    tiles = jnp.pad(tiles, ((0, 0), (0, 0), (0, 4), (0, 128 - part)))
    grad_in, gain_sums = leave(ways, dp_ways, d_qkv, w_all, grad_hidden, tiles)
    return (
        layer_out,
        grad_in,
        out_all[:, :cols],
        out_all[:, cols : 2 * cols],
        out_all[:, 2 * cols : 3 * cols],
        out_all[:, 3 * cols :].T,
        out_gate.astype(F32),
        out_up.astype(F32),
        out_down.astype(F32),
        gain_sums[0, :part],
        gain_sums[1, :part],
        gain_sums[2, :part],
        gain_sums[3, :part],
    )


def solution(mesh):
    both = P(("dp", "seq"))
    rows = P(("dp", "seq"), None)
    columns = P(None, ("dp", "seq"))
    square = P("dp", "seq")
    in_specs = (
        rows, rows, P("dp", None), square, square, square, P("seq", "dp"), columns, columns, rows, both, both, both, both,
    )
    out_specs = (
        rows, rows, square, square, square, P("seq", "dp"), columns, columns, rows, both, both, both, both,
    )
    return jax.shard_map(local, mesh=mesh, in_specs=in_specs, out_specs=out_specs, check_vma=False)
```

```python
import functools
import math

import jax
import jax.numpy as jnp
from jax import lax
from jax.experimental import pallas as pl
from jax.experimental.pallas import tpu as pltpu
from jax.sharding import PartitionSpec as P

HEADS = 16
NORM_EPS = 1e-06
ROPE_BASE = 500000.0
MASKED = -1e30
LONGEST = 1024
LOG2E = 1.4426950408889634

F32 = jnp.float32
BF16 = jnp.bfloat16
MESH = pl.DeviceIdType.MESH
VMEM_BYTES = 60 * 1024 * 1024
ANY = pl.BlockSpec(memory_space=pl.ANY)
VM = pl.BlockSpec(memory_space=pltpu.VMEM)


def dot_nn(a, b):
    return lax.dot_general(a, b, (((1,), (0,)), ((), ())), preferred_element_type=F32)


def dot_nt(a, b):
    return lax.dot_general(a, b, (((1,), (1,)), ((), ())), preferred_element_type=F32)


def dot_tn(a, b):
    return lax.dot_general(a, b, (((0,), (0,)), ((), ())), preferred_element_type=F32)


def row_sums(values):
    folded = values[:, 0:128]
    for k in range(1, values.shape[1] // 128):
        folded = folded + values[:, k * 128 : (k + 1) * 128]
    return jnp.sum(jnp.transpose(folded), axis=0, keepdims=True)


def as_columns(rows8):
    return jnp.transpose(jnp.concatenate([rows8] * 16, axis=0))


def tile_of(extent, most):
    return most if extent % most == 0 else extent


def bounds_of(lens_ref):
    first = lens_ref[0]
    second = first + lens_ref[1]
    return first, second, second + lens_ref[2]


def first_key(slot, bounds):
    a, b, c = bounds
    return jnp.where(slot < a, 0, jnp.where(slot < b, a, jnp.where(slot < c, b, slot)))


class Square:
    def __init__(self, ways):
        self.ways = ways
        self.me = lax.axis_index("seq")
        self.square = ways == 4
        if self.square:
            self.x = self.me + 1 - 2 * lax.rem(self.me, 2)
            self.y = lax.rem(self.me + 2, 4)
            self.d = 3 - self.me

    def peer(self, p):
        return lax.rem(self.me + p, self.ways)

    def near(self):
        if self.square:
            return [self.x, self.y]
        return [self.peer(p) for p in range(1, self.ways)]

    def everyone(self):
        return [self.peer(p) for p in range(1, self.ways)]

    def order(self):
        if self.square:
            return [self.d, self.x, self.y, self.me]
        return self.everyone() + [self.me]


def greet(devices):
    barrier = pltpu.get_barrier_semaphore()
    for device in devices:
        pl.semaphore_signal(barrier, inc=1, device_id=device, device_id_type=MESH)
    pl.semaphore_wait(barrier, len(devices))


def to_seq(src, dst, send, recv, peer):
    return pltpu.make_async_remote_copy(
        src_ref=src, dst_ref=dst, send_sem=send, recv_sem=recv, device_id={"seq": peer}, device_id_type=MESH
    )


def to_dp(src, dst, send, recv, peer):
    return pltpu.make_async_remote_copy(
        src_ref=src, dst_ref=dst, send_sem=send, recv_sem=recv, device_id={"dp": peer}, device_id_type=MESH
    )


class Gather:
    def __init__(self, group, src, full, send, recv, own_sem):
        self.g, self.src, self.full, self.send, self.recv = group, src, full, send, recv
        self.rows = src.shape[0]
        self.own = pltpu.make_async_copy(src, self.chunk(group.me), own_sem)
        self.seen = set()
        self.turned = {}

    @staticmethod
    def sems(ways):
        return 12 if ways == 4 else ways - 1

    def chunk(self, index):
        return self.full.at[pl.ds(index * self.rows, self.rows)]

    def quarter(self, index, which):
        h = self.rows // 4
        return self.full.at[pl.ds(index * self.rows + which * h, h)]

    def cp(self, k, src, dst, peer):
        return to_seq(src, dst, self.send.at[k], self.recv.at[k], peer)

    def start(self):
        g, h = self.g, self.rows // 4
        if g.square:
            parts = [self.src.at[pl.ds(j * h, h)] for j in range(4)]
            self.over_x = {j: self.cp(k, parts[j], self.quarter(g.me, j), g.x) for k, j in enumerate((0, 1, 2, 3))}
            self.over_y = {j: self.cp(4 + k, parts[j], self.quarter(g.me, j), g.y) for k, j in enumerate((1, 0, 3, 2))}
            for j, k in ((0, 1), (1, 0), (2, 3), (3, 2)):
                self.over_x[j].start()
                self.over_y[k].start()
        else:
            self.first = [self.cp(p - 1, self.src, self.chunk(g.me), g.peer(p)) for p in range(1, g.ways)]
            for c in self.first:
                c.start()
        self.own.start()

    def relay(self, quarters=(0, 1, 2, 3)):
        g = self.g
        if not g.square:
            return
        for j in quarters:
            here, there, copy = (g.x, g.y, self.over_x[j]) if j % 2 == 0 else (g.y, g.x, self.over_y[j])
            copy.wait_recv()
            self.turned[j] = self.cp(8 + j, self.quarter(here, j), self.quarter(here, j), there)
            self.turned[j].start()

    def arrive(self, k, halves=(0, 1)):
        g = self.g
        halves = [h for h in halves if (k, h) not in self.seen]
        self.seen.update((k, h) for h in halves)
        if k == 0:
            if 0 in halves:
                self.own.wait()
            return g.me
        if not g.square:
            if 0 in halves:
                self.first[k - 1].wait_recv()
            return lax.rem(g.me + g.ways - k, g.ways)
        for h in halves:
            if k == 1:
                self.over_x[2 * h + 1].wait_recv()
            elif k == 2:
                self.over_y[2 * h].wait_recv()
            else:
                self.turned[2 * h].wait_recv()
                self.turned[2 * h + 1].wait_recv()
        return (g.x, g.y, g.d)[k - 1]

    def drain(self):
        if self.g.square:
            for copies in (self.over_x, self.over_y, self.turned):
                for j in range(4):
                    copies[j].wait_send()
        else:
            for c in self.first:
                c.wait_send()


class Scatter:
    @staticmethod
    def buffers(ways, rows, width):
        if ways == 4:
            return [
                pltpu.VMEM((3, rows, width), BF16),
                pltpu.VMEM((2, rows, width), BF16),
                pltpu.VMEM((2, rows // 2, width), BF16),
            ]
        return [
            pltpu.VMEM((ways - 1, rows, width), BF16),
            pltpu.VMEM((ways - 1, rows, width), BF16),
            pltpu.VMEM((2, 16, width), BF16),
        ]

    def __init__(self, group, out, arrived, relayed, send, recv):
        self.g, self.out, self.arrived, self.relayed, self.send, self.recv = group, out, arrived, relayed, send, recv
        self.rows = out.shape[1]

    def cp(self, k, src, dst, peer):
        return to_seq(src, dst, self.send.at[k], self.recv.at[k], peer)

    def run(self, left, right, own):
        g, h = self.g, self.rows // 2
        out, arrived, relayed = self.out, self.arrived, self.relayed
        left.copy(1).start()
        if not g.square:
            self.sent = []
            for p in range(1, g.ways):
                right.product(left.get(p - 1), out.at[p - 1], BF16)
                if p + 1 < g.ways:
                    left.copy(p + 1).start()
                c = self.cp(p - 1, out.at[p - 1], arrived.at[p - 1], g.peer(p))
                c.start()
                self.sent.append(c)
            right.product(left.get(g.ways - 1), own, F32)
            return
        top, low = pl.ds(0, h), pl.ds(h, h)
        right.product(left.get(0, top), out.at[2, top], BF16)
        c0 = self.cp(0, out.at[2, top], relayed.at[0], g.x)
        c0.start()
        right.product(left.get(0, low), out.at[2, low], BF16)
        c1 = self.cp(1, out.at[2, low], relayed.at[1], g.y)
        c1.start()
        left.copy(2).start()
        right.product(left.get(1, top), out.at[0, top], BF16)
        c2 = self.cp(2, out.at[0, top], arrived.at[0, top], g.x)
        c2.start()
        right.product(left.get(2, low), out.at[1, low], BF16)
        c3 = self.cp(3, out.at[1, low], arrived.at[1, low], g.y)
        c3.start()
        right.product(left.get(1, low), out.at[0, low], BF16)
        left.copy(3).start()
        right.product(left.get(2, top), out.at[1, top], BF16)
        self.sent = [c0, c1, c2, c3]
        self.relay()
        right.product(left.get(3), own, F32)

    def relay(self):
        g, h = self.g, self.rows // 4
        out, arrived, relayed = self.out, self.arrived, self.relayed
        c0, c1, c2, c3 = self.sent
        step = tile_of(h, 64)

        def add(slot, base, which, offset):
            def body(t, carry):
                rows = pl.ds(base + t * step, step)
                have = out[slot, rows, :].astype(F32)
                more = relayed[which, pl.ds(offset + t * step, step), :].astype(F32)
                out[slot, rows, :] = (have + more).astype(BF16)
                return carry

            lax.fori_loop(0, h // step, body, 0)

        c1.wait_recv()
        self.last = [[], []]
        for j in range(2):
            add(0, 2 * h + j * h, 1, j * h)
            rows = pl.ds((2 + j) * h, h)
            c = self.cp(4 + j, out.at[0, rows], arrived.at[0, rows], g.x)
            c.start()
            self.last[j].append(c)
            if j == 0:
                c0.wait_recv()
            add(1, j * h, 0, j * h)
            rows = pl.ds(j * h, h)
            c = self.cp(6 + j, out.at[1, rows], arrived.at[1, rows], g.y)
            c.start()
            self.last[j].append(c)

    def results(self, step, handle, early=True):
        count = self.rows // step

        def run(first, n):
            def body(t, carry):
                handle(first + t)
                return carry

            lax.fori_loop(0, n, body, 0)

        if not early or not self.g.square or count % 4:
            self.finish()
            run(0, count)
            return
        for c in self.sent[2:]:
            c.wait_recv()
        for j in range(2):
            for c in self.last[j]:
                c.wait_recv()
            run(j * (count // 4), count // 4)
            run((2 + j) * (count // 4), count // 4)

    def finish(self):
        if self.g.square:
            for c in self.sent[2:] + self.last[0] + self.last[1]:
                c.wait_recv()
        else:
            for c in self.sent:
                c.wait_recv()

    def drain(self):
        for c in self.sent + (self.last[0] + self.last[1] if self.g.square else []):
            c.wait_send()

    def total(self, own, rows):
        value = own[rows, :]
        for k in range(self.arrived.shape[0]):
            value = value + self.arrived[k, rows, :].astype(F32)
        return value


def remote_call(kernel, outs, in_specs, out_specs, scratch, collective_id, flops, nbytes):
    return pl.pallas_call(
        kernel,
        out_shape=outs,
        in_specs=in_specs,
        out_specs=out_specs,
        scratch_shapes=scratch,
        compiler_params=pltpu.CompilerParams(
            collective_id=collective_id, has_side_effects=True, vmem_limit_bytes=VMEM_BYTES
        ),
        cost_estimate=pl.CostEstimate(flops=0, bytes_accessed=nbytes, transcendentals=0),
    )


def sems(n):
    return [pltpu.SemaphoreType.DMA((n,)), pltpu.SemaphoreType.DMA((n,))]


def write_tables(lens_ref, cos_ref, sin_ref):
    count, head_width = cos_ref.shape
    half = head_width // 2
    step = tile_of(count, 256)
    bounds = bounds_of(lens_ref)
    lane = lax.broadcasted_iota(jnp.int32, (1, head_width), 1)
    folded = jnp.where(lane < half, lane, lane - half).astype(F32)
    frequency = jnp.exp(folded * (-2.0 / head_width * math.log(ROPE_BASE)))
    sign = jnp.where(lane < half, -1.0, 1.0)

    def body(t, carry):
        rows = pl.ds(pl.multiple_of(t * step, step), step)
        slots = t * step + lax.broadcasted_iota(jnp.int32, (step, head_width), 0)
        a, b, c = bounds
        begin = jnp.where(slots < a, 0, jnp.where(slots < b, a, jnp.where(slots < c, b, c)))
        angles = (slots - begin).astype(F32) * frequency
        cos_ref[rows, :] = jnp.cos(angles)
        sin_ref[rows, :] = jnp.sin(angles) * sign
        return carry

    lax.fori_loop(0, count // step, body, 0)


def enter_kernel(
    ways, dp_ways, lens_ref, x_ref, gain_ref, full_ref, gains_ref, cos_ref, sin_ref,
    send, recv, own_sem, gsend, grecv,
):
    g = Square(ways)
    dp_me = lax.axis_index("dp")
    dp_peers = [lax.rem(dp_me + p, dp_ways) for p in range(1, dp_ways)]
    greet([{"seq": q} for q in g.everyone()] + [{"dp": p} for p in dp_peers])
    ag = Gather(g, x_ref, full_ref, send, recv, own_sem.at[0])
    ag.start()

    gains_ref[g.me, dp_me] = gain_ref[...]
    first = [
        to_dp(gain_ref, gains_ref.at[g.me, dp_me], gsend.at[k], grecv.at[k], p) for k, p in enumerate(dp_peers)
    ]
    for c in first:
        c.start()
    write_tables(lens_ref, cos_ref, sin_ref)
    for c in first:
        c.wait_recv()
    base = dp_ways - 1
    second = [
        to_seq(gains_ref.at[g.me], gains_ref.at[g.me], gsend.at[base + k], grecv.at[base + k], q)
        for k, q in enumerate(g.everyone())
    ]
    for c in second:
        c.start()
    ag.relay()
    for c in second:
        c.wait_recv()
    for c in first + second:
        c.wait_send()
    for k in range(ways):
        ag.arrive(k)
    ag.drain()


def enter(ways, dp_ways, lens, x, gains):
    rows, width = x.shape
    count, head_width = ways * rows, width // HEADS
    table = jax.ShapeDtypeStruct((count, head_width), F32)
    return remote_call(
        functools.partial(enter_kernel, ways, dp_ways),
        (
            jax.ShapeDtypeStruct((count, width), BF16),
            jax.ShapeDtypeStruct((ways, dp_ways, 8, 128), F32),
            table,
            table,
        ),
        [pl.BlockSpec(memory_space=pltpu.SMEM), ANY, VM],
        (ANY, VM, VM, VM),
        sems(Gather.sems(ways))
        + [pltpu.SemaphoreType.DMA((1,))]
        + sems(dp_ways - 1 + ways - 1),
        0,
        0,
        1_000_000,
    )(lens, x, gains)


def exchange_rows(g, mine, arrived, send, recv):
    copies = [
        to_seq(mine, arrived.at[k], send.at[k], recv.at[k], q) for k, q in enumerate(g.everyone())
    ]
    for c in copies:
        c.start()
    for c in copies:
        c.wait_recv()
    total = mine[...]
    for k in range(g.ways - 1):
        total = total + arrived[k]
    for c in copies:
        c.wait_send()
    return total


def project_kernel(
    ways, x_ref, w_ref, gain_ref, cos_ref, sin_ref, q_ref, k_ref, v_ref, qn_ref, kn_ref, stat_ref,
    qf, kf, mine, arrived, send, recv, buffer, ready,
):
    g = Square(ways)
    count, width = x_ref.shape
    cols = q_ref.shape[1]
    step = buffer.shape[1]
    steps = count // step

    def fetch(i, slot):
        rows = pl.ds(pl.multiple_of(i * step, step), step)
        return pltpu.make_async_copy(x_ref.at[rows], buffer.at[slot], ready.at[slot])

    fetch(0, 0).start()
    greet([{"seq": q} for q in g.everyone()])
    mine[...] = jnp.zeros_like(mine)

    def project(i, carry):
        slot = lax.rem(i, 2)

        @pl.when(i + 1 < steps)
        def _():
            fetch(i + 1, 1 - slot).start()

        fetch(i, slot).wait()
        rows = pl.ds(pl.multiple_of(i * step, step), step)
        xs = buffer[slot]
        for part, ref in ((0, qf), (1, kf)):
            value = dot_nn(xs, w_ref[:, part * cols : (part + 1) * cols])
            ref[rows, :] = value
            mine[part : part + 1, rows] = row_sums(value * value)
        v_ref[rows, :] = dot_nn(xs, w_ref[:, 2 * cols : 3 * cols]).astype(BF16)
        return carry

    lax.fori_loop(0, steps, project, 0)
    stat_ref[...] = exchange_rows(g, mine, arrived, send, recv)
    small = tile_of(count, 256)

    def finish(i, carry):
        rows = pl.ds(pl.multiple_of(i * small, small), small)
        inverse = lax.rsqrt(as_columns(stat_ref[:, rows]) * (1.0 / width) + NORM_EPS)
        cosine, sine = cos_ref[rows, :], sin_ref[rows, :]
        for part, src, normed, out in ((0, qf, qn_ref, q_ref), (1, kf, kn_ref, k_ref)):
            scale = inverse[:, part : part + 1]
            for h in range(cols // 128):
                at = slice(h * 128, (h + 1) * 128)
                unit = src[rows, at] * scale
                normed[rows, at] = unit.astype(BF16)
                start = pl.multiple_of(g.me * cols + h * 128, 128)
                value = unit * gain_ref[part : part + 1, pl.ds(start, 128)]
                out[rows, at] = (value * cosine + pltpu.roll(value, 64, 1) * sine).astype(BF16)
        return carry

    lax.fori_loop(0, count // small, finish, 0)


def project(ways, x_full, w_all, gains, cosine, sine):
    count, width = x_full.shape
    cols = w_all.shape[1] // 4
    step = tile_of(count, 512)
    low = jax.ShapeDtypeStruct((count, cols), BF16)
    return remote_call(
        functools.partial(project_kernel, ways),
        (low, low, low, low, low, jax.ShapeDtypeStruct((8, count), F32)),
        [ANY, VM, VM, VM, VM],
        (VM,) * 6,
        [
            pltpu.VMEM((count, cols), F32),
            pltpu.VMEM((count, cols), F32),
            pltpu.VMEM((8, count), F32),
            pltpu.VMEM((ways - 1, 8, count), F32),
        ]
        + sems(ways - 1)
        + [pltpu.VMEM((2, step, width), BF16), pltpu.SemaphoreType.DMA((2,))],
        1,
        2 * count * width * 3 * cols,
        1_000_000,
    )(x_full, w_all, gains, cosine, sine)


def attend_kernel(head_width, lens_ref, q_ref, k_ref, v_ref, o_ref, lse_ref, acc, top, tot):
    block, cols = q_ref.shape
    heads = cols // head_width
    i = pl.program_id(0)
    bounds = bounds_of(lens_ref)
    slots = i * block + lax.broadcasted_iota(jnp.int32, (1, block), 1)
    begins = first_key(slots, bounds)
    factor = head_width ** (-0.5) * LOG2E

    def scores_of(kb, h):
        at = slice(h * head_width, (h + 1) * head_width)
        rows = pl.ds(pl.multiple_of(kb * block, block), block)
        keys = kb * block + lax.broadcasted_iota(jnp.int32, (block, block), 0)
        visible = (keys <= slots) & (keys >= begins)
        scores = dot_nt(k_ref[rows, at], q_ref[:, at]) * factor
        return jnp.where(visible, scores, MASKED), v_ref[rows, at], at

    for h in range(heads):
        scores, values, at = scores_of(i, h)
        largest = jnp.max(scores, axis=0, keepdims=True)
        weights = jnp.exp2(scores - largest)
        top[h : h + 1, :] = largest
        tot[h : h + 1, :] = jnp.sum(weights, axis=0, keepdims=True)
        acc[at, :] = dot_tn(values, weights.astype(BF16))

    def earlier(t, carry):
        kb = i - 1 - t
        for h in range(heads):
            scores, values, at = scores_of(kb, h)
            before = top[h : h + 1, :]
            largest = jnp.maximum(before, jnp.max(scores, axis=0, keepdims=True))
            weights = jnp.exp2(scores - largest)
            shrink = jnp.exp2(before - largest)
            top[h : h + 1, :] = largest
            tot[h : h + 1, :] = tot[h : h + 1, :] * shrink + jnp.sum(weights, axis=0, keepdims=True)
            acc[at, :] = acc[at, :] * shrink + dot_tn(values, weights.astype(BF16))
        return carry

    lowest = first_key(i * block, bounds) // block
    lax.fori_loop(0, i - lowest, earlier, 0)
    lse_ref[...] = jnp.zeros_like(lse_ref)
    for h in range(heads):
        at = slice(h * head_width, (h + 1) * head_width)
        total = tot[h : h + 1, :]
        o_ref[:, at] = jnp.transpose(acc[at, :] * (1.0 / total)).astype(BF16)
        lse_ref[h : h + 1, :] = top[h : h + 1, :] + jnp.log2(total)


def attend(lens, q_low, k_low, v_low, head_width):
    count, cols = q_low.shape
    block = tile_of(count, 512)
    tile = pl.BlockSpec((block, cols), lambda i, lens: (i, 0))
    whole = pl.BlockSpec((count, cols), lambda i, lens: (0, 0))
    line = pl.BlockSpec((8, block), lambda i, lens: (0, i))
    return pl.pallas_call(
        functools.partial(attend_kernel, head_width),
        out_shape=(jax.ShapeDtypeStruct((count, cols), BF16), jax.ShapeDtypeStruct((8, count), F32)),
        grid_spec=pltpu.PrefetchScalarGridSpec(
            num_scalar_prefetch=1,
            grid=(count // block,),
            in_specs=[tile, whole, whole],
            out_specs=(tile, line),
            scratch_shapes=[pltpu.VMEM((cols, block), F32), pltpu.VMEM((8, block), F32), pltpu.VMEM((8, block), F32)],
        ),
        compiler_params=pltpu.CompilerParams(dimension_semantics=("arbitrary",), vmem_limit_bytes=VMEM_BYTES),
        cost_estimate=pl.CostEstimate(flops=0, bytes_accessed=1_000_000, transcendentals=0),
    )(lens, q_low, k_low, v_low)


class Right:
    def __init__(self, src, ref, loaded, transposed, first_column):
        self.ref, self.transposed, self.loaded = ref, transposed, loaded
        self.width = ref.shape[0] if transposed else ref.shape[1]
        self.tile = self.width // self.tiles(self.width)
        self.src = src.at[:, pl.ds(first_column, ref.shape[1])] if transposed else src
        self.fresh = True

    @staticmethod
    def tiles(width):
        return width // tile_of(width, 512)

    @staticmethod
    def scratch(shape, transposed):
        width = shape[0] if transposed else shape[1]
        return [pltpu.VMEM(shape, BF16), pltpu.SemaphoreType.DMA((Right.tiles(width),))]

    def copy(self, t):
        at = pl.ds(pl.multiple_of(t * self.tile, self.tile), self.tile)
        if self.transposed:
            return pltpu.make_async_copy(self.src.at[at], self.ref.at[at], self.loaded.at[t])
        return pltpu.make_async_copy(self.src.at[:, at], self.ref.at[:, at], self.loaded.at[t])

    def start(self):
        for t in range(self.width // self.tile):
            self.copy(t).start()

    def product(self, lhs, out, dtype):
        fresh, self.fresh = self.fresh, False

        def body(t, carry):
            at = pl.ds(pl.multiple_of(t * self.tile, self.tile), self.tile)
            if fresh:
                self.copy(t).wait()
            value = dot_nt(lhs[...], self.ref[at, :]) if self.transposed else dot_nn(lhs[...], self.ref[:, at])
            out[:, at] = value.astype(dtype)
            return carry

        lax.fori_loop(0, self.width // self.tile, body, 0)


class Rows:
    def __init__(self, order, ref, buffer, ready):
        self.order, self.ref, self.buffer, self.ready = order, ref, buffer, ready
        self.waited = set()

    @staticmethod
    def scratch(rows, depth):
        return [pltpu.VMEM((2, rows, depth), BF16), pltpu.SemaphoreType.DMA((2,))]

    def copy(self, turn):
        count = self.buffer.shape[1]
        rows = pl.ds(pl.multiple_of(self.order[turn] * count, count), count)
        return pltpu.make_async_copy(self.ref.at[rows], self.buffer.at[turn % 2], self.ready.at[turn % 2])

    def get(self, turn, part=None):
        if turn not in self.waited:
            self.copy(turn).wait()
            self.waited.add(turn)
        return self.buffer.at[turn % 2] if part is None else self.buffer.at[turn % 2, part]


def fold8(value):
    return jnp.sum(value.reshape(value.shape[0] // 8, 8, value.shape[1]), axis=0)


def meet_kernel(ways, transposed, first_column, epilogue, n_extra, n_out, own_is_out, lhs, rhs, *refs):
    sources, outs, scratch = refs[:n_extra], refs[n_extra : n_extra + n_out], refs[n_extra + n_out :]
    own = outs[0] if own_is_out else scratch[0]
    scratch = scratch if own_is_out else scratch[1:]
    out, arrived, relayed, send, recv, buffer, ready, w_ref, loaded, fetched = scratch[:10]
    extra = scratch[10:]
    g = Square(ways)
    left = Rows(g.order(), lhs, buffer, ready)
    right = Right(rhs, w_ref, loaded, transposed, first_column)
    left.copy(0).start()
    right.start()
    fetches = [pltpu.make_async_copy(a, b, fetched.at[j]) for j, (a, b) in enumerate(zip(sources, extra))]
    greet([{"seq": q} for q in g.near()])
    count = own.shape[0]
    rs = Scatter(g, out, arrived, relayed, send, recv)
    for c in fetches:
        c.start()
    rs.run(left, right, own)
    for c in fetches:
        c.wait()
    step = tile_of(count, 64)

    def handle(t):
        rows = pl.ds(pl.multiple_of(t * step, step), step)
        epilogue(rows, rs.total(own, rows), extra, outs, t)

    rs.results(step, handle, transposed)
    rs.drain()


def meet(ways, lhs, rhs, transposed, epilogue, extra, outs, collective_id, first_column=0):
    count, depth = lhs.shape
    width = rhs.shape[0] if transposed else rhs.shape[1]
    rows = count // ways
    n = 8 if ways == 4 else ways - 1
    own_is_out = outs[0].dtype == F32
    scratch = [] if own_is_out else [pltpu.VMEM((rows, width), F32)]
    scratch += Scatter.buffers(ways, rows, width) + sems(n) + Rows.scratch(rows, depth)
    scratch += Right.scratch((width, depth) if transposed else (depth, width), transposed)
    scratch += [pltpu.SemaphoreType.DMA((len(extra),))] + [pltpu.VMEM(e.shape, e.dtype) for e in extra]
    return remote_call(
        functools.partial(meet_kernel, ways, transposed, first_column, epilogue, len(extra), len(outs), own_is_out),
        tuple(outs),
        [ANY] * (2 + len(extra)),
        (VM,) * len(outs),
        scratch,
        collective_id,
        2 * count * width * depth,
        1_000_000,
    )(lhs, rhs, *extra)


def after_attention(rows, branch, extra, outs, t):
    x_ref, gain_ref = extra
    hidden_ref, unit_ref, inv_ref, source = outs
    inverse = lax.rsqrt(jnp.mean(branch * branch, axis=1, keepdims=True) + NORM_EPS)
    unit = branch * inverse
    hidden = x_ref[rows, :].astype(F32) + unit * gain_ref[2:3, :]
    hidden_ref[rows, :] = hidden
    unit_ref[rows, :] = unit.astype(BF16)
    inv_ref[rows, :] = jnp.broadcast_to(inverse, (inverse.shape[0], 128))
    source[rows, :] = hidden.astype(BF16)


def after_ffn(rows, branch, extra, outs, t):
    hidden_ref, cot_ref, gain_ref = extra
    out_ref, sums_ref, source = outs
    gain = gain_ref[3:4, :]
    inverse = lax.rsqrt(jnp.mean(branch * branch, axis=1, keepdims=True) + NORM_EPS)
    unit = branch * inverse
    out_ref[rows, :] = (hidden_ref[rows, :] + unit * gain).astype(BF16)
    e = cot_ref[rows, :].astype(F32)
    term = fold8(e * unit)

    @pl.when(t == 0)
    def _():
        sums_ref[...] = term

    @pl.when(t > 0)
    def _():
        sums_ref[...] += term

    eg = e * gain
    mean = jnp.mean(eg * unit, axis=1, keepdims=True)
    source[rows, :] = (inverse * (eg - unit * mean)).astype(BF16)


def before_ffn(rows, terms, extra, outs, t):
    cot_ref, unit_ref, inv_ref, gain_ref = extra
    hidden_ref, sums_ref, source = outs
    e = cot_ref[rows, :].astype(F32) + terms
    hidden_ref[rows, :] = e
    unit = unit_ref[rows, :].astype(F32)
    term = fold8(e * unit)

    @pl.when(t == 0)
    def _():
        sums_ref[...] = term

    @pl.when(t > 0)
    def _():
        sums_ref[...] += term

    eg = e * gain_ref[2:3, :]
    mean = jnp.mean(eg * unit, axis=1, keepdims=True)
    source[rows, :] = (inv_ref[rows, 0:1] * (eg - unit * mean)).astype(BF16)


def leave_kernel(
    ways, dp_ways, d_ref, w_hbm, hidden_hbm, tiles_ref, grad_ref, gains_ref,
    hidden_ref, out, arrived, relayed, send, recv, from_dp, partial, from_seq, gsend, grecv, buffer, ready,
    w_ref, loaded, fetched,
):
    g = Square(ways)
    left = Rows(g.order(), d_ref, buffer, ready)
    right = Right(w_hbm, w_ref, loaded, True, 0)
    left.copy(0).start()
    right.start()
    fetch = pltpu.make_async_copy(hidden_hbm, hidden_ref, fetched.at[0])
    dp_me = lax.axis_index("dp")
    dp_peers = [lax.rem(dp_me + p, dp_ways) for p in range(1, dp_ways)]
    greet([{"seq": q} for q in g.everyone()] + [{"dp": p} for p in dp_peers])
    first = [
        to_dp(tiles_ref.at[p], from_dp.at[k], gsend.at[k], grecv.at[k], p) for k, p in enumerate(dp_peers)
    ]
    for c in first:
        c.start()
    fetch.start()
    count = grad_ref.shape[0]
    rs = Scatter(g, out, arrived, relayed, send, recv)
    rs.run(left, right, grad_ref)
    for c in first:
        c.wait_recv()
    value = tiles_ref[dp_me]
    for k in range(dp_ways - 1):
        value = value + from_dp[k]
    partial[...] = value
    base = dp_ways - 1
    second = [
        to_seq(partial.at[q], from_seq.at[k], gsend.at[base + k], grecv.at[base + k], q)
        for k, q in enumerate(g.everyone())
    ]
    for c in second:
        c.start()
    for c in second:
        c.wait_recv()
    value = partial[g.me]
    for k in range(ways - 1):
        value = value + from_seq[k]
    gains_ref[...] = value
    fetch.wait()
    step = tile_of(count, 64)

    def handle(t):
        rows = pl.ds(pl.multiple_of(t * step, step), step)
        grad_ref[rows, :] = hidden_ref[rows, :] + rs.total(grad_ref, rows)

    rs.results(step, handle)
    for c in first + second:
        c.wait_send()
    rs.drain()


def leave(ways, dp_ways, d_qkv, w_all, grad_hidden, tiles):
    count, depth = d_qkv.shape
    rows, width = grad_hidden.shape
    n = 8 if ways == 4 else ways - 1
    m = dp_ways - 1 + ways - 1
    return remote_call(
        functools.partial(leave_kernel, ways, dp_ways),
        (jax.ShapeDtypeStruct((rows, width), F32), jax.ShapeDtypeStruct((8, 128), F32)),
        [ANY, ANY, ANY, VM],
        (VM, VM),
        [pltpu.VMEM((rows, width), F32)]
        + Scatter.buffers(ways, rows, width)
        + sems(n)
        + [
            pltpu.VMEM((dp_ways - 1, ways, 8, 128), F32),
            pltpu.VMEM((ways, 8, 128), F32),
            pltpu.VMEM((ways - 1, 8, 128), F32),
        ]
        + sems(m)
        + Rows.scratch(rows, depth)
        + Right.scratch((width, depth), True)
        + [pltpu.SemaphoreType.DMA((1,))],
        6,
        2 * count * width * depth,
        1_000_000,
    )(d_qkv, w_all, grad_hidden, tiles)


def sigmoid(v):
    return 1.0 / (1.0 + jnp.exp(-v))


def halves(unit, blocks):
    return [
        (slice(2 * j * unit, (2 * j + 1) * unit), slice((2 * j + 1) * unit, (2 * j + 2) * unit)) for j in range(blocks)
    ]


def expand_kernel(
    ways, unit, blocks, src_ref, w_hbm, all_ref, both_ref, act_ref,
    full_ref, w_ref, loaded, out_sem, stage, act_stage, done, send, recv, own_sem,
):
    g = Square(ways)
    load = pltpu.make_async_copy(w_hbm, w_ref, loaded.at[0])
    greet([{"seq": q} for q in g.near()])
    ag = Gather(g, src_ref, full_ref, send, recv, own_sem.at[0])
    ag.start()
    load.start()
    load.wait()
    count = src_ref.shape[0]
    outgoing = []
    tile = unit * blocks
    tiles = w_ref.shape[1] // (2 * tile)

    def results(slot, rows, t):
        wide = pl.ds(pl.multiple_of(t * 2 * tile, 2 * tile), 2 * tile)
        at = pl.ds(pl.multiple_of(t * tile, tile), tile)
        return [
            pltpu.make_async_copy(stage.at[slot], both_ref.at[rows, wide], done.at[slot, 0]),
            pltpu.make_async_copy(act_stage.at[slot], act_ref.at[rows, at], done.at[slot, 1]),
        ]

    half = count // 2
    turns = []

    def part(k, h):
        index = ag.arrive(k, (h,))
        rows = pl.ds(pl.multiple_of(index * count + h * half, half), half)
        turn = len(turns)
        turns.append((k, h))
        outgoing.append(pltpu.make_async_copy(full_ref.at[rows], all_ref.at[rows], out_sem.at[turn]))
        outgoing[-1].start()

        def body(t, carry):
            slot = lax.rem(turn * tiles + t, 2)
            both = dot_nn(full_ref[rows, :], w_ref[:, pl.ds(pl.multiple_of(t * 2 * tile, 2 * tile), 2 * tile)])

            @pl.when(turn * tiles + t >= 2)
            def _():
                for c in results(slot, rows, t):
                    c.wait()

            stage[slot] = both.astype(BF16)
            for j, (first, second) in enumerate(halves(unit, blocks)):
                gate, up = both[:, first], both[:, second]
                value = gate * sigmoid(gate) * up
                act_stage[slot, :, j * unit : (j + 1) * unit] = value.astype(BF16)
            for c in results(slot, rows, t):
                c.start()
            return carry

        lax.fori_loop(0, tiles, body, 0)

    part(0, 0)
    part(0, 1)
    ag.relay()
    for k in range(1, ways - 1, 2):
        for h in range(2):
            for j in (k, k + 1):
                if j < ways - 1:
                    part(j, h)
    part(ways - 1, 0)
    part(ways - 1, 1)
    last = len(turns) * tiles
    for u in range(max(0, last - 2), last):
        for c in results(u % 2, pl.ds(0, half), 0):
            c.wait()
    for c in outgoing:
        c.wait()
    ag.drain()


def blocks_of(units, unit):
    return 2 if (units // unit) % 2 == 0 else 1


def expand(ways, hidden, w_both, unit):
    rows, width = hidden.shape
    units = w_both.shape[1] // 2
    count = ways * rows
    blocks = blocks_of(units, unit)
    tile = unit * blocks
    return remote_call(
        functools.partial(expand_kernel, ways, unit, blocks),
        (
            jax.ShapeDtypeStruct((count, width), BF16),
            jax.ShapeDtypeStruct((count, 2 * units), BF16),
            jax.ShapeDtypeStruct((count, units), BF16),
        ),
        [VM, ANY],
        (ANY,) * 3,
        [
            pltpu.VMEM((count, width), BF16),
            pltpu.VMEM((width, 2 * units), BF16),
            pltpu.SemaphoreType.DMA((1,)),
            pltpu.SemaphoreType.DMA((2 * ways,)),
            pltpu.VMEM((2, rows // 2, 2 * tile), BF16),
            pltpu.VMEM((2, rows // 2, tile), BF16),
            pltpu.SemaphoreType.DMA((2, 2)),
        ]
        + sems(Gather.sems(ways))
        + [pltpu.SemaphoreType.DMA((1,))],
        7,
        4 * count * width * units,
        1_000_000,
    )(hidden, w_both)


def expand_back_kernel(
    ways, unit, blocks, src_ref, w_hbm, act_hbm, both_ref, dboth_ref, down_hbm,
    full, acc, down_ref, w_ref, act_ref, loaded, out_sem, inputs, stage, ready, done, send, recv, own_sem,
):
    g = Square(ways)
    loads = [pltpu.make_async_copy(a, b, loaded.at[j]) for j, (a, b) in enumerate(((w_hbm, w_ref), (act_hbm, act_ref)))]
    greet([{"seq": q} for q in g.near()])
    ag = Gather(g, src_ref, full, send, recv, own_sem.at[0])
    ag.start()
    for c in loads:
        c.start()
    for c in loads:
        c.wait()
    count, width = src_ref.shape
    half = count // 2
    tile = unit * blocks
    units = w_ref.shape[0]
    tiles = units // tile
    wide = tile_of(width, 1024)
    across = width // wide

    def view(ref, rows, t):
        return ref.at[rows, pl.ds(pl.multiple_of(t * 2 * tile, 2 * tile), 2 * tile)]

    turns = []

    def back(k, h):
        index = ag.arrive(k, (h,))
        rows = pl.ds(pl.multiple_of(index * count + h * half, half), half)
        turn = len(turns)
        turns.append((k, h))

        def load(slot, t):
            return pltpu.make_async_copy(view(both_ref, rows, t), inputs.at[slot], ready.at[slot])

        def result(slot, t):
            return pltpu.make_async_copy(stage.at[slot], view(dboth_ref, rows, t), done.at[slot])

        load((turn * tiles) % 2, 0).start()

        def body(t, carry):
            slot = lax.rem(turn * tiles + t, 2)
            at = pl.ds(pl.multiple_of(t * tile, tile), tile)

            @pl.when(t + 1 < tiles)
            def _():
                load(1 - slot, t + 1).start()

            grads = dot_nt(full[rows, :], w_ref[at, :])
            load(slot, t).wait()

            @pl.when(turn * tiles + t >= 2)
            def _():
                result(slot, t).wait()

            for j, (first, second) in enumerate(halves(unit, blocks)):
                grad = grads[:, j * unit : (j + 1) * unit]
                gate = inputs[slot, :, first].astype(F32)
                up = inputs[slot, :, second].astype(F32)
                s = sigmoid(gate)
                part = grad * s
                stage[slot, :, first] = (part * up * (1.0 + gate * (1.0 - s))).astype(BF16)
                stage[slot, :, second] = (part * gate).astype(BF16)
            result(slot, t).start()
            return carry

        lax.fori_loop(0, tiles, body, 0)

    def written(u):
        own = pl.ds(pl.multiple_of(lax.rem(u, tiles) * tile, tile), tile)
        at = pl.ds(pl.multiple_of(u // tiles * wide, wide), wide)
        return pltpu.make_async_copy(down_ref.at[own, at], down_hbm.at[own, at], out_sem.at[u])

    def down(k, first, rows, last=False):
        index = ag.arrive(k, ())
        those = pl.ds(pl.multiple_of(index * count + first, rows), rows)

        def body(u, carry):
            own = pl.ds(pl.multiple_of(lax.rem(u, tiles) * tile, tile), tile)
            at = pl.ds(pl.multiple_of(u // tiles * wide, wide), wide)
            term = dot_tn(act_ref[those, own], full[those, at])
            if k == 0:
                acc[own, at] = term
            elif not last:
                acc[own, at] += term
            else:
                down_ref[own, at] = (acc[own, at] + term).astype(BF16)
                written(u).start()
            return carry

        lax.fori_loop(0, tiles * across, body, 0)

    back(0, 0)
    back(0, 1)
    down(0, 0, count)
    ag.relay((0, 1))
    for k in range(1, ways - 1, 2):
        pair = [j for j in (k, k + 1) if j < ways - 1]
        for h in range(2):
            for j in pair:
                back(j, h)
            if k == 1 and h == 0:
                down(1, 0, half)
                ag.relay((2, 3))
        for j in pair:
            if j == 1:
                down(1, half, half)
            else:
                down(j, 0, count)
    back(ways - 1, 0)
    down(ways - 1, 0, half)
    back(ways - 1, 1)
    down(ways - 1, half, half, last=True)
    last = len(turns) * tiles
    for u in range(max(0, last - 2), last):
        pltpu.make_async_copy(stage.at[u % 2], view(dboth_ref, pl.ds(0, half), 0), done.at[u % 2]).wait()
    for u in range(tiles * across):
        written(u).wait()
    ag.drain()


def expand_back(ways, grad, w_down, act, both, unit):
    rows, width = grad.shape
    count, units = act.shape
    blocks = blocks_of(units, unit)
    tile = unit * blocks
    return remote_call(
        functools.partial(expand_back_kernel, ways, unit, blocks),
        (jax.ShapeDtypeStruct((count, 2 * units), BF16), jax.ShapeDtypeStruct((units, width), BF16)),
        [VM, ANY, ANY, ANY],
        (ANY, ANY),
        [
            pltpu.VMEM((count, width), BF16),
            pltpu.VMEM((units, width), F32),
            pltpu.VMEM((units, width), BF16),
            pltpu.VMEM((units, width), BF16),
            pltpu.VMEM((count, units), BF16),
            pltpu.SemaphoreType.DMA((2,)),
            pltpu.SemaphoreType.DMA((units // tile * (width // tile_of(width, 1024)),)),
            pltpu.VMEM((2, rows // 2, 2 * tile), BF16),
            pltpu.VMEM((2, rows // 2, 2 * tile), BF16),
            pltpu.SemaphoreType.DMA((2,)),
            pltpu.SemaphoreType.DMA((2,)),
        ]
        + sems(Gather.sems(ways))
        + [pltpu.SemaphoreType.DMA((1,))],
        8,
        4 * count * width * units,
        1_000_000,
    )(grad, w_down, act, both)


def attention_back_kernel(
    ways, head_width, lens_ref, src_ref, w_hbm, attn_hbm, q_hbm, k_hbm, v_hbm, qn_hbm, kn_hbm, cos_hbm, sin_hbm,
    lse_ref, stat_ref, gain_ref, out_ref, sums_ref, all_ref,
    attn_ref, q_ref, k_ref, v_ref, qn_ref, kn_ref, cos_ref, sin_ref, fetched, full, acc, w_ref, out_t, loaded, grad, gq, qacc, kacc, vacc, centre, mine, arrived, total,
    send, recv, own_sem, xsend, xrecv,
):
    g = Square(ways)
    load = pltpu.make_async_copy(w_hbm.at[:, pl.ds(3 * w_ref.shape[1], w_ref.shape[1])], w_ref, loaded.at[0])
    load.start()
    greet([{"seq": q} for q in g.everyone()])
    ag = Gather(g, src_ref, full, send, recv, own_sem.at[0])
    ag.start()
    fetches = [
        pltpu.make_async_copy(a, b, fetched.at[j])
        for j, (a, b) in enumerate(
            (
                (attn_hbm, attn_ref), (q_hbm, q_ref), (k_hbm, k_ref), (v_hbm, v_ref),
                (qn_hbm, qn_ref), (kn_hbm, kn_ref), (cos_hbm, cos_ref), (sin_hbm, sin_ref),
            )
        )
    ]
    for c in fetches:
        c.start()
    kacc[...] = jnp.zeros_like(kacc)
    vacc[...] = jnp.zeros_like(vacc)
    mine[...] = jnp.zeros_like(mine)
    count, width = src_ref.shape
    cols = attn_ref.shape[1]
    heads = cols // head_width
    wide = tile_of(width, 1024)
    bounds = bounds_of(lens_ref)
    root = head_width ** (-0.5)
    factor = root * LOG2E
    back = (LONGEST - 1 + count - 1) // count
    load.wait()
    for c in fetches[:4]:
        c.wait()
    for k in range(ways):
        index = ag.arrive(k)
        rows = pl.ds(pl.multiple_of(index * count, count), count)
        grad[...] = dot_nn(full[rows, :], w_ref[...]).astype(BF16)

        def body(u, carry):
            at = pl.ds(pl.multiple_of(u * wide, wide), wide)
            term = dot_tn(full[rows, at], attn_ref[rows, :])
            if k == 0:
                acc[at, :] = term
            elif k < ways - 1:
                acc[at, :] += term
            else:
                out_t[at, :] = (acc[at, :] + term).astype(BF16)
            return carry

        lax.fori_loop(0, width // wide, body, 0)
        slots = index * count + lax.broadcasted_iota(jnp.int32, (1, count), 1)
        begins = first_key(slots, bounds)
        for h in range(heads):
            at = slice(h * head_width, (h + 1) * head_width)
            centre[h : h + 1, :] = row_sums(grad[:, at].astype(F32) * attn_ref[rows, at].astype(F32))
        qacc[...] = jnp.zeros_like(qacc)

        def keys_block(t, carry):
            kb = index - t
            there = pl.ds(pl.multiple_of(kb * count, count), count)
            keys = kb * count + lax.broadcasted_iota(jnp.int32, (count, count), 0)
            visible = (keys <= slots) & (keys >= begins)
            for h in range(heads):
                at = slice(h * head_width, (h + 1) * head_width)
                keys_h, query, grad_h = k_ref[there, at], q_ref[rows, at], grad[:, at]
                scores = dot_nt(keys_h, query) * factor - lse_ref[h : h + 1, rows]
                weights = jnp.where(visible, jnp.exp2(scores), 0.0)
                grad_probs = dot_nt(v_ref[there, at], grad_h)
                grad_scores = (weights * (grad_probs - centre[h : h + 1, :])).astype(BF16)
                vacc[there, at] += dot_nn(weights.astype(BF16), grad_h)
                kacc[there, at] += dot_nn(grad_scores, query)
                qacc[:, at] += dot_tn(grad_scores, keys_h)
            return carry

        lax.fori_loop(0, jnp.minimum(index, back) + 1, keys_block, 0)
        gq[rows, :] = (qacc[...] * root).astype(BF16)
        mine[0:1, rows] = row_sums(gq[rows, :].astype(F32) * q_ref[rows, :].astype(F32))
        if k == 0:
            ag.relay()
    ag.drain()
    written = pltpu.make_async_copy(out_t, all_ref.at[:, pl.ds(3 * cols, cols)], loaded.at[1])
    written.start()

    for c in fetches[4:]:
        c.wait()

    def key_grad(rows, at):
        return (kacc[rows, at] * root).astype(BF16).astype(F32)

    def inner(i, carry):
        rows = pl.ds(pl.multiple_of(i * count, count), count)
        mine[1:2, rows] = row_sums(key_grad(rows, slice(0, cols)) * k_ref[rows, :].astype(F32))
        out_ref[rows, 2 * cols : 3 * cols] = vacc[rows, :].astype(BF16)
        return carry

    lax.fori_loop(0, ways, inner, 0)
    total[...] = exchange_rows(g, mine, arrived, xsend, xrecv)
    sums_ref[...] = jnp.zeros_like(sums_ref)
    small = tile_of(count, 256)

    def finish(i, carry):
        rows = pl.ds(pl.multiple_of(i * small, small), small)
        inverse = lax.rsqrt(as_columns(stat_ref[:, rows]) * (1.0 / width) + NORM_EPS)
        mean = as_columns(total[:, rows]) * (1.0 / width)
        cosine, sine = cos_ref[rows, :], sin_ref[rows, :]
        for part, normed in ((0, qn_ref), (1, kn_ref)):
            scale, middle = inverse[:, part : part + 1], mean[:, part : part + 1]
            for h in range(heads):
                at = slice(h * head_width, (h + 1) * head_width)
                value = gq[rows, at].astype(F32) if part == 0 else key_grad(rows, at)
                e = value * cosine - pltpu.roll(value, head_width // 2, 1) * sine
                unit = normed[rows, at].astype(F32)
                start = pl.multiple_of(g.me * cols + h * head_width, head_width)
                gain = gain_ref[part : part + 1, pl.ds(start, head_width)]
                to = slice(part * cols + h * head_width, part * cols + (h + 1) * head_width)
                out_ref[rows, to] = (scale * (e * gain - unit * middle)).astype(BF16)
                sums_ref[part : part + 1, at] += jnp.sum(e * unit, axis=0, keepdims=True)
        return carry

    lax.fori_loop(0, ways * count // small, finish, 0)
    written.wait()


def attention_back(ways, lens, grad, w_all, attn, q_low, k_low, v_low, qn, kn, lse, stats, gains, cosine, sine):
    rows, width = grad.shape
    count, cols = attn.shape
    head_width = cosine.shape[1]
    return remote_call(
        functools.partial(attention_back_kernel, ways, head_width),
        (
            jax.ShapeDtypeStruct((count, 3 * cols), BF16),
            jax.ShapeDtypeStruct((8, cols), F32),
            jax.ShapeDtypeStruct((width, 4 * cols), BF16),
        ),
        [pl.BlockSpec(memory_space=pltpu.SMEM), VM] + [ANY] * 9 + [VM] * 3,
        (VM, VM, ANY),
        [pltpu.VMEM((count, cols), BF16)] * 6
        + [pltpu.VMEM((count, head_width), F32)] * 2
        + [
            pltpu.SemaphoreType.DMA((8,)),
            pltpu.VMEM((count, width), BF16),
            pltpu.VMEM((width, cols), F32),
            pltpu.VMEM((width, cols), BF16),
            pltpu.VMEM((width, cols), BF16),
            pltpu.SemaphoreType.DMA((2,)),
            pltpu.VMEM((rows, cols), BF16),
            pltpu.VMEM((count, cols), BF16),
            pltpu.VMEM((rows, cols), F32),
            pltpu.VMEM((count, cols), F32),
            pltpu.VMEM((count, cols), F32),
            pltpu.VMEM((8, rows), F32),
            pltpu.VMEM((8, count), F32),
            pltpu.VMEM((ways - 1, 8, count), F32),
            pltpu.VMEM((8, count), F32),
        ]
        + sems(Gather.sems(ways))
        + [pltpu.SemaphoreType.DMA((1,))]
        + sems(ways - 1),
        9,
        4 * count * width * cols,
        1_000_000,
    )(lens, grad, w_all, attn, q_low, k_low, v_low, qn, kn, cosine, sine, lse, stats, gains)


def weight_grads_kernel(x_ref, d_ref, old_ref, out_ref):
    out_ref[...] = dot_tn(x_ref[...], d_ref[...]).astype(BF16)


def weight_grads(x_full, d_qkv, grads):
    count, width = x_full.shape
    depth = d_qkv.shape[1]
    tm, tn = tile_of(width, 512), depth
    return pl.pallas_call(
        weight_grads_kernel,
        out_shape=jax.ShapeDtypeStruct(grads.shape, BF16),
        grid=(width // tm, depth // tn),
        in_specs=[
            pl.BlockSpec((count, tm), lambda i, j: (0, i)),
            pl.BlockSpec((count, tn), lambda i, j: (0, j)),
            ANY,
        ],
        out_specs=pl.BlockSpec((tm, tn), lambda i, j: (i, j)),
        input_output_aliases={2: 0},
        compiler_params=pltpu.CompilerParams(
            dimension_semantics=("arbitrary", "arbitrary"), vmem_limit_bytes=VMEM_BYTES
        ),
        cost_estimate=pl.CostEstimate(flops=0, bytes_accessed=1_000_000, transcendentals=0),
    )(x_full, d_qkv, grads)


def scatter_dp(terms, axis):
    return lax.psum_scatter(terms.astype(BF16), "dp", scatter_dimension=axis, tiled=True)


def gather_dp(weights, axis):
    return lax.all_gather(weights, "dp", axis=axis, tiled=True)


def interleave(gate, up, unit):
    rows = gate.shape[0]
    return jnp.stack([gate.reshape(rows, -1, unit), up.reshape(rows, -1, unit)], axis=2).reshape(rows, -1)


def local(
    layer_in, cotangent, lengths, w_query, w_key, w_value, w_out, w_gate, w_up, w_down,
    gain_query, gain_key, gain_attn, gain_ffn,
):
    rows, width = layer_in.shape
    ways, dp_ways = lax.axis_size("seq"), lax.axis_size("dp")
    count = rows * ways
    head_width = width // HEADS
    cols = width // ways
    part = gain_query.shape[0]
    lens = lengths[0]
    seq_me = lax.axis_index("seq")
    mine = w_gate.shape[1]
    joined = mine % 128 == 0
    unit = mine if joined else tile_of(mine * dp_ways, 256)

    w_all = gather_dp(jnp.concatenate([w_query, w_key, w_value, w_out.T], axis=1), 0)
    if joined:
        w_both = gather_dp(jnp.concatenate([w_gate, w_up], axis=1), 1)
    else:
        w_both = interleave(gather_dp(w_gate, 1), gather_dp(w_up, 1), unit)
    all_down = gather_dp(w_down, 0)

    four = jnp.stack([gain_query, gain_key, gain_attn, gain_ffn]).astype(F32)
    x_full, gain_tiles, cosine, sine = enter(
        ways, dp_ways, lens, layer_in, jnp.pad(four, ((0, 4), (0, 128 - part)))
    )
    gains = gain_tiles[:, :, :4, :part].transpose(2, 1, 0, 3).reshape(4, width)

    q_low, k_low, v_low, qn, kn, stats = project(ways, x_full, w_all, gains, cosine, sine)
    attn, lse = attend(lens, q_low, k_low, v_low, head_width)

    whole = jax.ShapeDtypeStruct((rows, width), F32)
    half = jax.ShapeDtypeStruct((rows, width), BF16)
    eight = jax.ShapeDtypeStruct((8, width), F32)
    hidden, unit_a, inv_a, hidden_low = meet(
        ways, attn, w_all, True, after_attention, (layer_in, gains),
        (whole, half, jax.ShapeDtypeStruct((rows, 128), F32), half), 3, 3 * cols,
    )
    hidden_full, both, act = expand(ways, hidden_low, w_both, unit)
    layer_out, sums_f, grad_m = meet(
        ways, act, all_down, False, after_ffn, (hidden, cotangent, gains), (half, eight, half), 4
    )
    d_both, grad_down = expand_back(ways, grad_m, all_down, act, both, unit)
    out_down = scatter_dp(grad_down, 0)
    grad_both = dot_tn(hidden_full, d_both).astype(BF16)
    d_both, grad_both = lax.optimization_barrier((d_both, grad_both))
    if joined:
        out_both = [scatter_dp(grad_both, 1)]
    else:
        pieces = grad_both.reshape(width, -1, 2, unit)
        out_both = [scatter_dp(pieces[:, :, j].reshape(width, -1), 1) for j in range(2)]
    grad_hidden, sums_a, grad_a = meet(
        ways, d_both, w_both, True, before_ffn, (cotangent, unit_a, inv_a, gains), (whole, eight, half), 5
    )
    grad_a, out_down = lax.optimization_barrier((grad_a, out_down))
    d_qkv, sums_qk, grad_all = attention_back(
        ways, lens, grad_a, w_all, attn, q_low, k_low, v_low, qn, kn, lse, stats, gains, cosine, sine
    )
    grad_all = weight_grads(x_full, d_qkv, grad_all)
    d_qkv, grad_all, out_both = lax.optimization_barrier((d_qkv, grad_all, out_both))
    out_all = scatter_dp(grad_all, 0)
    out_gate, out_up = (out_both[0][:, :mine], out_both[0][:, mine:]) if joined else out_both

    own = lax.dynamic_update_slice(jnp.zeros((2, width), F32), sums_qk[:2], (0, seq_me * cols))
    norms = jnp.stack([jnp.sum(sums_a, axis=0), jnp.sum(sums_f, axis=0)])
    tiles = jnp.concatenate([own, norms]).reshape(4, dp_ways, ways, part).transpose(1, 2, 0, 3)
    tiles = jnp.pad(tiles, ((0, 0), (0, 0), (0, 4), (0, 128 - part)))
    grad_in, gain_sums = leave(ways, dp_ways, d_qkv, w_all, grad_hidden, tiles)
    return (
        layer_out,
        grad_in,
        out_all[:, :cols].astype(F32),
        out_all[:, cols : 2 * cols].astype(F32),
        out_all[:, 2 * cols : 3 * cols].astype(F32),
        out_all[:, 3 * cols :].T.astype(F32),
        out_gate.astype(F32),
        out_up.astype(F32),
        out_down.astype(F32),
        gain_sums[0, :part],
        gain_sums[1, :part],
        gain_sums[2, :part],
        gain_sums[3, :part],
    )


def solution(mesh):
    both = P(("dp", "seq"))
    rows = P(("dp", "seq"), None)
    columns = P(None, ("dp", "seq"))
    square = P("dp", "seq")
    in_specs = (
        rows, rows, P("dp", None), square, square, square, P("seq", "dp"), columns, columns, rows, both, both, both, both,
    )
    out_specs = (
        rows, rows, square, square, square, P("seq", "dp"), columns, columns, rows, both, both, both, both,
    )
    return jax.shard_map(local, mesh=mesh, in_specs=in_specs, out_specs=out_specs, check_vma=False)
```
